128 devices in a mesh: tile: 64 (over z_hi, y, x, core), vec: 2 (over z_lo).
Axes of the slice: x: 4, y: 4, z: 4 (z_hi: 2, z_lo: 2; z = z_hi * 2 + z_lo), core: 2. Of those that a mesh axis runs over, the one named last changes fastest.
Arguments:
- trial: bfloat16 [1, 1024, 1024], P(None, ('tile', 'vec')), may hold values from -0.005859375 to 0.005859375
- psi_v: bfloat16 [1024, 8192], P(None, 'tile'), may hold values from -16 to 16
- psi_c: bfloat16 [1024, 2, 4096], P(None, 'vec', 'tile'), may hold values from -6 to 6
- screened: float32 [8192, 8192], P('tile', 'vec'), may hold values from -0.0007324219 to 0.0007324219
Outputs:
- result: float32 [1, 1024, 1024], P(None, ('tile', 'vec'))
The draws below stay inside these ranges and needn't reach their ends.
All inputs are finite; a program needn't handle non-finite values.
Results may differ from the reference program's by a relative error of at most 0.0041.
Values may be sent and summed in bfloat16 or wider, within the bound.
No kernel may reach another device: no remote copies, remote signals or barrier semaphores. Data moves between devices by JAX's collectives and lax.ppermute only.
A program may use at most 64 MiB of HBM per device.

```python
import jax
import jax.numpy as jnp
from jax import lax

NV = 1024
NC = 1024
NP = 8192
NVEC = 1
NPH = 4096
N_VEC = 2


def with_spikes(values, stream_key, source, target, blocks, factor):
    owner, partner = [(jnp.arange(values.shape[axis_at]) // (values.shape[axis_at] // blocks)).reshape([-1 if axis == axis_at else 1 for axis in range(values.ndim)]) for axis_at in (source, target)]
    chosen = jax.random.permutation(stream_key, blocks)[partner]
    strong = (owner == chosen) | (owner == (partner + blocks // 2) % blocks)
    return jnp.where(strong, factor * values, values)


def steps_of(rng, dims, cuts, smallest, largest):
    level, own = 1.0, jax.random.fold_in(rng, 6)
    for axis_at, shards_of in cuts:
        draws = jnp.exp(jax.random.uniform(jax.random.fold_in(own, axis_at), (shards_of,), jnp.float32, smallest / len(cuts), largest / len(cuts)))
        level = level * jnp.repeat(draws, dims[axis_at] // shards_of).reshape([-1 if axis == axis_at else 1 for axis in range(len(dims))])
    return level


def noise(stream_key, shape, spread, bound, cuts=(), held_as=jnp.bfloat16):
    factor_of = steps_of(stream_key, shape, cuts, -0.22, 0.18) if cuts else 1.0
    drawn = jax.random.normal(stream_key, shape, jnp.float32) * spread * factor_of
    return jnp.minimum(jnp.maximum(drawn, -bound), bound).astype(held_as)


def bell_draw_with(own_key, shape, scale, reach, pieces, heavy, kind=jnp.bfloat16):
    result = scale * jax.random.normal(own_key, shape, jnp.float32)
    if pieces:
        result = result * steps_of(own_key, shape, pieces, -0.22, 0.18)
    return jnp.clip(with_spikes(result, jax.random.fold_in(own_key, 3), *heavy), -reach, reach).astype(kind)


def setup_inputs(seed: int = 0) -> dict:
    splits = jax.random.split(jax.random.key(seed), 5)
    trial = noise(splits[0], (NVEC, NV, NC), (NV * NC) ** -0.5, 0.005859375, ((1, 128),))
    psi_v = bell_draw_with(splits[1], (NV, NP), 1.0, 16.0, ((1, 64),), (1, 0, 64, 4.0))
    psi_c = noise(splits[2], (NC, N_VEC, NPH), 1.0, 6.0, ((1, 2), (2, 64)))
    screened = noise(splits[3], (NP, NP), (NP * NP) ** -0.5, 0.0007324219, ((0, 64), (1, 2)), jnp.float32)
    return dict(trial=trial, psi_v=psi_v, psi_c=psi_c, screened=screened)


def reference(trial, psi_v, psi_c, screened):
    conduction = psi_c.reshape(NC, NP)
    left = psi_v.astype(jnp.float32)

    def one_vector(single):
        projected = jnp.dot(psi_v.T, single, preferred_element_type=jnp.float32).astype(jnp.bfloat16)
        pair = jnp.dot(projected, conduction, preferred_element_type=jnp.float32)
        weighted = (screened * pair).astype(jnp.bfloat16)
        back = jnp.dot(weighted, conduction.T, preferred_element_type=jnp.float32)
        return jnp.dot(left, back, precision=lax.Precision.HIGHEST)

    return lax.map(one_vector, trial)
```

```python
import jax
import jax.numpy as jnp
from jax import lax
from jax.experimental import pallas as pl
from jax.experimental.pallas import tpu as pltpu
from jax.sharding import Mesh
from jax.sharding import PartitionSpec as P

TILE_VEC = ("zh", "y", "x", "core", "zl")
TILE = ("zh", "y", "x", "core")
VMEM_LIMIT = 48 * 1024 * 1024
F32 = jnp.float32
BF16 = jnp.bfloat16


def shift(value, axis, by):
    n = lax.axis_size(axis)
    return lax.ppermute(value, axis, [(k, (k + by) % n) for k in range(n)])


def around(value, axis):
    return [value, shift(value, axis, 1), shift(value, axis, -1), shift(value, axis, 2)]


STEPS = (0, -1, 1, -2)


def any_spec():
    return pl.BlockSpec(memory_space=pl.ANY)


def vmem_spec():
    return pl.BlockSpec(memory_space=pltpu.VMEM)


def params():
    return pltpu.CompilerParams(vmem_limit_bytes=VMEM_LIMIT)


def project(trial_half, left_own, left_other):
    points = left_own.shape[1]
    cols = trial_half.shape[1]

    def kernel(trial_ref, own_ref, other_ref, out_ref):
        core = lax.axis_index("core")
        for ref, at in ((own_ref, core), (other_ref, 1 - core)):
            part = lax.dot_general(
                ref[...], trial_ref[...], (((0,), (0,)), ((), ())), preferred_element_type=F32
            )
            out_ref[pl.ds(pl.multiple_of(at * points, points), points), :] = part.astype(BF16)

    return pl.pallas_call(
        kernel,
        out_shape=jax.ShapeDtypeStruct((2 * points, cols), BF16),
        in_specs=[vmem_spec()] * 3,
        out_specs=vmem_spec(),
        compiler_params=params(),
        name="project",
    )(trial_half, left_own, left_other)


def direct(proj_own, proj_other, sets_a, sets_b, screened, screened_other):
    rows, half = proj_own.shape
    points = screened.shape[0]
    states = 2 * half
    block = sets_a[0].shape[0] // 4
    count = 32 * block
    chunk = 512

    def kernel(*refs):
        own_ref, other_ref = refs[:2]
        a_refs, b_refs = refs[2:6], refs[6:10]
        scr_ref, scr_other_ref = refs[10:12]
        keep_ref, send_ref = refs[12:14]
        proj, panel, scr, back, sems = refs[14:]
        core, y, x = lax.axis_index("core"), lax.axis_index("y"), lax.axis_index("x")
        copies = [
            (own_ref, proj.at[:, pl.ds(pl.multiple_of(core * half, half), half)]),
            (other_ref, proj.at[:, pl.ds(pl.multiple_of((1 - core) * half, half), half)]),
            (
                scr_ref.at[:, pl.ds(pl.multiple_of(core * count, count), count)],
                scr.at[pl.ds(pl.multiple_of(core * points, points), points), :],
            ),
            (scr_other_ref, scr.at[pl.ds(pl.multiple_of((1 - core) * points, points), points), :]),
        ]
        for outer in range(4):
            for inner in range(4):
                for which, ref in ((0, a_refs[outer]), (1, b_refs[outer])):
                    dy, dx = (outer, inner) if which == 0 else (inner, outer)
                    at = lax.rem(y + STEPS[dy] + 4, 4) * 4 + lax.rem(x + STEPS[dx] + 4, 4)
                    start = pl.multiple_of(at * (2 * block) + which * block, block)
                    copies.append(
                        (ref.at[pl.ds(inner * block, block), :], panel.at[pl.ds(start, block), :])
                    )
        made = [
            pltpu.make_async_copy(source, target, sems.at[k])
            for k, (source, target) in enumerate(copies)
        ]
        for copy in made:
            copy.start()
        for copy in made:
            copy.wait()
        for k in range(count // chunk):
            here = pl.ds(k * chunk, chunk)
            pair = lax.dot_general(
                proj[...], panel[here, :], (((1,), (1,)), ((), ())), preferred_element_type=F32
            )
            weighted = (scr[:, here] * pair).astype(BF16)
            part = jnp.dot(weighted, panel[here, :], preferred_element_type=F32)
            if k == 0:
                back[...] = part
            else:
                back[...] += part
        keep_ref[...] = back[:, pl.ds(pl.multiple_of(core * half, half), half)]
        send_ref[...] = back[:, pl.ds(pl.multiple_of((1 - core) * half, half), half)]

    return pl.pallas_call(
        kernel,
        out_shape=[jax.ShapeDtypeStruct((rows, half), F32)] * 2,
        in_specs=[any_spec()] * 12,
        out_specs=[vmem_spec()] * 2,
        scratch_shapes=[
            pltpu.VMEM((rows, states), BF16),
            pltpu.VMEM((count, states), BF16),
            pltpu.VMEM((rows, count), F32),
            pltpu.VMEM((rows, states), F32),
            pltpu.SemaphoreType.DMA((36,)),
        ],
        compiler_params=params(),
        name="direct",
    )(proj_own, proj_other, *sets_a, *sets_b, screened, screened_other)


def finish(left_own, left_other, back_own, back_other):
    states, points = left_own.shape
    cols = back_own.shape[1]

    def kernel(own_ref, other_ref, a_ref, b_ref, out_ref, high, low):
        core = lax.axis_index("core")
        back = a_ref[...] + b_ref[...]
        top = back.astype(BF16)
        high[...] = top
        low[...] = (back - top.astype(F32)).astype(BF16)
        total = None
        for ref, at in ((own_ref, core), (other_ref, 1 - core)):
            here = pl.ds(pl.multiple_of(at * points, points), points)
            for piece in (high, low):
                part = jnp.dot(ref[...], piece[here, :], preferred_element_type=F32)
                total = part if total is None else total + part
        out_ref[...] = total.astype(BF16)

    return pl.pallas_call(
        kernel,
        out_shape=jax.ShapeDtypeStruct((states, cols), BF16),
        in_specs=[vmem_spec()] * 4,
        out_specs=vmem_spec(),
        scratch_shapes=[pltpu.VMEM((2 * points, cols), BF16)] * 2,
        compiler_params=params(),
        name="finish",
    )(left_own, left_other, back_own, back_other)


def shards(trial, psi_v, psi_c, screened):
    rows, states = trial.shape[1:]
    half = states // 2
    devices = lax.axis_size(TILE_VEC)
    core = lax.axis_index("core")
    zh = lax.axis_index("zh")
    halves = trial[0].reshape(rows, 2, half).transpose(1, 0, 2)
    outgoing = jnp.broadcast_to(
        halves[None, :, None], (devices // 4, 2, 2, rows, half)
    ).reshape(devices, rows, half)
    trial_half = lax.all_to_all(outgoing, TILE_VEC, split_axis=0, concat_axis=0, tiled=True)
    trial_half = trial_half.reshape(devices * rows, half)
    own = psi_c[:, 0, :].T
    first = lax.ppermute(own, ("zh", "core"), [(1, 0), (2, 1), (0, 2), (3, 3)])
    second = lax.ppermute(own, ("zh", "core"), [(0, 0), (3, 1), (1, 2), (2, 3)])
    same = core == zh
    block_a = jnp.where(same, second, first)
    block_b = jnp.where(same, first, second)
    left_other = shift(psi_v, "core", 1)
    width = screened.shape[1] // 2
    screened_other = shift(
        lax.dynamic_slice_in_dim(screened, (1 - core) * width, width, 1), "core", 1
    )
    line_a = jnp.concatenate(around(block_a, "x"), 0)
    line_b = jnp.concatenate(around(block_b, "y"), 0)
    sets_a = around(line_a, "y")
    sets_b = around(line_b, "x")
    proj_own = project(trial_half, psi_v, left_other)
    proj_other = shift(proj_own, "core", 1)
    keep, send = direct(proj_own, proj_other, sets_a, sets_b, screened, screened_other)
    got = shift(send, "core", 1)
    term = finish(psi_v, left_other, keep, got)
    pieces = lax.all_to_all(
        term.reshape(devices, rows, half), TILE_VEC, split_axis=0, concat_axis=0, tiled=True
    )
    pieces = pieces.reshape(devices // 4, 2, 2, rows, half).astype(F32)
    total = jnp.sum(pieces, axis=(0, 2))
    return total.transpose(1, 0, 2).reshape(1, rows, states)


def solution(mesh):
    split = Mesh(
        mesh.devices.reshape(2, 4, 4, 2, mesh.shape["vec"]),
        TILE_VEC,
    )
    return jax.shard_map(
        shards,
        mesh=split,
        in_specs=(P(None, TILE_VEC, None), P(None, TILE), P(None, "zl", TILE), P(TILE, "zl")),
        out_specs=P(None, TILE_VEC, None),
        check_vma=False,
    )
```

```python
import jax
import jax.numpy as jnp
from jax import lax
from jax.experimental import pallas as pl
from jax.experimental.pallas import tpu as pltpu
from jax.sharding import Mesh
from jax.sharding import PartitionSpec as P

TILE_VEC = ("zh", "y", "x", "core", "zl")
TILE = ("zh", "y", "x", "core")
F32 = jnp.float32
BF16 = jnp.bfloat16
SIBLING = (1, 0, 3, 2)


def others(sibling, partner, diagonal):
    return [
        lax.ppermute(sibling, "core", [(0, 1), (1, 0)]),
        lax.ppermute(partner, "zh", [(0, 1), (1, 0)]),
        lax.ppermute(diagonal, ("zh", "core"), [(0, 3), (1, 2), (2, 1), (3, 0)]),
    ]


def vmem_spec():
    return pl.BlockSpec(memory_space=pltpu.VMEM)


def params(mebibytes):
    return pltpu.CompilerParams(vmem_limit_bytes=mebibytes * 1024 * 1024)


def pack(screened):
    points, count = screened.shape
    plane, steps = count // 2, 4
    width = plane // 2

    def kernel(in_ref, *out_refs):
        core, zh = lax.axis_index("core"), lax.axis_index("zh")
        rows = in_ref.shape[0]
        low = lax.broadcasted_iota(jnp.int32, (rows, 128), 1) < 64
        first = core == 0
        for far in range(2):
            base = plane * (zh if far == 0 else 1 - zh)
            for m in range(width // 128):
                a = in_ref[:, pl.ds(pl.multiple_of(base + m * 256, 256), 128)]
                b = in_ref[:, pl.ds(pl.multiple_of(base + m * 256 + 128, 128), 128)]
                zero = jnp.where(low, a, pltpu.roll(b, 64, 1))
                one = jnp.where(low, pltpu.roll(a, 64, 1), b)
                here = pl.ds(m * 128, 128)
                out_refs[2 * far][:, here] = jnp.where(first, zero, one)
                out_refs[2 * far + 1][:, here] = jnp.where(first, one, zero)

    return pl.pallas_call(
        kernel,
        grid=(steps,),
        out_shape=[jax.ShapeDtypeStruct((points, width), F32)] * 4,
        in_specs=[pl.BlockSpec((points // steps, count), lambda k: (k, 0))],
        out_specs=[pl.BlockSpec((points // steps, width), lambda k: (k, 0))] * 4,
        compiler_params=params(8),
        name="pack",
    )(screened)


def project(trial_half, lefts):
    points = lefts[0].shape[1]
    cols = trial_half.shape[1]

    def kernel(trial_ref, *refs):
        out_ref = refs[4]
        for k in range(4):
            part = lax.dot_general(
                refs[k][...], trial_ref[...], (((0,), (0,)), ((), ())), preferred_element_type=F32
            )
            out_ref[k * points : (k + 1) * points, :] = part.astype(BF16)

    return pl.pallas_call(
        kernel,
        out_shape=jax.ShapeDtypeStruct((4 * points, cols), BF16),
        in_specs=[vmem_spec()] * 5,
        out_specs=vmem_spec(),
        compiler_params=params(8),
        name="project",
    )(trial_half, *lefts)


def direct(proj_own, proj_other, panel, weights):
    rows, half = proj_own.shape
    points = rows // 4
    count = panel.shape[0]
    chunk = 512

    def kernel(own_ref, other_ref, panel_ref, *refs):
        scr_refs, (keep_ref, send_ref, proj) = refs[:4], refs[4:]
        core = lax.axis_index("core")
        mine = pl.ds(pl.multiple_of(core * half, half), half)
        sibs = pl.ds(pl.multiple_of((1 - core) * half, half), half)
        for k in range(4):
            proj[k * points : (k + 1) * points, :] = other_ref[
                SIBLING[k] * points : (SIBLING[k] + 1) * points, :
            ]
        nt = (((1,), (1,)), ((), ()))
        for k in range(count // chunk):
            here = pl.ds(k * chunk, chunk)
            pair = lax.dot_general(own_ref[...], panel_ref[here, mine], nt, preferred_element_type=F32)
            pair += lax.dot_general(proj[...], panel_ref[here, sibs], nt, preferred_element_type=F32)
            weighted = jnp.concatenate(
                [
                    (scr_refs[j][:, here] * pair[j * points : (j + 1) * points]).astype(BF16)
                    for j in range(4)
                ],
                0,
            )
            send = jnp.dot(weighted, panel_ref[here, sibs], preferred_element_type=F32)
            keep = jnp.dot(weighted, panel_ref[here, mine], preferred_element_type=F32)
            if k == 0:
                send_ref[...] = send
                keep_ref[...] = keep
            else:
                send_ref[...] += send
                keep_ref[...] += keep

    return pl.pallas_call(
        kernel,
        out_shape=[jax.ShapeDtypeStruct((rows, half), F32)] * 2,
        in_specs=[vmem_spec()] * 7,
        out_specs=[vmem_spec()] * 2,
        scratch_shapes=[pltpu.VMEM((rows, half), BF16)],
        compiler_params=params(24),
        name="direct",
    )(proj_own, proj_other, panel, *weights)


def finish(lefts, keep, got):
    states, points = lefts[0].shape
    cols = keep.shape[1]

    def kernel(*refs):
        left_refs, (keep_ref, got_ref, out_ref, left, high, low) = refs[:4], refs[4:]
        for k in range(4):
            here = slice(k * points, (k + 1) * points)
            there = slice(SIBLING[k] * points, (SIBLING[k] + 1) * points)
            back = keep_ref[here, :] + got_ref[there, :]
            top = back.astype(BF16)
            high[here, :] = top
            low[here, :] = (back - top.astype(F32)).astype(BF16)
            left[:, here] = left_refs[k][...]
        total = jnp.dot(left[...], high[...], preferred_element_type=F32)
        total += jnp.dot(left[...], low[...], preferred_element_type=F32)
        out_ref[...] = total.astype(BF16)

    return pl.pallas_call(
        kernel,
        out_shape=jax.ShapeDtypeStruct((states, cols), BF16),
        in_specs=[vmem_spec()] * 6,
        out_specs=vmem_spec(),
        scratch_shapes=[
            pltpu.VMEM((states, 4 * points), BF16),
            pltpu.VMEM((4 * points, cols), BF16),
            pltpu.VMEM((4 * points, cols), BF16),
        ],
        compiler_params=params(16),
        name="finish",
    )(*lefts, keep, got)


def shards(trial, psi_v, psi_c, screened):
    rows, states = trial.shape[1:]
    half = states // 2
    devices = lax.axis_size(TILE_VEC)
    own = psi_c[:, 0, :].T
    plane = lax.axis_size(("y", "x"))
    panel = lax.all_to_all(
        jnp.broadcast_to(own[None], (plane, *own.shape)), ("y", "x"), split_axis=0, concat_axis=0, tiled=True
    ).reshape(plane * own.shape[0], states)
    packed = pack(screened)
    weights = [packed[0], *others(*packed[1:])]
    halves = trial[0].reshape(rows, 2, half).transpose(1, 0, 2)
    outgoing = jnp.broadcast_to(
        halves[None, :, None], (devices // 4, 2, 2, rows, half)
    ).reshape(devices, rows, half)
    trial_half = lax.all_to_all(outgoing, TILE_VEC, split_axis=0, concat_axis=0, tiled=True)
    trial_half = trial_half.reshape(devices * rows, half)
    lefts = [psi_v, *others(psi_v, psi_v, psi_v)]
    proj_own = project(trial_half, lefts)
    proj_other = lax.ppermute(proj_own, "core", [(0, 1), (1, 0)])
    keep, send = direct(proj_own, proj_other, panel, weights)
    got = lax.ppermute(send, "core", [(0, 1), (1, 0)])
    term = finish(lefts, keep, got)
    pieces = lax.all_to_all(
        term.reshape(devices, rows, half), TILE_VEC, split_axis=0, concat_axis=0, tiled=True
    )
    pieces = pieces.reshape(devices // 4, 2, 2, rows, half).astype(F32)
    total = jnp.sum(pieces, axis=(0, 2))
    return total.transpose(1, 0, 2).reshape(1, rows, states)


def solution(mesh):
    split = Mesh(
        mesh.devices.reshape(2, 4, 4, 2, mesh.shape["vec"]),
        TILE_VEC,
    )
    return jax.shard_map(
        shards,
        mesh=split,
        in_specs=(P(None, TILE_VEC, None), P(None, TILE), P(None, "zl", TILE), P(TILE, "zl")),
        out_specs=P(None, TILE_VEC, None),
        check_vma=False,
    )
```

```python
import jax
import jax.numpy as jnp
from jax import lax
from jax.experimental import pallas as pl
from jax.experimental.pallas import tpu as pltpu
from jax.sharding import Mesh
from jax.sharding import PartitionSpec as P

TILE_VEC = ("zh", "y", "x", "core", "zl")
TILE = ("zh", "y", "x", "core")
F32 = jnp.float32
BF16 = jnp.bfloat16
SIBLING = (1, 0, 3, 2)


def swap(value):
    return lax.ppermute(value, "core", [(0, 1), (1, 0)])


def others(sibling, partner, diagonal):
    return [
        swap(sibling),
        lax.ppermute(partner, "zh", [(0, 1), (1, 0)]),
        lax.ppermute(diagonal, ("zh", "core"), [(0, 3), (1, 2), (2, 1), (3, 0)]),
    ]


def vmem_spec():
    return pl.BlockSpec(memory_space=pltpu.VMEM)


def params(mebibytes):
    return pltpu.CompilerParams(vmem_limit_bytes=mebibytes * 1024 * 1024)


def pack(screened):
    points, count = screened.shape
    plane, steps = count // 2, 4
    width = plane // 2

    def kernel(in_ref, *out_refs):
        core, zh = lax.axis_index("core"), lax.axis_index("zh")
        rows = in_ref.shape[0]
        low = lax.broadcasted_iota(jnp.int32, (rows, 128), 1) < 64
        first = core == 0
        for far in range(2):
            base = plane * (zh if far == 0 else 1 - zh)
            for m in range(width // 128):
                a = in_ref[:, pl.ds(pl.multiple_of(base + m * 256, 256), 128)]
                b = in_ref[:, pl.ds(pl.multiple_of(base + m * 256 + 128, 128), 128)]
                zero = jnp.where(low, a, pltpu.roll(b, 64, 1))
                one = jnp.where(low, pltpu.roll(a, 64, 1), b)
                here = pl.ds(m * 128, 128)
                for ref, piece in (
                    (out_refs[2 * far], jnp.where(first, zero, one)),
                    (out_refs[2 * far + 1], jnp.where(first, one, zero)),
                ):
                    ref[:, here] = piece.astype(ref.dtype)

    return pl.pallas_call(
        kernel,
        grid=(steps,),
        out_shape=[jax.ShapeDtypeStruct((points, width), kind) for kind in (F32, BF16, BF16, BF16)],
        in_specs=[pl.BlockSpec((points // steps, count), lambda k: (k, 0))],
        out_specs=[pl.BlockSpec((points // steps, width), lambda k: (k, 0))] * 4,
        compiler_params=params(8),
        name="pack",
    )(screened)


def project(trial_half, lefts):
    points = lefts[0].shape[1]
    cols = trial_half.shape[1]

    def kernel(trial_ref, *refs):
        out_ref = refs[4]
        for k in range(4):
            part = lax.dot_general(
                refs[k][...], trial_ref[...], (((0,), (0,)), ((), ())), preferred_element_type=F32
            )
            out_ref[k * points : (k + 1) * points, :] = part.astype(BF16)

    return pl.pallas_call(
        kernel,
        out_shape=jax.ShapeDtypeStruct((4 * points, cols), BF16),
        in_specs=[vmem_spec()] * 5,
        out_specs=vmem_spec(),
        compiler_params=params(8),
        name="project",
    )(trial_half, *lefts)


def direct(proj_own, proj_other, panel, weights):
    rows, half = proj_own.shape
    points = rows // 4
    count = panel.shape[0]
    chunk = 512

    def kernel(own_ref, other_ref, panel_ref, *refs):
        scr_refs, (keep_ref, send_ref, proj) = refs[:4], refs[4:]
        core = lax.axis_index("core")
        mine = pl.ds(pl.multiple_of(core * half, half), half)
        sibs = pl.ds(pl.multiple_of((1 - core) * half, half), half)
        for k in range(4):
            proj[k * points : (k + 1) * points, :] = other_ref[
                SIBLING[k] * points : (SIBLING[k] + 1) * points, :
            ]
        nt = (((1,), (1,)), ((), ()))
        for k in range(count // chunk):
            here = pl.ds(k * chunk, chunk)
            pair = lax.dot_general(own_ref[...], panel_ref[here, mine], nt, preferred_element_type=F32)
            pair += lax.dot_general(proj[...], panel_ref[here, sibs], nt, preferred_element_type=F32)
            weighted = jnp.concatenate(
                [
                    (scr_refs[j][:, here].astype(F32) * pair[j * points : (j + 1) * points]).astype(BF16)
                    for j in range(4)
                ],
                0,
            )
            send = jnp.dot(weighted, panel_ref[here, sibs], preferred_element_type=F32)
            keep = jnp.dot(weighted, panel_ref[here, mine], preferred_element_type=F32)
            if k == 0:
                send_ref[...] = send
                keep_ref[...] = keep
            else:
                send_ref[...] += send
                keep_ref[...] += keep

    return pl.pallas_call(
        kernel,
        out_shape=[jax.ShapeDtypeStruct((rows, half), F32)] * 2,
        in_specs=[vmem_spec()] * 7,
        out_specs=[vmem_spec()] * 2,
        scratch_shapes=[pltpu.VMEM((rows, half), BF16)],
        compiler_params=params(24),
        name="direct",
    )(proj_own, proj_other, panel, *weights)


def finish(lefts, keep, got):
    states, points = lefts[0].shape
    cols = keep.shape[1]

    def kernel(*refs):
        left_refs, (keep_ref, got_ref, out_ref, left, high, low) = refs[:4], refs[4:]
        for k in range(4):
            here = slice(k * points, (k + 1) * points)
            there = slice(SIBLING[k] * points, (SIBLING[k] + 1) * points)
            back = keep_ref[here, :] + got_ref[there, :]
            top = back.astype(BF16)
            high[here, :] = top
            low[here, :] = (back - top.astype(F32)).astype(BF16)
            left[:, here] = left_refs[k][...]
        total = jnp.dot(left[...], high[...], preferred_element_type=F32)
        total += jnp.dot(left[...], low[...], preferred_element_type=F32)
        out_ref[...] = total.astype(BF16)

    return pl.pallas_call(
        kernel,
        out_shape=jax.ShapeDtypeStruct((states, cols), BF16),
        in_specs=[vmem_spec()] * 6,
        out_specs=vmem_spec(),
        scratch_shapes=[
            pltpu.VMEM((states, 4 * points), BF16),
            pltpu.VMEM((4 * points, cols), BF16),
            pltpu.VMEM((4 * points, cols), BF16),
        ],
        compiler_params=params(16),
        name="finish",
    )(*lefts, keep, got)


def shards(trial, psi_v, psi_c, screened):
    rows, states = trial.shape[1:]
    half = states // 2
    devices = lax.axis_size(TILE_VEC)
    own = psi_c[:, 0, :].T
    panel = lax.all_gather(own, ("y", "x"), axis=0, tiled=True)
    packed = pack(screened)
    weights = [packed[0], *others(*packed[1:])]
    halves = trial[0].reshape(rows, 2, half).transpose(1, 0, 2)
    outgoing = jnp.broadcast_to(
        halves[None, :, None], (devices // 4, 2, 2, rows, half)
    ).reshape(devices, rows, half)
    trial_half = lax.all_to_all(outgoing, TILE_VEC, split_axis=0, concat_axis=0, tiled=True)
    trial_half = trial_half.reshape(devices * rows, half)
    partner = lax.ppermute(psi_v, "zh", [(0, 1), (1, 0)])
    lefts = [psi_v, swap(psi_v), partner, swap(partner)]
    proj_own = project(trial_half, lefts)
    proj_other = swap(proj_own)
    keep, send = direct(proj_own, proj_other, panel, weights)
    got = swap(send)
    term = finish(lefts, keep, got)
    pieces = lax.all_to_all(
        term.reshape(devices, rows, half), TILE_VEC, split_axis=0, concat_axis=0, tiled=True
    )
    pieces = pieces.reshape(devices // 4, 2, 2, rows, half).astype(F32)
    total = jnp.sum(pieces, axis=(0, 2))
    return total.transpose(1, 0, 2).reshape(1, rows, states)


def solution(mesh):
    split = Mesh(
        mesh.devices.reshape(2, 4, 4, 2, mesh.shape["vec"]),
        TILE_VEC,
    )
    return jax.shard_map(
        shards,
        mesh=split,
        in_specs=(P(None, TILE_VEC, None), P(None, TILE), P(None, "zl", TILE), P(TILE, "zl")),
        out_specs=P(None, TILE_VEC, None),
        check_vma=False,
    )
```

```python
import jax
import jax.numpy as jnp
from jax import lax
from jax.experimental import pallas as pl
from jax.experimental.pallas import tpu as pltpu
from jax.sharding import Mesh
from jax.sharding import PartitionSpec as P

TILE_VEC = ("zh", "y", "x", "core", "zl")
TILE = ("zh", "y", "x", "core")
PLANE = ("y", "x")
ORDER = ("zh", "core", "zl", "y", "x")
STEPS = (0, -1, 1, -2)
F32 = jnp.float32
BF16 = jnp.bfloat16
SIBLING = (1, 0, 3, 2)


def exchange(value, axes):
    return lax.all_to_all(value, axes, split_axis=0, concat_axis=0, tiled=True)


def swap(value):
    return lax.ppermute(value, "core", [(0, 1), (1, 0)])


def others(sibling, partner, diagonal):
    return [
        swap(sibling),
        lax.ppermute(partner, "zh", [(0, 1), (1, 0)]),
        lax.ppermute(diagonal, ("zh", "core"), [(0, 3), (1, 2), (2, 1), (3, 0)]),
    ]


def vmem_spec():
    return pl.BlockSpec(memory_space=pltpu.VMEM)


def hbm_spec():
    return pl.BlockSpec(memory_space=pltpu.HBM)


def params(mebibytes):
    return pltpu.CompilerParams(vmem_limit_bytes=mebibytes * 1024 * 1024)


def pack(screened):
    points, count = screened.shape
    plane, steps = count // 2, 4
    width = plane // 2

    def kernel(in_ref, *out_refs):
        core, zh = lax.axis_index("core"), lax.axis_index("zh")
        rows = in_ref.shape[0]
        low = lax.broadcasted_iota(jnp.int32, (rows, 128), 1) < 64
        first = core == 0
        for far in range(2):
            base = plane * (zh if far == 0 else 1 - zh)
            for m in range(width // 128):
                a = in_ref[:, pl.ds(pl.multiple_of(base + m * 256, 256), 128)]
                b = in_ref[:, pl.ds(pl.multiple_of(base + m * 256 + 128, 128), 128)]
                zero = jnp.where(low, a, pltpu.roll(b, 64, 1))
                one = jnp.where(low, pltpu.roll(a, 64, 1), b)
                here = pl.ds(m * 128, 128)
                for ref, piece in (
                    (out_refs[2 * far], jnp.where(first, zero, one)),
                    (out_refs[2 * far + 1], jnp.where(first, one, zero)),
                ):
                    ref[:, here] = piece.astype(ref.dtype)

    return pl.pallas_call(
        kernel,
        grid=(steps,),
        out_shape=[jax.ShapeDtypeStruct((points, width), kind) for kind in (F32, BF16, BF16, BF16)],
        in_specs=[pl.BlockSpec((points // steps, count), lambda k: (k, 0))],
        out_specs=[pl.BlockSpec((points // steps, width), lambda k: (k, 0))] * 4,
        compiler_params=params(8),
        name="pack",
    )(screened)


def project(rounds, lefts):
    states, points = lefts[0].shape
    block = rounds[0].shape[0] // 2
    cols = rounds[0].shape[1]

    def kernel(*refs):
        trial_refs, left_refs, (out_ref, trial) = refs[:4], refs[4:8], refs[8:]
        core = lax.axis_index("core")
        place = 2 * lax.axis_index("zh") + lax.axis_index("zl")
        for k in range(4):
            source = lax.rem(place + STEPS[k] + 4, 4)
            for m in range(2):
                owner = core if m == 0 else 1 - core
                group = lax.div(source, 2) * 4 + owner * 2 + lax.rem(source, 2)
                trial[pl.ds(pl.multiple_of(group * block, block), block), :] = trial_refs[k][
                    m * block : (m + 1) * block, :
                ]
        for k in range(4):
            part = lax.dot_general(
                left_refs[k][...], trial[...], (((0,), (0,)), ((), ())), preferred_element_type=F32
            )
            out_ref[k * points : (k + 1) * points, :] = part.astype(BF16)

    return pl.pallas_call(
        kernel,
        out_shape=jax.ShapeDtypeStruct((4 * points, cols), BF16),
        in_specs=[vmem_spec()] * 8,
        out_specs=vmem_spec(),
        scratch_shapes=[pltpu.VMEM((states, cols), BF16)],
        compiler_params=params(8),
        name="project",
    )(*rounds, *lefts)


def direct(proj_own, proj_other, panel, weights):
    rows, half = proj_own.shape
    points = rows // 4
    count = panel.shape[0]
    chunk = 512

    def kernel(own_hbm, other_hbm, panel_ref, *refs):
        scr_hbm, (keep_ref, send_ref, own_ref, proj), refs = refs[:4], refs[4:8], refs[8:]
        scr_refs, sems = refs[:4], refs[4]
        core = lax.axis_index("core")
        mine = pl.ds(pl.multiple_of(core * half, half), half)
        sibs = pl.ds(pl.multiple_of((1 - core) * half, half), half)
        first = [pltpu.make_async_copy(own_hbm, own_ref, sems.at[0])]
        for k in range(4):
            source = other_hbm.at[SIBLING[k] * points : (SIBLING[k] + 1) * points, :]
            target = proj.at[k * points : (k + 1) * points, :]
            first.append(pltpu.make_async_copy(source, target, sems.at[1 + k]))
        later = [
            pltpu.make_async_copy(scr_hbm[j], scr_refs[j], sems.at[5 + j]) for j in range(4)
        ]
        for copy in first + later:
            copy.start()
        for copy in first:
            copy.wait()
        nt = (((1,), (1,)), ((), ()))
        for k in range(count // chunk):
            here = pl.ds(k * chunk, chunk)
            pair = lax.dot_general(own_ref[...], panel_ref[here, mine], nt, preferred_element_type=F32)
            pair += lax.dot_general(proj[...], panel_ref[here, sibs], nt, preferred_element_type=F32)
            if k == 0:
                for copy in later:
                    copy.wait()
            weighted = jnp.concatenate(
                [
                    (scr_refs[j][:, here].astype(F32) * pair[j * points : (j + 1) * points]).astype(BF16)
                    for j in range(4)
                ],
                0,
            )
            send = jnp.dot(weighted, panel_ref[here, sibs], preferred_element_type=F32)
            keep = jnp.dot(weighted, panel_ref[here, mine], preferred_element_type=F32)
            if k == 0:
                send_ref[...] = send
                keep_ref[...] = keep
            else:
                send_ref[...] += send
                keep_ref[...] += keep

    return pl.pallas_call(
        kernel,
        out_shape=[jax.ShapeDtypeStruct((rows, half), F32)] * 2,
        in_specs=[hbm_spec(), hbm_spec(), vmem_spec()] + [hbm_spec()] * 4,
        out_specs=[vmem_spec()] * 2,
        scratch_shapes=[
            pltpu.VMEM((rows, half), BF16),
            pltpu.VMEM((rows, half), BF16),
            *(pltpu.VMEM(w.shape, w.dtype) for w in weights),
            pltpu.SemaphoreType.DMA((9,)),
        ],
        compiler_params=params(24),
        name="direct",
    )(proj_own, proj_other, panel, *weights)


def finish(lefts, keep, got):
    states, points = lefts[0].shape
    cols = keep.shape[1]

    def kernel(*refs):
        left_refs, (keep_ref, got_ref, out_ref, left, high, low) = refs[:4], refs[4:]
        for k in range(4):
            here = slice(k * points, (k + 1) * points)
            there = slice(SIBLING[k] * points, (SIBLING[k] + 1) * points)
            back = keep_ref[here, :] + got_ref[there, :]
            top = back.astype(BF16)
            high[here, :] = top
            low[here, :] = (back - top.astype(F32)).astype(BF16)
            left[:, here] = left_refs[k][...]
        total = jnp.dot(left[...], high[...], preferred_element_type=F32)
        total += jnp.dot(left[...], low[...], preferred_element_type=F32)
        out_ref[...] = total.astype(BF16)

    return pl.pallas_call(
        kernel,
        out_shape=jax.ShapeDtypeStruct((states, cols), BF16),
        in_specs=[vmem_spec()] * 6,
        out_specs=vmem_spec(),
        scratch_shapes=[
            pltpu.VMEM((states, 4 * points), BF16),
            pltpu.VMEM((4 * points, cols), BF16),
            pltpu.VMEM((4 * points, cols), BF16),
        ],
        compiler_params=params(16),
        name="finish",
    )(*lefts, keep, got)


def ring(value, by):
    return lax.ppermute(value, ("zh", "zl"), [(k, (k + by) % 4) for k in range(4)])


def to_all(value):
    copies = jnp.broadcast_to(value[None], (lax.axis_size(PLANE), *value.shape))
    return copies


def shards(trial, psi_v, psi_c, screened):
    rows, states = trial.shape[1:]
    half = states // 2
    devices = lax.axis_size(ORDER)
    core = lax.axis_index("core")
    left = psi_v.reshape(2, 4, 4, 2, 2, rows, -1).transpose(0, 3, 4, 1, 2, 5, 6).reshape(psi_v.shape)
    level = exchange(to_all(trial[0]), PLANE).reshape(-1, states)
    outgoing, level = lax.optimization_barrier((to_all(psi_c[:, 0, :].T), level))
    panel = exchange(outgoing, PLANE).reshape(-1, states)
    packed = pack(screened)
    weights = [packed[0], *others(*packed[1:])]
    partner = lax.ppermute(left, "zh", [(0, 1), (1, 0)])
    lefts = [left, swap(left), partner, swap(partner)]
    mine = lax.dynamic_slice_in_dim(level, core * half, half, 1)
    sent = lax.dynamic_slice_in_dim(level, (1 - core) * half, half, 1)
    pieces = jnp.concatenate([mine, swap(sent)], 0)
    rounds = [pieces, ring(pieces, 1), ring(pieces, -1), ring(pieces, 2)]
    proj_own = project(rounds, lefts)
    proj_other = swap(proj_own)
    keep, send = direct(proj_own, proj_other, panel, weights)
    got = swap(send)
    term = finish(lefts, keep, got)
    parts = exchange(term.reshape(devices, rows, half), ORDER)
    parts = parts.reshape(2, 2, 2, -1, rows, half).astype(F32)
    total = jnp.sum(parts, axis=(0, 2, 3))
    return total.transpose(1, 0, 2).reshape(1, rows, states)


def solution(mesh):
    split = Mesh(
        mesh.devices.reshape(2, 4, 4, 2, mesh.shape["vec"]),
        TILE_VEC,
    )
    return jax.shard_map(
        shards,
        mesh=split,
        in_specs=(P(None, TILE_VEC, None), P(None, TILE), P(None, "zl", TILE), P(TILE, "zl")),
        out_specs=P(None, TILE_VEC, None),
        check_vma=False,
    )
```

```python
import jax
import jax.numpy as jnp
from jax import lax
from jax.experimental import pallas as pl
from jax.experimental.pallas import tpu as pltpu
from jax.sharding import Mesh
from jax.sharding import PartitionSpec as P

TILE_VEC = ("zh", "y", "x", "core", "zl")
TILE = ("zh", "y", "x", "core")
PLANE = ("y", "x")
ORDER = ("zh", "core", "zl", "y", "x")
STEPS = (0, -1, 1, -2)
F32 = jnp.float32
BF16 = jnp.bfloat16
SIBLING = (1, 0, 3, 2)


def exchange(value, axes):
    return lax.all_to_all(value, axes, split_axis=0, concat_axis=0, tiled=True)


def swap(value):
    return lax.ppermute(value, "core", [(0, 1), (1, 0)])


def others(sibling, partner, diagonal):
    return [
        swap(sibling),
        lax.ppermute(partner, "zh", [(0, 1), (1, 0)]),
        lax.ppermute(diagonal, ("zh", "core"), [(0, 3), (1, 2), (2, 1), (3, 0)]),
    ]


def vmem_spec():
    return pl.BlockSpec(memory_space=pltpu.VMEM)


def hbm_spec():
    return pl.BlockSpec(memory_space=pltpu.HBM)


def params(mebibytes):
    return pltpu.CompilerParams(vmem_limit_bytes=mebibytes * 1024 * 1024)


def pack(screened):
    points, count = screened.shape
    plane, steps = count // 2, 4
    width = plane // 2

    def kernel(in_ref, *out_refs):
        core, zh = lax.axis_index("core"), lax.axis_index("zh")
        rows = in_ref.shape[0]
        low = lax.broadcasted_iota(jnp.int32, (rows, 128), 1) < 64
        first = core == 0
        for far in range(2):
            base = plane * (zh if far == 0 else 1 - zh)
            for m in range(width // 128):
                a = in_ref[:, pl.ds(pl.multiple_of(base + m * 256, 256), 128)]
                b = in_ref[:, pl.ds(pl.multiple_of(base + m * 256 + 128, 128), 128)]
                zero = jnp.where(low, a, pltpu.roll(b, 64, 1))
                one = jnp.where(low, pltpu.roll(a, 64, 1), b)
                here = pl.ds(m * 128, 128)
                for ref, piece in (
                    (out_refs[2 * far], jnp.where(first, zero, one)),
                    (out_refs[2 * far + 1], jnp.where(first, one, zero)),
                ):
                    ref[:, here] = piece.astype(ref.dtype)

    return pl.pallas_call(
        kernel,
        grid=(steps,),
        out_shape=[jax.ShapeDtypeStruct((points, width), kind) for kind in (F32, BF16, BF16, BF16)],
        in_specs=[pl.BlockSpec((points // steps, count), lambda k: (k, 0))],
        out_specs=[pl.BlockSpec((points // steps, width), lambda k: (k, 0))] * 4,
        compiler_params=params(8),
        name="pack",
    )(screened)


def project(rounds, lefts):
    states, points = lefts[0].shape
    block = rounds[0].shape[0] // 2
    cols = rounds[0].shape[1]

    def kernel(*refs):
        trial_refs, left_refs, (out_ref, trial) = refs[:4], refs[4:8], refs[8:]
        core = lax.axis_index("core")
        place = 2 * lax.axis_index("zh") + lax.axis_index("zl")
        for k in range(4):
            source = lax.rem(place + STEPS[k] + 4, 4)
            for m in range(2):
                owner = core if m == 0 else 1 - core
                group = lax.div(source, 2) * 4 + owner * 2 + lax.rem(source, 2)
                trial[pl.ds(pl.multiple_of(group * block, block), block), :] = trial_refs[k][
                    m * block : (m + 1) * block, :
                ]
        for k in range(4):
            part = lax.dot_general(
                left_refs[k][...], trial[...], (((0,), (0,)), ((), ())), preferred_element_type=F32
            )
            out_ref[k * points : (k + 1) * points, :] = part.astype(BF16)

    return pl.pallas_call(
        kernel,
        out_shape=jax.ShapeDtypeStruct((4 * points, cols), BF16),
        in_specs=[vmem_spec()] * 8,
        out_specs=vmem_spec(),
        scratch_shapes=[pltpu.VMEM((states, cols), BF16)],
        compiler_params=params(8),
        name="project",
    )(*rounds, *lefts)


def direct(proj_own, proj_other, panel, weights):
    rows, half = proj_own.shape
    points = rows // 4
    count, states = panel.shape
    chunk = 256

    def kernel(own_hbm, other_hbm, panel_hbm, *refs):
        scr_hbm, (keep_ref, send_ref, own_ref, proj, panel_ref), refs = refs[:4], refs[4:9], refs[9:]
        scr_refs, (sems, chunk_sems) = refs[:4], refs[4:]
        core = lax.axis_index("core")
        mine = pl.ds(pl.multiple_of(core * half, half), half)
        sibs = pl.ds(pl.multiple_of((1 - core) * half, half), half)
        first = [pltpu.make_async_copy(own_hbm, own_ref, sems.at[0])]
        for k in range(4):
            source = other_hbm.at[SIBLING[k] * points : (SIBLING[k] + 1) * points, :]
            target = proj.at[k * points : (k + 1) * points, :]
            first.append(pltpu.make_async_copy(source, target, sems.at[1 + k]))
        chunks = []
        for k in range(count // chunk):
            here = pl.ds(k * chunk, chunk)
            chunks.append(
                [pltpu.make_async_copy(panel_hbm.at[here, :], panel_ref.at[here, :], chunk_sems.at[k, 0])]
                + [
                    pltpu.make_async_copy(
                        scr_hbm[j].at[:, here], scr_refs[j].at[:, here], chunk_sems.at[k, 1 + j]
                    )
                    for j in range(4)
                ]
            )
        for copies in (first, *chunks):
            for copy in copies:
                copy.start()
        for copy in first:
            copy.wait()
        nt = (((1,), (1,)), ((), ()))
        for k in range(count // chunk):
            here = pl.ds(k * chunk, chunk)
            for copy in chunks[k]:
                copy.wait()
            pair = lax.dot_general(own_ref[...], panel_ref[here, mine], nt, preferred_element_type=F32)
            pair += lax.dot_general(proj[...], panel_ref[here, sibs], nt, preferred_element_type=F32)
            weighted = jnp.concatenate(
                [
                    (scr_refs[j][:, here].astype(F32) * pair[j * points : (j + 1) * points]).astype(BF16)
                    for j in range(4)
                ],
                0,
            )
            send = jnp.dot(weighted, panel_ref[here, sibs], preferred_element_type=F32)
            keep = jnp.dot(weighted, panel_ref[here, mine], preferred_element_type=F32)
            if k == 0:
                send_ref[...] = send
                keep_ref[...] = keep
            else:
                send_ref[...] += send
                keep_ref[...] += keep

    return pl.pallas_call(
        kernel,
        out_shape=[jax.ShapeDtypeStruct((rows, half), F32)] * 2,
        in_specs=[hbm_spec()] * 7,
        out_specs=[vmem_spec()] * 2,
        scratch_shapes=[
            pltpu.VMEM((rows, half), BF16),
            pltpu.VMEM((rows, half), BF16),
            pltpu.VMEM((count, states), BF16),
            *(pltpu.VMEM(w.shape, w.dtype) for w in weights),
            pltpu.SemaphoreType.DMA((5,)),
            pltpu.SemaphoreType.DMA((count // chunk, 5)),
        ],
        compiler_params=params(58),
        name="direct",
    )(proj_own, proj_other, panel, *weights)


def finish(lefts, keep, got):
    states, points = lefts[0].shape
    cols = keep.shape[1]

    def kernel(*refs):
        left_refs, (keep_ref, got_ref, out_ref, left, high, low) = refs[:4], refs[4:]
        for k in range(4):
            here = slice(k * points, (k + 1) * points)
            there = slice(SIBLING[k] * points, (SIBLING[k] + 1) * points)
            back = keep_ref[here, :] + got_ref[there, :]
            top = back.astype(BF16)
            high[here, :] = top
            low[here, :] = (back - top.astype(F32)).astype(BF16)
            left[:, here] = left_refs[k][...]
        total = jnp.dot(left[...], high[...], preferred_element_type=F32)
        total += jnp.dot(left[...], low[...], preferred_element_type=F32)
        out_ref[...] = total.astype(BF16)

    return pl.pallas_call(
        kernel,
        out_shape=jax.ShapeDtypeStruct((states, cols), BF16),
        in_specs=[vmem_spec()] * 6,
        out_specs=vmem_spec(),
        scratch_shapes=[
            pltpu.VMEM((states, 4 * points), BF16),
            pltpu.VMEM((4 * points, cols), BF16),
            pltpu.VMEM((4 * points, cols), BF16),
        ],
        compiler_params=params(16),
        name="finish",
    )(*lefts, keep, got)


def ring(value, by):
    return lax.ppermute(value, ("zh", "zl"), [(k, (k + by) % 4) for k in range(4)])


def to_all(value):
    copies = jnp.broadcast_to(value[None], (lax.axis_size(PLANE), *value.shape))
    return copies


def shards(trial, psi_v, psi_c, screened):
    rows, states = trial.shape[1:]
    half = states // 2
    devices = lax.axis_size(ORDER)
    core = lax.axis_index("core")
    left = psi_v.reshape(2, 4, 4, 2, 2, rows, -1).transpose(0, 3, 4, 1, 2, 5, 6).reshape(psi_v.shape)
    packed = pack(screened)
    copies, packed = lax.optimization_barrier((to_all(trial[0]), packed))
    level = exchange(copies, PLANE).reshape(-1, states)
    weights = [packed[0], *others(*packed[1:])]
    partner = lax.ppermute(left, "zh", [(0, 1), (1, 0)])
    outgoing, level, weights, partner = lax.optimization_barrier(
        (to_all(psi_c[:, 0, :].T), level, weights, partner)
    )
    panel = exchange(outgoing, PLANE).reshape(-1, states)
    lefts = [left, swap(left), partner, swap(partner)]
    mine = lax.dynamic_slice_in_dim(level, core * half, half, 1)
    sent = lax.dynamic_slice_in_dim(level, (1 - core) * half, half, 1)
    pieces = jnp.concatenate([mine, swap(sent)], 0)
    rounds = [pieces, ring(pieces, 1), ring(pieces, -1), ring(pieces, 2)]
    proj_own = project(rounds, lefts)
    proj_other = swap(proj_own)
    keep, send = direct(proj_own, proj_other, panel, weights)
    got = swap(send)
    term = finish(lefts, keep, got)
    parts = exchange(term.reshape(devices, rows, half), ORDER)
    parts = parts.reshape(2, 2, 2, -1, rows, half).astype(F32)
    total = jnp.sum(parts, axis=(0, 2, 3))
    return total.transpose(1, 0, 2).reshape(1, rows, states)


def solution(mesh):
    split = Mesh(
        mesh.devices.reshape(2, 4, 4, 2, mesh.shape["vec"]),
        TILE_VEC,
    )
    return jax.shard_map(
        shards,
        mesh=split,
        in_specs=(P(None, TILE_VEC, None), P(None, TILE), P(None, "zl", TILE), P(TILE, "zl")),
        out_specs=P(None, TILE_VEC, None),
        check_vma=False,
    )
```

```python
import jax
import jax.numpy as jnp
from jax import lax
from jax.experimental import pallas as pl
from jax.experimental.pallas import tpu as pltpu
from jax.sharding import Mesh
from jax.sharding import PartitionSpec as P

TILE_VEC = ("zh", "y", "x", "core", "zl")
TILE = ("zh", "y", "x", "core")
PLANE = ("y", "x")
ORDER = ("zh", "core", "zl", "y", "x")
STEPS = (0, -1, 1, -2)
F32 = jnp.float32
BF16 = jnp.bfloat16
SIBLING = (1, 0, 3, 2)


def shift(value, axis, by):
    n = lax.axis_size(axis)
    return lax.ppermute(value, axis, [(k, (k + by) % n) for k in range(n)])


def exchange(value, axes):
    return lax.all_to_all(value, axes, split_axis=0, concat_axis=0, tiled=True)


def swap(value):
    return lax.ppermute(value, "core", [(0, 1), (1, 0)])


def vmem_spec():
    return pl.BlockSpec(memory_space=pltpu.VMEM)


def params(mebibytes):
    return pltpu.CompilerParams(vmem_limit_bytes=mebibytes * 1024 * 1024)


def pack(screened, left):
    points, count = screened.shape
    plane, steps = count // 2, 4
    width = plane // 2
    rows = points // steps

    def kernel(in_ref, left_ref, own_ref, near_ref, far_ref):
        core, zh = lax.axis_index("core"), lax.axis_index("zh")
        low = lax.broadcasted_iota(jnp.int32, (rows, 128), 1) < 64
        first = core == 0
        for far in range(2):
            base = plane * (zh if far == 0 else 1 - zh)
            for m in range(width // 128):
                a = in_ref[:, pl.ds(pl.multiple_of(base + m * 256, 256), 128)]
                b = in_ref[:, pl.ds(pl.multiple_of(base + m * 256 + 128, 128), 128)]
                zero = jnp.where(low, a, pltpu.roll(b, 64, 1))
                one = jnp.where(low, pltpu.roll(a, 64, 1), b)
                here = pl.ds(m * 128, 128)
                mine, others = jnp.where(first, zero, one), jnp.where(first, one, zero)
                if far == 0:
                    own_ref[:, here] = mine
                    near_ref[0, :, here] = others.astype(BF16)
                else:
                    far_ref[0, :, here] = mine.astype(BF16)
                    far_ref[1, :, here] = others.astype(BF16)
        for g in range(left_ref.shape[0] // points):
            start = pl.multiple_of(g * points + pl.program_id(0) * rows, rows)
            piece = left_ref[pl.ds(start, rows), :]
            near_ref[1, :, pl.ds(g * points, points)] = piece
            far_ref[2, :, pl.ds(g * points, points)] = piece

    return pl.pallas_call(
        kernel,
        grid=(steps,),
        out_shape=[
            jax.ShapeDtypeStruct((points, width), F32),
            jax.ShapeDtypeStruct((2, points, width), BF16),
            jax.ShapeDtypeStruct((3, points, width), BF16),
        ],
        in_specs=[
            pl.BlockSpec((rows, count), lambda k: (k, 0)),
            pl.BlockSpec(left.shape, lambda k: (0, 0)),
        ],
        out_specs=[
            pl.BlockSpec((rows, width), lambda k: (k, 0)),
            pl.BlockSpec((2, rows, width), lambda k: (0, k, 0)),
            pl.BlockSpec((3, rows, width), lambda k: (0, k, 0)),
        ],
        compiler_params=params(8),
        name="pack",
    )(screened, left)


def project(rounds, left, near, far, passed):
    states, points = left.shape
    block = rounds[0].shape[0] // 2
    cols = rounds[0].shape[1]

    def kernel(*refs):
        trial_refs, left_ref, boxes, (out_ref, psi_ref, trial) = refs[:4], refs[4], refs[5:8], refs[8:]
        core = lax.axis_index("core")
        place = 2 * lax.axis_index("zh") + lax.axis_index("zl")
        for k in range(4):
            source = lax.rem(place + STEPS[k] + 4, 4)
            for m in range(2):
                owner = core if m == 0 else 1 - core
                group = lax.div(source, 2) * 4 + owner * 2 + lax.rem(source, 2)
                trial[pl.ds(pl.multiple_of(group * block, block), block), :] = trial_refs[k][
                    m * block : (m + 1) * block, :
                ]
        psi_ref[:, :points] = left_ref[...]
        for k in range(1, 4):
            box = boxes[k - 1]
            for g in range(states // points):
                psi_ref[g * points : (g + 1) * points, k * points : (k + 1) * points] = box[
                    box.shape[0] - 1, :, g * points : (g + 1) * points
                ]
        out_ref[...] = lax.dot_general(
            psi_ref[...], trial[...], (((0,), (0,)), ((), ())), preferred_element_type=F32
        ).astype(BF16)

    return pl.pallas_call(
        kernel,
        out_shape=[
            jax.ShapeDtypeStruct((4 * points, cols), BF16),
            jax.ShapeDtypeStruct((states, 4 * points), BF16),
        ],
        in_specs=[vmem_spec()] * 8,
        out_specs=[vmem_spec()] * 2,
        scratch_shapes=[pltpu.VMEM((states, cols), BF16)],
        compiler_params=params(12),
        name="project",
    )(*rounds, left, near, far, passed)


def direct(proj_own, proj_other, lines, own, boxes):
    rows, half = proj_own.shape
    points = rows // 4
    block = lines[0].shape[0] // 2
    count, states = 16 * block, lines[0].shape[1]
    chunk = 512

    def kernel(own_ref, other_ref, *refs):
        line_refs, scr_refs, (keep_ref, send_ref, proj, panel_ref) = refs[:8], refs[8:12], refs[12:]
        y, x = lax.axis_index("y"), lax.axis_index("x")
        for k in range(16):
            at = lax.rem(y + STEPS[k // 4] + 4, 4) * 4 + lax.rem(x + STEPS[k % 4] + 4, 4)
            panel_ref[pl.ds(pl.multiple_of(at * block, block), block), :] = line_refs[k // 2][
                k % 2 * block : (k % 2 + 1) * block, :
            ]
        core = lax.axis_index("core")
        mine = pl.ds(pl.multiple_of(core * half, half), half)
        sibs = pl.ds(pl.multiple_of((1 - core) * half, half), half)
        for k in range(4):
            proj[k * points : (k + 1) * points, :] = other_ref[
                SIBLING[k] * points : (SIBLING[k] + 1) * points, :
            ]
        nt = (((1,), (1,)), ((), ()))
        for k in range(count // chunk):
            here = pl.ds(k * chunk, chunk)
            pair = lax.dot_general(own_ref[...], panel_ref[here, mine], nt, preferred_element_type=F32)
            pair += lax.dot_general(proj[...], panel_ref[here, sibs], nt, preferred_element_type=F32)
            weighted = jnp.concatenate(
                [
                    (
                        (scr_refs[0][:, here] if j == 0 else scr_refs[j][0, :, here].astype(F32))
                        * pair[j * points : (j + 1) * points]
                    ).astype(BF16)
                    for j in range(4)
                ],
                0,
            )
            send = jnp.dot(weighted, panel_ref[here, sibs], preferred_element_type=F32)
            keep = jnp.dot(weighted, panel_ref[here, mine], preferred_element_type=F32)
            if k == 0:
                send_ref[...] = send
                keep_ref[...] = keep
            else:
                send_ref[...] += send
                keep_ref[...] += keep

    return pl.pallas_call(
        kernel,
        out_shape=[jax.ShapeDtypeStruct((rows, half), F32)] * 2,
        in_specs=[vmem_spec()] * 14,
        out_specs=[vmem_spec()] * 2,
        scratch_shapes=[pltpu.VMEM((rows, half), BF16), pltpu.VMEM((count, states), BF16)],
        compiler_params=params(24),
        name="direct",
    )(proj_own, proj_other, *lines, own, *boxes)


def finish(psi, keep, got):
    states, count = psi.shape
    points = count // 4
    cols = keep.shape[1]

    def kernel(psi_ref, keep_ref, got_ref, out_ref, high, low):
        for k in range(4):
            here = slice(k * points, (k + 1) * points)
            there = slice(SIBLING[k] * points, (SIBLING[k] + 1) * points)
            back = keep_ref[here, :] + got_ref[there, :]
            top = back.astype(BF16)
            high[here, :] = top
            low[here, :] = (back - top.astype(F32)).astype(BF16)
        total = jnp.dot(psi_ref[...], high[...], preferred_element_type=F32)
        total += jnp.dot(psi_ref[...], low[...], preferred_element_type=F32)
        out_ref[...] = total.astype(BF16)

    return pl.pallas_call(
        kernel,
        out_shape=jax.ShapeDtypeStruct((states, cols), BF16),
        in_specs=[vmem_spec()] * 3,
        out_specs=vmem_spec(),
        scratch_shapes=[pltpu.VMEM((count, cols), BF16)] * 2,
        compiler_params=params(16),
        name="finish",
    )(psi, keep, got)


def ring(value, by):
    return lax.ppermute(value, ("zh", "zl"), [(k, (k + by) % 4) for k in range(4)])


def to_all(value):
    copies = jnp.broadcast_to(value[None], (lax.axis_size(PLANE), *value.shape))
    return copies


def shards(trial, psi_v, psi_c, screened):
    rows, states = trial.shape[1:]
    half = states // 2
    devices = lax.axis_size(ORDER)
    core = lax.axis_index("core")
    left = psi_v.reshape(2, 4, 4, 2, 2, rows, -1).transpose(0, 3, 4, 1, 2, 5, 6).reshape(psi_v.shape)
    own, near, far = pack(screened, left)
    block = psi_c[:, 0, :].T
    line = [
        jnp.concatenate([block, shift(block, "x", 1)], 0),
        jnp.concatenate([shift(block, "x", -1), shift(block, "x", 2)], 0),
    ]
    copies, near, far = lax.optimization_barrier((to_all(trial[0]), near, far))
    level = exchange(copies, PLANE).reshape(-1, states)
    near = swap(near)
    far = lax.ppermute(far, "zh", [(0, 1), (1, 0)])
    behind = [shift(part, "y", 1) for part in line]
    ahead = [shift(part, "y", -1) for part in line]
    mine = lax.dynamic_slice_in_dim(level, core * half, half, 1)
    sent = lax.dynamic_slice_in_dim(level, (1 - core) * half, half, 1)
    pieces = jnp.concatenate([mine, swap(sent)], 0)
    pieces, near, far, behind[0], ahead[1] = lax.optimization_barrier(
        (pieces, near, far, behind[0], ahead[1])
    )
    passed = swap(far[1:])
    rounds = [pieces, ring(pieces, 1), ring(pieces, -1), ring(pieces, 2)]
    beyond = [shift(behind[0], "y", 1), shift(ahead[1], "y", -1)]
    rounds, behind[1], ahead[0], beyond = lax.optimization_barrier(
        (rounds, behind[1], ahead[0], beyond)
    )
    proj_own, psi = project(rounds, left, near, far, passed)
    proj_other = swap(proj_own)
    panel = [*line, *behind, *ahead, *beyond]
    keep, send = direct(proj_own, proj_other, panel, own, [near, far, passed])
    got = swap(send)
    term = finish(psi, keep, got)
    parts = exchange(term.reshape(devices, rows, half), ORDER)
    parts = parts.reshape(2, 2, 2, -1, rows, half).astype(F32)
    total = jnp.sum(parts, axis=(0, 2, 3))
    return total.transpose(1, 0, 2).reshape(1, rows, states)


def solution(mesh):
    split = Mesh(
        mesh.devices.reshape(2, 4, 4, 2, mesh.shape["vec"]),
        TILE_VEC,
    )
    return jax.shard_map(
        shards,
        mesh=split,
        in_specs=(P(None, TILE_VEC, None), P(None, TILE), P(None, "zl", TILE), P(TILE, "zl")),
        out_specs=P(None, TILE_VEC, None),
        check_vma=False,
    )
```

```python
import jax
import jax.numpy as jnp
from jax import lax
from jax.experimental import pallas as pl
from jax.experimental.pallas import tpu as pltpu
from jax.sharding import Mesh
from jax.sharding import PartitionSpec as P

TILE_VEC = ("zh", "y", "x", "core", "zl")
TILE = ("zh", "y", "x", "core")
PLANE = ("y", "x")
ORDER = ("zh", "core", "zl", "y", "x")
STEPS = (0, -1, 1, -2)
F32 = jnp.float32
BF16 = jnp.bfloat16
SIBLING = (1, 0, 3, 2)


def shift(value, axis, by):
    n = lax.axis_size(axis)
    return lax.ppermute(value, axis, [(k, (k + by) % n) for k in range(n)])


def exchange(value, axes):
    return lax.all_to_all(value, axes, split_axis=0, concat_axis=0, tiled=True)


def swap(value):
    return lax.ppermute(value, "core", [(0, 1), (1, 0)])


def vmem_spec():
    return pl.BlockSpec(memory_space=pltpu.VMEM)


def params(mebibytes):
    return pltpu.CompilerParams(vmem_limit_bytes=mebibytes * 1024 * 1024)


def pack(screened, left):
    points, count = screened.shape
    plane, steps = count // 2, 4
    width = plane // 2
    rows = points // steps

    def kernel(in_ref, left_ref, own_ref, near_ref, far_ref):
        core, zh = lax.axis_index("core"), lax.axis_index("zh")
        low = lax.broadcasted_iota(jnp.int32, (rows, 128), 1) < 64
        first = core == 0
        for far in range(2):
            base = plane * (zh if far == 0 else 1 - zh)
            for m in range(width // 128):
                a = in_ref[:, pl.ds(pl.multiple_of(base + m * 256, 256), 128)]
                b = in_ref[:, pl.ds(pl.multiple_of(base + m * 256 + 128, 128), 128)]
                zero = jnp.where(low, a, pltpu.roll(b, 64, 1))
                one = jnp.where(low, pltpu.roll(a, 64, 1), b)
                here = pl.ds(m * 128, 128)
                mine, others = jnp.where(first, zero, one), jnp.where(first, one, zero)
                if far == 0:
                    own_ref[:, here] = mine
                    near_ref[0, :, here] = others.astype(BF16)
                else:
                    far_ref[0, :, here] = mine.astype(BF16)
                    far_ref[1, :, here] = others.astype(BF16)
        for g in range(left_ref.shape[0] // points):
            start = pl.multiple_of(g * points + pl.program_id(0) * rows, rows)
            piece = left_ref[pl.ds(start, rows), :]
            near_ref[1, :, pl.ds(g * points, points)] = piece
            far_ref[2, :, pl.ds(g * points, points)] = piece

    return pl.pallas_call(
        kernel,
        grid=(steps,),
        out_shape=[
            jax.ShapeDtypeStruct((points, width), F32),
            jax.ShapeDtypeStruct((2, points, width), BF16),
            jax.ShapeDtypeStruct((3, points, width), BF16),
        ],
        in_specs=[
            pl.BlockSpec((rows, count), lambda k: (k, 0)),
            pl.BlockSpec(left.shape, lambda k: (0, 0)),
        ],
        out_specs=[
            pl.BlockSpec((rows, width), lambda k: (k, 0)),
            pl.BlockSpec((2, rows, width), lambda k: (0, k, 0)),
            pl.BlockSpec((3, rows, width), lambda k: (0, k, 0)),
        ],
        compiler_params=params(8),
        name="pack",
    )(screened, left)


def project(rounds, left, near, far, passed):
    states, points = left.shape
    block = rounds[0].shape[0] // 2
    cols = rounds[0].shape[1]

    def kernel(*refs):
        trial_refs, left_ref, boxes, (out_ref, psi_ref, trial) = refs[:4], refs[4], refs[5:8], refs[8:]
        core = lax.axis_index("core")
        place = 2 * lax.axis_index("zh") + lax.axis_index("zl")
        for k in range(4):
            source = lax.rem(place + STEPS[k] + 4, 4)
            for m in range(2):
                owner = core if m == 0 else 1 - core
                group = lax.div(source, 2) * 4 + owner * 2 + lax.rem(source, 2)
                trial[pl.ds(pl.multiple_of(group * block, block), block), :] = trial_refs[k][
                    m * block : (m + 1) * block, :
                ]
        psi_ref[:, :points] = left_ref[...]
        for k in range(1, 4):
            box = boxes[k - 1]
            for g in range(states // points):
                psi_ref[g * points : (g + 1) * points, k * points : (k + 1) * points] = box[
                    box.shape[0] - 1, :, g * points : (g + 1) * points
                ]
        out_ref[...] = lax.dot_general(
            psi_ref[...], trial[...], (((0,), (0,)), ((), ())), preferred_element_type=F32
        ).astype(BF16)

    return pl.pallas_call(
        kernel,
        out_shape=[
            jax.ShapeDtypeStruct((4 * points, cols), BF16),
            jax.ShapeDtypeStruct((states, 4 * points), BF16),
        ],
        in_specs=[vmem_spec()] * 8,
        out_specs=[vmem_spec()] * 2,
        scratch_shapes=[pltpu.VMEM((states, cols), BF16)],
        compiler_params=params(12),
        name="project",
    )(*rounds, left, near, far, passed)


def direct(proj_own, proj_other, lines, own, boxes):
    rows, half = proj_own.shape
    points = rows // 4
    block = lines[0].shape[0] // 2
    count, states = 16 * block, lines[0].shape[1]
    chunk = 512

    def kernel(own_ref, other_ref, *refs):
        line_refs, scr_refs, (keep_ref, send_ref, proj, panel_ref) = refs[:8], refs[8:12], refs[12:]
        y, x = lax.axis_index("y"), lax.axis_index("x")
        for k in range(16):
            at = lax.rem(y + STEPS[k // 4] + 4, 4) * 4 + lax.rem(x + STEPS[k % 4] + 4, 4)
            panel_ref[pl.ds(pl.multiple_of(at * block, block), block), :] = line_refs[k // 2][
                k % 2 * block : (k % 2 + 1) * block, :
            ]
        core = lax.axis_index("core")
        mine = pl.ds(pl.multiple_of(core * half, half), half)
        sibs = pl.ds(pl.multiple_of((1 - core) * half, half), half)
        for k in range(4):
            proj[k * points : (k + 1) * points, :] = other_ref[
                SIBLING[k] * points : (SIBLING[k] + 1) * points, :
            ]
        nt = (((1,), (1,)), ((), ()))
        for k in range(count // chunk):
            here = pl.ds(k * chunk, chunk)
            pair = lax.dot_general(own_ref[...], panel_ref[here, mine], nt, preferred_element_type=F32)
            pair += lax.dot_general(proj[...], panel_ref[here, sibs], nt, preferred_element_type=F32)
            weighted = jnp.concatenate(
                [
                    (
                        (scr_refs[0][:, here] if j == 0 else scr_refs[j][0, :, here].astype(F32))
                        * pair[j * points : (j + 1) * points]
                    ).astype(BF16)
                    for j in range(4)
                ],
                0,
            )
            send = jnp.dot(weighted, panel_ref[here, sibs], preferred_element_type=F32)
            keep = jnp.dot(weighted, panel_ref[here, mine], preferred_element_type=F32)
            if k == 0:
                send_ref[...] = send
                keep_ref[...] = keep
            else:
                send_ref[...] += send
                keep_ref[...] += keep

    return pl.pallas_call(
        kernel,
        out_shape=[jax.ShapeDtypeStruct((rows, half), F32)] * 2,
        in_specs=[vmem_spec()] * 14,
        out_specs=[vmem_spec()] * 2,
        scratch_shapes=[pltpu.VMEM((rows, half), BF16), pltpu.VMEM((count, states), BF16)],
        compiler_params=params(24),
        name="direct",
    )(proj_own, proj_other, *lines, own, *boxes)


def finish(psi, keep, got):
    states, count = psi.shape
    points = count // 4
    cols = keep.shape[1]

    def kernel(psi_ref, keep_ref, got_ref, out_ref, high, low):
        for k in range(4):
            here = slice(k * points, (k + 1) * points)
            there = slice(SIBLING[k] * points, (SIBLING[k] + 1) * points)
            back = keep_ref[here, :] + got_ref[there, :]
            top = back.astype(BF16)
            high[here, :] = top
            low[here, :] = (back - top.astype(F32)).astype(BF16)
        total = jnp.dot(psi_ref[...], high[...], preferred_element_type=F32)
        total += jnp.dot(psi_ref[...], low[...], preferred_element_type=F32)
        out_ref[...] = total.astype(BF16)

    return pl.pallas_call(
        kernel,
        out_shape=jax.ShapeDtypeStruct((states, cols), BF16),
        in_specs=[vmem_spec()] * 3,
        out_specs=vmem_spec(),
        scratch_shapes=[pltpu.VMEM((count, cols), BF16)] * 2,
        compiler_params=params(16),
        name="finish",
    )(psi, keep, got)


def ring(value, by):
    return lax.ppermute(value, ("zh", "zl"), [(k, (k + by) % 4) for k in range(4)])


def to_all(value):
    copies = jnp.broadcast_to(value[None], (lax.axis_size(PLANE), *value.shape))
    return copies


def shards(trial, psi_v, psi_c, screened):
    rows, states = trial.shape[1:]
    half = states // 2
    devices = lax.axis_size(ORDER)
    core = lax.axis_index("core")
    left = psi_v.reshape(2, 4, 4, 2, 2, rows, -1).transpose(0, 3, 4, 1, 2, 5, 6).reshape(psi_v.shape)
    own, near, far = pack(screened, left)
    block = psi_c[:, 0, :].T
    line = [
        jnp.concatenate([block, shift(block, "x", 1)], 0),
        jnp.concatenate([shift(block, "x", -1), shift(block, "x", 2)], 0),
    ]
    copies, near, far = lax.optimization_barrier((to_all(trial[0]), near, far))
    level = exchange(copies, PLANE).reshape(-1, states)
    near = swap(near)
    far = lax.ppermute(far, "zh", [(0, 1), (1, 0)])
    behind = [shift(part, "y", 1) for part in line]
    ahead = [shift(part, "y", -1) for part in line]
    mine = lax.dynamic_slice_in_dim(level, core * half, half, 1)
    sent = lax.dynamic_slice_in_dim(level, (1 - core) * half, half, 1)
    pieces = jnp.concatenate([mine, swap(sent)], 0)
    pieces, near, far, behind[0], ahead[1] = lax.optimization_barrier(
        (pieces, near, far, behind[0], ahead[1])
    )
    passed = swap(far[1:])
    rounds = [pieces, ring(pieces, 1), ring(pieces, -1), ring(pieces, 2)]
    beyond = [shift(behind[0], "y", 1), shift(ahead[1], "y", -1)]
    proj_own, psi = project(rounds, left, near, far, passed)
    proj_own, behind[1], ahead[0], beyond = lax.optimization_barrier(
        (proj_own, behind[1], ahead[0], beyond)
    )
    proj_other = swap(proj_own)
    panel = [*line, *behind, *ahead, *beyond]
    keep, send = direct(proj_own, proj_other, panel, own, [near, far, passed])
    got = swap(send)
    term = finish(psi, keep, got)
    parts = exchange(term.reshape(devices, rows, half), ORDER)
    parts = parts.reshape(2, 2, 2, -1, rows, half).astype(F32)
    total = jnp.sum(parts, axis=(0, 2, 3))
    return total.transpose(1, 0, 2).reshape(1, rows, states)


def solution(mesh):
    split = Mesh(
        mesh.devices.reshape(2, 4, 4, 2, mesh.shape["vec"]),
        TILE_VEC,
    )
    return jax.shard_map(
        shards,
        mesh=split,
        in_specs=(P(None, TILE_VEC, None), P(None, TILE), P(None, "zl", TILE), P(TILE, "zl")),
        out_specs=P(None, TILE_VEC, None),
        check_vma=False,
    )
```

```python
import jax
import jax.numpy as jnp
from jax import lax
from jax.experimental import pallas as pl
from jax.experimental.pallas import tpu as pltpu
from jax.sharding import Mesh
from jax.sharding import PartitionSpec as P

TILE_VEC = ("zh", "y", "x", "core", "zl")
TILE = ("zh", "y", "x", "core")
PLANE = ("y", "x")
ORDER = ("y", "x", "zh", "zl", "core")
STEPS = (0, -1, 1, -2)
F32 = jnp.float32
BF16 = jnp.bfloat16
SIBLING = (1, 0, 3, 2)


def shift(value, axis, by):
    n = lax.axis_size(axis)
    return lax.ppermute(value, axis, [(k, (k + by) % n) for k in range(n)])


def exchange(value, axes):
    return lax.all_to_all(value, axes, split_axis=0, concat_axis=0, tiled=True)


def swap(value):
    return lax.ppermute(value, "core", [(0, 1), (1, 0)])


def vmem_spec():
    return pl.BlockSpec(memory_space=pltpu.VMEM)


def params(mebibytes):
    return pltpu.CompilerParams(vmem_limit_bytes=mebibytes * 1024 * 1024)


def pack(screened, left):
    points, count = screened.shape
    plane, steps = count // 2, 4
    width = plane // 2
    rows = points // steps

    def kernel(in_ref, left_ref, own_ref, near_ref, far_ref):
        core, zh = lax.axis_index("core"), lax.axis_index("zh")
        low = lax.broadcasted_iota(jnp.int32, (rows, 128), 1) < 64
        first = core == 0
        for far in range(2):
            base = plane * (zh if far == 0 else 1 - zh)
            for m in range(width // 128):
                a = in_ref[:, pl.ds(pl.multiple_of(base + m * 256, 256), 128)]
                b = in_ref[:, pl.ds(pl.multiple_of(base + m * 256 + 128, 128), 128)]
                zero = jnp.where(low, a, pltpu.roll(b, 64, 1))
                one = jnp.where(low, pltpu.roll(a, 64, 1), b)
                here = pl.ds(m * 128, 128)
                mine, others = jnp.where(first, zero, one), jnp.where(first, one, zero)
                if far == 0:
                    own_ref[:, here] = mine
                    near_ref[0, :, here] = others.astype(BF16)
                else:
                    far_ref[0, :, here] = mine.astype(BF16)
                    far_ref[1, :, here] = others.astype(BF16)
        for g in range(left_ref.shape[0] // points):
            start = pl.multiple_of(g * points + pl.program_id(0) * rows, rows)
            piece = left_ref[pl.ds(start, rows), :]
            near_ref[1, :, pl.ds(g * points, points)] = piece
            far_ref[2, :, pl.ds(g * points, points)] = piece

    return pl.pallas_call(
        kernel,
        grid=(steps,),
        out_shape=[
            jax.ShapeDtypeStruct((points, width), F32),
            jax.ShapeDtypeStruct((2, points, width), BF16),
            jax.ShapeDtypeStruct((3, points, width), BF16),
        ],
        in_specs=[
            pl.BlockSpec((rows, count), lambda k: (k, 0)),
            pl.BlockSpec(left.shape, lambda k: (0, 0)),
        ],
        out_specs=[
            pl.BlockSpec((rows, width), lambda k: (k, 0)),
            pl.BlockSpec((2, rows, width), lambda k: (0, k, 0)),
            pl.BlockSpec((3, rows, width), lambda k: (0, k, 0)),
        ],
        compiler_params=params(8),
        name="pack",
    )(screened, left)


def project(trial_half, left, near, far, passed):
    states, points = left.shape
    cols = trial_half.shape[1]

    def kernel(trial_ref, left_ref, *refs):
        boxes, (out_ref, psi_ref) = refs[:3], refs[3:]
        psi_ref[:, :points] = left_ref[...]
        for k in range(1, 4):
            box = boxes[k - 1]
            for g in range(states // points):
                psi_ref[g * points : (g + 1) * points, k * points : (k + 1) * points] = box[
                    box.shape[0] - 1, :, g * points : (g + 1) * points
                ]
        out_ref[...] = lax.dot_general(
            psi_ref[...], trial_ref[...], (((0,), (0,)), ((), ())), preferred_element_type=F32
        ).astype(BF16)

    return pl.pallas_call(
        kernel,
        out_shape=[
            jax.ShapeDtypeStruct((4 * points, cols), BF16),
            jax.ShapeDtypeStruct((states, 4 * points), BF16),
        ],
        in_specs=[vmem_spec()] * 5,
        out_specs=[vmem_spec()] * 2,
        compiler_params=params(12),
        name="project",
    )(trial_half, left, near, far, passed)


def direct(proj_own, proj_other, lines, own, boxes):
    rows, half = proj_own.shape
    points = rows // 4
    block = lines[0].shape[0] // 4
    count, states = 16 * block, lines[0].shape[1]
    chunk = 512

    def kernel(own_ref, other_ref, *refs):
        line_refs, scr_refs, (keep_ref, send_ref, proj, panel_ref) = refs[:5], refs[5:9], refs[9:]
        y, x = lax.axis_index("y"), lax.axis_index("x")
        for k in range(16):
            at = lax.rem(y + STEPS[k // 4] + 4, 4) * 4 + lax.rem(x + STEPS[k % 4] + 4, 4)
            ref, row = (line_refs[k // 4], k % 4) if k < 12 else (line_refs[k // 2 - 3], k % 2)
            panel_ref[pl.ds(pl.multiple_of(at * block, block), block), :] = ref[
                row * block : (row + 1) * block, :
            ]
        core = lax.axis_index("core")
        mine = pl.ds(pl.multiple_of(core * half, half), half)
        sibs = pl.ds(pl.multiple_of((1 - core) * half, half), half)
        for k in range(4):
            proj[k * points : (k + 1) * points, :] = other_ref[
                SIBLING[k] * points : (SIBLING[k] + 1) * points, :
            ]
        nt = (((1,), (1,)), ((), ()))
        for k in range(count // chunk):
            here = pl.ds(k * chunk, chunk)
            pair = lax.dot_general(own_ref[...], panel_ref[here, mine], nt, preferred_element_type=F32)
            pair += lax.dot_general(proj[...], panel_ref[here, sibs], nt, preferred_element_type=F32)
            weighted = jnp.concatenate(
                [
                    (
                        (scr_refs[0][:, here] if j == 0 else scr_refs[j][0, :, here].astype(F32))
                        * pair[j * points : (j + 1) * points]
                    ).astype(BF16)
                    for j in range(4)
                ],
                0,
            )
            send = jnp.dot(weighted, panel_ref[here, sibs], preferred_element_type=F32)
            keep = jnp.dot(weighted, panel_ref[here, mine], preferred_element_type=F32)
            if k == 0:
                send_ref[...] = send
                keep_ref[...] = keep
            else:
                send_ref[...] += send
                keep_ref[...] += keep

    return pl.pallas_call(
        kernel,
        out_shape=[jax.ShapeDtypeStruct((rows, half), F32)] * 2,
        in_specs=[vmem_spec()] * 11,
        out_specs=[vmem_spec()] * 2,
        scratch_shapes=[pltpu.VMEM((rows, half), BF16), pltpu.VMEM((count, states), BF16)],
        compiler_params=params(24),
        name="direct",
    )(proj_own, proj_other, *lines, own, *boxes)


def finish(psi, keep, got):
    states, count = psi.shape
    points = count // 4
    cols = keep.shape[1]

    def kernel(psi_ref, keep_ref, got_ref, out_ref, high, low):
        for k in range(4):
            here = slice(k * points, (k + 1) * points)
            there = slice(SIBLING[k] * points, (SIBLING[k] + 1) * points)
            back = keep_ref[here, :] + got_ref[there, :]
            top = back.astype(BF16)
            high[here, :] = top
            low[here, :] = (back - top.astype(F32)).astype(BF16)
        total = jnp.dot(psi_ref[...], high[...], preferred_element_type=F32)
        total += jnp.dot(psi_ref[...], low[...], preferred_element_type=F32)
        out_ref[...] = total.astype(BF16)

    return pl.pallas_call(
        kernel,
        out_shape=jax.ShapeDtypeStruct((states, cols), BF16),
        in_specs=[vmem_spec()] * 3,
        out_specs=vmem_spec(),
        scratch_shapes=[pltpu.VMEM((count, cols), BF16)] * 2,
        compiler_params=params(16),
        name="finish",
    )(psi, keep, got)


def ring(value, by):
    return lax.ppermute(value, ("zh", "zl"), [(k, (k + by) % 4) for k in range(4)])


def to_all(value):
    copies = jnp.broadcast_to(value[None], (lax.axis_size(PLANE), *value.shape))
    return copies


def shards(trial, psi_v, psi_c, screened):
    rows, states = trial.shape[1:]
    half = states // 2
    devices = lax.axis_size(ORDER)
    core = lax.axis_index("core")
    place = 2 * lax.axis_index("zh") + lax.axis_index("zl")
    left = psi_v.reshape(2, 4, 4, 2, 2, rows, -1).transpose(1, 2, 0, 4, 3, 5, 6).reshape(psi_v.shape)
    mine = lax.dynamic_slice_in_dim(trial[0], core * half, half, 1)
    got = swap(lax.dynamic_slice_in_dim(trial[0], (1 - core) * half, half, 1))
    pair = jnp.concatenate([jnp.where(core == 0, mine, got), jnp.where(core == 0, got, mine)], 0)
    steps = [pair, ring(pair, -1), ring(pair, 2), ring(pair, 1)]
    column = jnp.concatenate(
        [lax.select_n(place, *(steps[(to - at) % 4] for at in range(4))) for to in range(4)], 0
    )
    block = psi_c[:, 0, :].T
    line = jnp.concatenate([block, shift(block, "x", 1), shift(block, "x", -1), shift(block, "x", 2)], 0)
    own, near, far = pack(screened, left)
    copies, near, far, line = lax.optimization_barrier((to_all(column), near, far, line))
    trial_half = exchange(copies, PLANE).reshape(-1, half)
    near = swap(near)
    far = lax.ppermute(far, "zh", [(0, 1), (1, 0)])
    behind, ahead = shift(line, "y", 1), shift(line, "y", -1)
    far, behind, ahead = lax.optimization_barrier((far, behind, ahead))
    passed = swap(far[1:])
    middle = line.shape[0] // 2
    beyond = [shift(behind[:middle], "y", 1), shift(ahead[middle:], "y", -1)]
    proj_own, psi = project(trial_half, left, near, far, passed)
    proj_other = swap(proj_own)
    panel = [line, behind, ahead, *beyond]
    keep, send = direct(proj_own, proj_other, panel, own, [near, far, passed])
    got = swap(send)
    term = finish(psi, keep, got)
    parts = exchange(term.reshape(devices, rows, half), ORDER)
    parts = parts.reshape(-1, 2, rows, half).astype(F32)
    total = jnp.sum(parts, axis=0)
    return total.transpose(1, 0, 2).reshape(1, rows, states)


def solution(mesh):
    split = Mesh(
        mesh.devices.reshape(2, 4, 4, 2, mesh.shape["vec"]),
        TILE_VEC,
    )
    return jax.shard_map(
        shards,
        mesh=split,
        in_specs=(P(None, TILE_VEC, None), P(None, TILE), P(None, "zl", TILE), P(TILE, "zl")),
        out_specs=P(None, TILE_VEC, None),
        check_vma=False,
    )
```

```python
import jax
import jax.numpy as jnp
from jax import lax
from jax.experimental import pallas as pl
from jax.experimental.pallas import tpu as pltpu
from jax.sharding import Mesh
from jax.sharding import PartitionSpec as P

TILE_VEC = ("zh", "y", "x", "core", "zl")
TILE = ("zh", "y", "x", "core")
PLANE = ("y", "x")
ORDER = ("zh", "core", "zl", "y", "x")
STEPS = (0, -1, 1, -2)
F32 = jnp.float32
BF16 = jnp.bfloat16
SIBLING = (1, 0, 3, 2)


def shift(value, axis, by):
    n = lax.axis_size(axis)
    return lax.ppermute(value, axis, [(k, (k + by) % n) for k in range(n)])


def exchange(value, axes):
    return lax.all_to_all(value, axes, split_axis=0, concat_axis=0, tiled=True)


def swap(value):
    return lax.ppermute(value, "core", [(0, 1), (1, 0)])


def vmem_spec():
    return pl.BlockSpec(memory_space=pltpu.VMEM)


def params(mebibytes):
    return pltpu.CompilerParams(vmem_limit_bytes=mebibytes * 1024 * 1024)


def pack(screened, left):
    points, count = screened.shape
    plane, steps = count // 2, 4
    width = plane // 2
    rows = points // steps

    def kernel(in_ref, left_ref, own_ref, near_ref, far_ref):
        core, zh = lax.axis_index("core"), lax.axis_index("zh")
        low = lax.broadcasted_iota(jnp.int32, (rows, 128), 1) < 64
        first = core == 0
        for far in range(2):
            base = plane * (zh if far == 0 else 1 - zh)
            for m in range(width // 128):
                a = in_ref[:, pl.ds(pl.multiple_of(base + m * 256, 256), 128)]
                b = in_ref[:, pl.ds(pl.multiple_of(base + m * 256 + 128, 128), 128)]
                zero = jnp.where(low, a, pltpu.roll(b, 64, 1))
                one = jnp.where(low, pltpu.roll(a, 64, 1), b)
                here = pl.ds(m * 128, 128)
                mine, others = jnp.where(first, zero, one), jnp.where(first, one, zero)
                if far == 0:
                    own_ref[:, here] = mine
                    near_ref[0, :, here] = others.astype(BF16)
                else:
                    far_ref[0, :, here] = mine.astype(BF16)
                    far_ref[1, :, here] = others.astype(BF16)
        for g in range(left_ref.shape[0] // points):
            start = pl.multiple_of(g * points + pl.program_id(0) * rows, rows)
            piece = left_ref[pl.ds(start, rows), :]
            near_ref[1, :, pl.ds(g * points, points)] = piece
            far_ref[2, :, pl.ds(g * points, points)] = piece

    return pl.pallas_call(
        kernel,
        grid=(steps,),
        out_shape=[
            jax.ShapeDtypeStruct((points, width), F32),
            jax.ShapeDtypeStruct((2, points, width), BF16),
            jax.ShapeDtypeStruct((3, points, width), BF16),
        ],
        in_specs=[
            pl.BlockSpec((rows, count), lambda k: (k, 0)),
            pl.BlockSpec(left.shape, lambda k: (0, 0)),
        ],
        out_specs=[
            pl.BlockSpec((rows, width), lambda k: (k, 0)),
            pl.BlockSpec((2, rows, width), lambda k: (0, k, 0)),
            pl.BlockSpec((3, rows, width), lambda k: (0, k, 0)),
        ],
        compiler_params=params(8),
        name="pack",
    )(screened, left)


def project(rounds, left, near, far, passed):
    states, points = left.shape
    block = rounds[0].shape[0] // 2
    cols = rounds[0].shape[1]

    def kernel(*refs):
        trial_refs, left_ref, boxes, (out_ref, psi_ref, trial) = refs[:4], refs[4], refs[5:8], refs[8:]
        core = lax.axis_index("core")
        place = 2 * lax.axis_index("zh") + lax.axis_index("zl")
        for k in range(4):
            source = lax.rem(place + STEPS[k] + 4, 4)
            for m in range(2):
                owner = core if m == 0 else 1 - core
                group = lax.div(source, 2) * 4 + owner * 2 + lax.rem(source, 2)
                trial[pl.ds(pl.multiple_of(group * block, block), block), :] = trial_refs[k][
                    m * block : (m + 1) * block, :
                ]
        psi_ref[:, :points] = left_ref[...]
        for k in range(1, 4):
            box = boxes[k - 1]
            for g in range(states // points):
                psi_ref[g * points : (g + 1) * points, k * points : (k + 1) * points] = box[
                    box.shape[0] - 1, :, g * points : (g + 1) * points
                ]
        out_ref[...] = lax.dot_general(
            psi_ref[...], trial[...], (((0,), (0,)), ((), ())), preferred_element_type=F32
        ).astype(BF16)

    return pl.pallas_call(
        kernel,
        out_shape=[
            jax.ShapeDtypeStruct((4 * points, cols), BF16),
            jax.ShapeDtypeStruct((states, 4 * points), BF16),
        ],
        in_specs=[vmem_spec()] * 8,
        out_specs=[vmem_spec()] * 2,
        scratch_shapes=[pltpu.VMEM((states, cols), BF16)],
        compiler_params=params(12),
        name="project",
    )(*rounds, left, near, far, passed)


def direct(proj_own, proj_other, lines, own, boxes):
    rows, half = proj_own.shape
    points = rows // 4
    block = lines[0].shape[0] // 4
    count, states = 16 * block, lines[0].shape[1]
    chunk = 512

    def kernel(own_ref, other_ref, *refs):
        line_refs, scr_refs, (keep_ref, send_ref, proj, panel_ref) = refs[:5], refs[5:9], refs[9:]
        y, x = lax.axis_index("y"), lax.axis_index("x")
        for k in range(16):
            at = lax.rem(y + STEPS[k // 4] + 4, 4) * 4 + lax.rem(x + STEPS[k % 4] + 4, 4)
            ref, row = (line_refs[k // 4], k % 4) if k < 12 else (line_refs[k // 2 - 3], k % 2)
            panel_ref[pl.ds(pl.multiple_of(at * block, block), block), :] = ref[
                row * block : (row + 1) * block, :
            ]
        core = lax.axis_index("core")
        mine = pl.ds(pl.multiple_of(core * half, half), half)
        sibs = pl.ds(pl.multiple_of((1 - core) * half, half), half)
        for k in range(4):
            proj[k * points : (k + 1) * points, :] = other_ref[
                SIBLING[k] * points : (SIBLING[k] + 1) * points, :
            ]
        nt = (((1,), (1,)), ((), ()))
        for k in range(count // chunk):
            here = pl.ds(k * chunk, chunk)
            pair = lax.dot_general(own_ref[...], panel_ref[here, mine], nt, preferred_element_type=F32)
            pair += lax.dot_general(proj[...], panel_ref[here, sibs], nt, preferred_element_type=F32)
            weighted = jnp.concatenate(
                [
                    (
                        (scr_refs[0][:, here] if j == 0 else scr_refs[j][0, :, here].astype(F32))
                        * pair[j * points : (j + 1) * points]
                    ).astype(BF16)
                    for j in range(4)
                ],
                0,
            )
            send = jnp.dot(weighted, panel_ref[here, sibs], preferred_element_type=F32)
            keep = jnp.dot(weighted, panel_ref[here, mine], preferred_element_type=F32)
            if k == 0:
                send_ref[...] = send
                keep_ref[...] = keep
            else:
                send_ref[...] += send
                keep_ref[...] += keep

    return pl.pallas_call(
        kernel,
        out_shape=[jax.ShapeDtypeStruct((rows, half), F32)] * 2,
        in_specs=[vmem_spec()] * 11,
        out_specs=[vmem_spec()] * 2,
        scratch_shapes=[pltpu.VMEM((rows, half), BF16), pltpu.VMEM((count, states), BF16)],
        compiler_params=params(24),
        name="direct",
    )(proj_own, proj_other, *lines, own, *boxes)


def finish(psi, keep, got):
    states, count = psi.shape
    points = count // 4
    cols = keep.shape[1]

    def kernel(psi_ref, keep_ref, got_ref, out_ref, high, low):
        for k in range(4):
            here = slice(k * points, (k + 1) * points)
            there = slice(SIBLING[k] * points, (SIBLING[k] + 1) * points)
            back = keep_ref[here, :] + got_ref[there, :]
            top = back.astype(BF16)
            high[here, :] = top
            low[here, :] = (back - top.astype(F32)).astype(BF16)
        total = jnp.dot(psi_ref[...], high[...], preferred_element_type=F32)
        total += jnp.dot(psi_ref[...], low[...], preferred_element_type=F32)
        out_ref[...] = total.astype(BF16)

    return pl.pallas_call(
        kernel,
        out_shape=jax.ShapeDtypeStruct((states, cols), BF16),
        in_specs=[vmem_spec()] * 3,
        out_specs=vmem_spec(),
        scratch_shapes=[pltpu.VMEM((count, cols), BF16)] * 2,
        compiler_params=params(16),
        name="finish",
    )(psi, keep, got)


def ring(value, by):
    return lax.ppermute(value, ("zh", "zl"), [(k, (k + by) % 4) for k in range(4)])


def to_all(value):
    copies = jnp.broadcast_to(value[None], (lax.axis_size(PLANE), *value.shape))
    return copies


def shards(trial, psi_v, psi_c, screened):
    rows, states = trial.shape[1:]
    half = states // 2
    devices = lax.axis_size(ORDER)
    core = lax.axis_index("core")
    left = psi_v.reshape(2, 4, 4, 2, 2, rows, -1).transpose(0, 3, 4, 1, 2, 5, 6).reshape(psi_v.shape)
    own, near, far = pack(screened, left)
    block = psi_c[:, 0, :].T
    line = jnp.concatenate([block, shift(block, "x", 1), shift(block, "x", -1), shift(block, "x", 2)], 0)
    copies, near, far = lax.optimization_barrier((to_all(trial[0]), near, far))
    level = exchange(copies, PLANE).reshape(-1, states)
    near = swap(near)
    far = lax.ppermute(far, "zh", [(0, 1), (1, 0)])
    behind, ahead = shift(line, "y", 1), shift(line, "y", -1)
    mine = lax.dynamic_slice_in_dim(level, core * half, half, 1)
    sent = lax.dynamic_slice_in_dim(level, (1 - core) * half, half, 1)
    pieces = jnp.concatenate([mine, swap(sent)], 0)
    pieces, near = lax.optimization_barrier((pieces, near))
    rounds = [pieces, ring(pieces, 1), ring(pieces, -1), ring(pieces, 2)]
    far, _ = lax.optimization_barrier((far, pieces))
    passed = swap(far[1:])
    middle = line.shape[0] // 2
    behind, ahead, passed = lax.optimization_barrier((behind, ahead, passed))
    beyond = [shift(behind[:middle], "y", 1), shift(ahead[middle:], "y", -1)]
    rounds, beyond = lax.optimization_barrier((rounds, beyond))
    proj_own, psi = project(rounds, left, near, far, passed)
    proj_other = swap(proj_own)
    panel = [line, behind, ahead, *beyond]
    keep, send = direct(proj_own, proj_other, panel, own, [near, far, passed])
    got = swap(send)
    term = finish(psi, keep, got)
    parts = exchange(term.reshape(devices, rows, half), ORDER)
    parts = parts.reshape(2, 2, 2, -1, rows, half).astype(F32)
    total = jnp.sum(parts, axis=(0, 2, 3))
    return total.transpose(1, 0, 2).reshape(1, rows, states)


def solution(mesh):
    split = Mesh(
        mesh.devices.reshape(2, 4, 4, 2, mesh.shape["vec"]),
        TILE_VEC,
    )
    return jax.shard_map(
        shards,
        mesh=split,
        in_specs=(P(None, TILE_VEC, None), P(None, TILE), P(None, "zl", TILE), P(TILE, "zl")),
        out_specs=P(None, TILE_VEC, None),
        check_vma=False,
    )
```

```python
import jax
import jax.numpy as jnp
from jax import lax
from jax.experimental import pallas as pl
from jax.experimental.pallas import tpu as pltpu
from jax.sharding import Mesh
from jax.sharding import PartitionSpec as P

TILE_VEC = ("zh", "y", "x", "core", "zl")
TILE = ("zh", "y", "x", "core")
PLANE = ("y", "x")
ORDER = ("zh", "core", "zl", "y", "x")
STEPS = (0, -1, 1, -2)
F32 = jnp.float32
BF16 = jnp.bfloat16
SIBLING = (1, 0, 3, 2)


def shift(value, axis, by):
    n = lax.axis_size(axis)
    return lax.ppermute(value, axis, [(k, (k + by) % n) for k in range(n)])


def exchange(value, axes):
    return lax.all_to_all(value, axes, split_axis=0, concat_axis=0, tiled=True)


def swap(value):
    return lax.ppermute(value, "core", [(0, 1), (1, 0)])


def vmem_spec():
    return pl.BlockSpec(memory_space=pltpu.VMEM)


def params(mebibytes):
    return pltpu.CompilerParams(vmem_limit_bytes=mebibytes * 1024 * 1024)


def pack(screened, left):
    points, count = screened.shape
    plane, steps = count // 2, 4
    width = plane // 2
    rows = points // steps

    def kernel(in_ref, left_ref, own_ref, near_ref, far_ref):
        core, zh = lax.axis_index("core"), lax.axis_index("zh")
        low = lax.broadcasted_iota(jnp.int32, (rows, 128), 1) < 64
        first = core == 0
        for far in range(2):
            base = plane * (zh if far == 0 else 1 - zh)
            for m in range(width // 128):
                a = in_ref[:, pl.ds(pl.multiple_of(base + m * 256, 256), 128)]
                b = in_ref[:, pl.ds(pl.multiple_of(base + m * 256 + 128, 128), 128)]
                zero = jnp.where(low, a, pltpu.roll(b, 64, 1))
                one = jnp.where(low, pltpu.roll(a, 64, 1), b)
                here = pl.ds(m * 128, 128)
                mine, others = jnp.where(first, zero, one), jnp.where(first, one, zero)
                if far == 0:
                    own_ref[:, here] = mine
                    near_ref[0, :, here] = others.astype(BF16)
                else:
                    far_ref[0, :, here] = mine.astype(BF16)
                    far_ref[1, :, here] = others.astype(BF16)
        for g in range(left_ref.shape[0] // points):
            start = pl.multiple_of(g * points + pl.program_id(0) * rows, rows)
            piece = left_ref[pl.ds(start, rows), :]
            near_ref[1, :, pl.ds(g * points, points)] = piece
            far_ref[2, :, pl.ds(g * points, points)] = piece

    return pl.pallas_call(
        kernel,
        grid=(steps,),
        out_shape=[
            jax.ShapeDtypeStruct((points, width), F32),
            jax.ShapeDtypeStruct((2, points, width), BF16),
            jax.ShapeDtypeStruct((3, points, width), BF16),
        ],
        in_specs=[
            pl.BlockSpec((rows, count), lambda k: (k, 0)),
            pl.BlockSpec(left.shape, lambda k: (0, 0)),
        ],
        out_specs=[
            pl.BlockSpec((rows, width), lambda k: (k, 0)),
            pl.BlockSpec((2, rows, width), lambda k: (0, k, 0)),
            pl.BlockSpec((3, rows, width), lambda k: (0, k, 0)),
        ],
        compiler_params=params(8),
        name="pack",
    )(screened, left)


def project(rounds, left, near, far, passed):
    states, points = left.shape
    block = rounds[0].shape[0] // 2
    cols = rounds[0].shape[1]

    def kernel(*refs):
        trial_refs, left_ref, boxes, (out_ref, psi_ref, trial) = refs[:4], refs[4], refs[5:8], refs[8:]
        core = lax.axis_index("core")
        place = 2 * lax.axis_index("zh") + lax.axis_index("zl")
        for k in range(4):
            source = lax.rem(place + STEPS[k] + 4, 4)
            for m in range(2):
                owner = core if m == 0 else 1 - core
                group = lax.div(source, 2) * 4 + owner * 2 + lax.rem(source, 2)
                trial[pl.ds(pl.multiple_of(group * block, block), block), :] = trial_refs[k][
                    m * block : (m + 1) * block, :
                ]
        psi_ref[:, :points] = left_ref[...]
        for k in range(1, 4):
            box = boxes[k - 1]
            for g in range(states // points):
                psi_ref[g * points : (g + 1) * points, k * points : (k + 1) * points] = box[
                    box.shape[0] - 1, :, g * points : (g + 1) * points
                ]
        out_ref[...] = lax.dot_general(
            psi_ref[...], trial[...], (((0,), (0,)), ((), ())), preferred_element_type=F32
        ).astype(BF16)

    return pl.pallas_call(
        kernel,
        out_shape=[
            jax.ShapeDtypeStruct((4 * points, cols), BF16),
            jax.ShapeDtypeStruct((states, 4 * points), BF16),
        ],
        in_specs=[vmem_spec()] * 8,
        out_specs=[vmem_spec()] * 2,
        scratch_shapes=[pltpu.VMEM((states, cols), BF16)],
        compiler_params=params(12),
        name="project",
    )(*rounds, left, near, far, passed)


def direct(proj_own, proj_other, lines, own, boxes):
    rows, half = proj_own.shape
    points = rows // 4
    block = lines[0].shape[0] // 4
    count, states = 16 * block, lines[0].shape[1]
    chunk = 512

    def kernel(own_ref, other_ref, *refs):
        line_refs, scr_refs, (keep_ref, send_ref, proj, panel_ref) = refs[:5], refs[5:9], refs[9:]
        y, x = lax.axis_index("y"), lax.axis_index("x")
        for k in range(16):
            at = lax.rem(y + STEPS[k // 4] + 4, 4) * 4 + lax.rem(x + STEPS[k % 4] + 4, 4)
            ref, row = (line_refs[k // 4], k % 4) if k < 12 else (line_refs[k // 2 - 3], k % 2)
            panel_ref[pl.ds(pl.multiple_of(at * block, block), block), :] = ref[
                row * block : (row + 1) * block, :
            ]
        core = lax.axis_index("core")
        mine = pl.ds(pl.multiple_of(core * half, half), half)
        sibs = pl.ds(pl.multiple_of((1 - core) * half, half), half)
        for k in range(4):
            proj[k * points : (k + 1) * points, :] = other_ref[
                SIBLING[k] * points : (SIBLING[k] + 1) * points, :
            ]
        nt = (((1,), (1,)), ((), ()))
        for k in range(count // chunk):
            here = pl.ds(k * chunk, chunk)
            pair = lax.dot_general(own_ref[...], panel_ref[here, mine], nt, preferred_element_type=F32)
            pair += lax.dot_general(proj[...], panel_ref[here, sibs], nt, preferred_element_type=F32)
            weighted = jnp.concatenate(
                [
                    (
                        (scr_refs[0][:, here] if j == 0 else scr_refs[j][0, :, here].astype(F32))
                        * pair[j * points : (j + 1) * points]
                    ).astype(BF16)
                    for j in range(4)
                ],
                0,
            )
            send = jnp.dot(weighted, panel_ref[here, sibs], preferred_element_type=F32)
            keep = jnp.dot(weighted, panel_ref[here, mine], preferred_element_type=F32)
            if k == 0:
                send_ref[...] = send
                keep_ref[...] = keep
            else:
                send_ref[...] += send
                keep_ref[...] += keep

    return pl.pallas_call(
        kernel,
        out_shape=[jax.ShapeDtypeStruct((rows, half), F32)] * 2,
        in_specs=[vmem_spec()] * 11,
        out_specs=[vmem_spec()] * 2,
        scratch_shapes=[pltpu.VMEM((rows, half), BF16), pltpu.VMEM((count, states), BF16)],
        compiler_params=params(24),
        name="direct",
    )(proj_own, proj_other, *lines, own, *boxes)


def finish(psi, keep, got):
    states, count = psi.shape
    points = count // 4
    cols = keep.shape[1]

    def kernel(psi_ref, keep_ref, got_ref, out_ref, high, low):
        for k in range(4):
            here = slice(k * points, (k + 1) * points)
            there = slice(SIBLING[k] * points, (SIBLING[k] + 1) * points)
            back = keep_ref[here, :] + got_ref[there, :]
            top = back.astype(BF16)
            high[here, :] = top
            low[here, :] = (back - top.astype(F32)).astype(BF16)
        total = jnp.dot(psi_ref[...], high[...], preferred_element_type=F32)
        total += jnp.dot(psi_ref[...], low[...], preferred_element_type=F32)
        out_ref[...] = total.astype(BF16)

    return pl.pallas_call(
        kernel,
        out_shape=jax.ShapeDtypeStruct((states, cols), BF16),
        in_specs=[vmem_spec()] * 3,
        out_specs=vmem_spec(),
        scratch_shapes=[pltpu.VMEM((count, cols), BF16)] * 2,
        compiler_params=params(16),
        name="finish",
    )(psi, keep, got)


def ring(value, by):
    return lax.ppermute(value, ("zh", "zl"), [(k, (k + by) % 4) for k in range(4)])


def to_all(value):
    copies = jnp.broadcast_to(value[None], (lax.axis_size(PLANE), *value.shape))
    return copies


def shards(trial, psi_v, psi_c, screened):
    rows, states = trial.shape[1:]
    half = states // 2
    devices = lax.axis_size(ORDER)
    core = lax.axis_index("core")
    left = psi_v.reshape(2, 4, 4, 2, 2, rows, -1).transpose(0, 3, 4, 1, 2, 5, 6).reshape(psi_v.shape)
    own, near, far = pack(screened, left)
    block = psi_c[:, 0, :].T
    line = jnp.concatenate([block, shift(block, "x", 1), shift(block, "x", -1), shift(block, "x", 2)], 0)
    copies, near, far, line = lax.optimization_barrier((to_all(trial[0]), near, far, line))
    level = exchange(copies, PLANE).reshape(-1, states)
    near = swap(near)
    far = lax.ppermute(far, "zh", [(0, 1), (1, 0)])
    behind, ahead = shift(line, "y", 1), shift(line, "y", -1)
    mine = lax.dynamic_slice_in_dim(level, core * half, half, 1)
    sent = lax.dynamic_slice_in_dim(level, (1 - core) * half, half, 1)
    pieces = jnp.concatenate([mine, swap(sent)], 0)
    pieces, near = lax.optimization_barrier((pieces, near))
    rounds = [pieces, ring(pieces, 1), ring(pieces, -1), ring(pieces, 2)]
    far, _ = lax.optimization_barrier((far, pieces))
    passed = swap(far[1:])
    middle = line.shape[0] // 2
    behind, ahead, passed = lax.optimization_barrier((behind, ahead, passed))
    beyond = [shift(behind[:middle], "y", 1), shift(ahead[middle:], "y", -1)]
    rounds, beyond = lax.optimization_barrier((rounds, beyond))
    proj_own, psi = project(rounds, left, near, far, passed)
    proj_other = swap(proj_own)
    panel = [line, behind, ahead, *beyond]
    keep, send = direct(proj_own, proj_other, panel, own, [near, far, passed])
    got = swap(send)
    term = finish(psi, keep, got)
    parts = exchange(term.reshape(devices, rows, half), ORDER)
    parts = parts.reshape(2, 2, 2, -1, rows, half).astype(F32)
    total = jnp.sum(parts, axis=(0, 2, 3))
    return total.transpose(1, 0, 2).reshape(1, rows, states)


def solution(mesh):
    split = Mesh(
        mesh.devices.reshape(2, 4, 4, 2, mesh.shape["vec"]),
        TILE_VEC,
    )
    return jax.shard_map(
        shards,
        mesh=split,
        in_specs=(P(None, TILE_VEC, None), P(None, TILE), P(None, "zl", TILE), P(TILE, "zl")),
        out_specs=P(None, TILE_VEC, None),
        check_vma=False,
    )
```

```python
import jax
import jax.numpy as jnp
from jax import lax
from jax.experimental import pallas as pl
from jax.experimental.pallas import tpu as pltpu
from jax.sharding import Mesh
from jax.sharding import PartitionSpec as P

TILE_VEC = ("zh", "y", "x", "core", "zl")
TILE = ("zh", "y", "x", "core")
STEPS = (0, -1, 1, -2)
F32 = jnp.float32
BF16 = jnp.bfloat16
SIBLING = (1, 0, 3, 2)


def shift(value, axis, by):
    n = lax.axis_size(axis)
    return lax.ppermute(value, axis, [(k, (k + by) % n) for k in range(n)])


def exchange(value, axes):
    return lax.all_to_all(value, axes, split_axis=0, concat_axis=0, tiled=True)


def swap(value):
    return lax.ppermute(value, "core", [(0, 1), (1, 0)])


def vmem_spec():
    return pl.BlockSpec(memory_space=pltpu.VMEM)


def params(mebibytes):
    return pltpu.CompilerParams(vmem_limit_bytes=mebibytes * 1024 * 1024)


def pack(screened, left):
    points, count = screened.shape
    plane, steps = count // 2, 4
    width = plane // 2
    rows = points // steps

    def kernel(in_ref, left_ref, own_ref, near_ref, far_ref):
        core, zh = lax.axis_index("core"), lax.axis_index("zh")
        low = lax.broadcasted_iota(jnp.int32, (rows, 128), 1) < 64
        first = core == 0
        for far in range(2):
            base = plane * (zh if far == 0 else 1 - zh)
            for m in range(width // 128):
                a = in_ref[:, pl.ds(pl.multiple_of(base + m * 256, 256), 128)]
                b = in_ref[:, pl.ds(pl.multiple_of(base + m * 256 + 128, 128), 128)]
                zero = jnp.where(low, a, pltpu.roll(b, 64, 1))
                one = jnp.where(low, pltpu.roll(a, 64, 1), b)
                here = pl.ds(m * 128, 128)
                mine, others = jnp.where(first, zero, one), jnp.where(first, one, zero)
                if far == 0:
                    own_ref[:, here] = mine
                    near_ref[0, :, here] = others.astype(BF16)
                else:
                    far_ref[0, :, here] = mine.astype(BF16)
                    far_ref[1, :, here] = others.astype(BF16)
        for g in range(left_ref.shape[0] // points):
            start = pl.multiple_of(g * points + pl.program_id(0) * rows, rows)
            piece = left_ref[pl.ds(start, rows), :]
            near_ref[1, :, pl.ds(g * points, points)] = piece
            far_ref[2, :, pl.ds(g * points, points)] = piece

    return pl.pallas_call(
        kernel,
        grid=(steps,),
        out_shape=[
            jax.ShapeDtypeStruct((points, width), F32),
            jax.ShapeDtypeStruct((2, points, width), BF16),
            jax.ShapeDtypeStruct((3, points, width), BF16),
        ],
        in_specs=[
            pl.BlockSpec((rows, count), lambda k: (k, 0)),
            pl.BlockSpec(left.shape, lambda k: (0, 0)),
        ],
        out_specs=[
            pl.BlockSpec((rows, width), lambda k: (k, 0)),
            pl.BlockSpec((2, rows, width), lambda k: (0, k, 0)),
            pl.BlockSpec((3, rows, width), lambda k: (0, k, 0)),
        ],
        compiler_params=params(8),
        name="pack",
    )(screened, left)


def project(trial_half, left, near, far, passed):
    states, points = left.shape
    cols = trial_half.shape[1]

    def kernel(trial_ref, left_ref, *refs):
        boxes, (out_ref, psi_ref) = refs[:3], refs[3:]
        psi_ref[:, :points] = left_ref[...]
        for k in range(1, 4):
            box = boxes[k - 1]
            for g in range(states // points):
                psi_ref[g * points : (g + 1) * points, k * points : (k + 1) * points] = box[
                    box.shape[0] - 1, :, g * points : (g + 1) * points
                ]
        out_ref[...] = lax.dot_general(
            psi_ref[...], trial_ref[...], (((0,), (0,)), ((), ())), preferred_element_type=F32
        ).astype(BF16)

    return pl.pallas_call(
        kernel,
        out_shape=[
            jax.ShapeDtypeStruct((4 * points, cols), BF16),
            jax.ShapeDtypeStruct((states, 4 * points), BF16),
        ],
        in_specs=[vmem_spec()] * 5,
        out_specs=[vmem_spec()] * 2,
        compiler_params=params(12),
        name="project",
    )(trial_half, left, near, far, passed)


def direct(proj_own, proj_other, lines, own, boxes):
    rows, half = proj_own.shape
    points = rows // 4
    block = lines[0].shape[0] // 4
    count, states = 16 * block, lines[0].shape[1]
    chunk = 512

    def kernel(own_ref, other_ref, *refs):
        line_refs, scr_refs, (keep_ref, send_ref, proj, panel_ref) = refs[:5], refs[5:9], refs[9:]
        y, x = lax.axis_index("y"), lax.axis_index("x")
        for k in range(16):
            at = lax.rem(y + STEPS[k // 4] + 4, 4) * 4 + lax.rem(x + STEPS[k % 4] + 4, 4)
            ref, row = (line_refs[k // 4], k % 4) if k < 12 else (line_refs[k // 2 - 3], k % 2)
            panel_ref[pl.ds(pl.multiple_of(at * block, block), block), :] = ref[
                row * block : (row + 1) * block, :
            ]
        core = lax.axis_index("core")
        mine = pl.ds(pl.multiple_of(core * half, half), half)
        sibs = pl.ds(pl.multiple_of((1 - core) * half, half), half)
        for k in range(4):
            proj[k * points : (k + 1) * points, :] = other_ref[
                SIBLING[k] * points : (SIBLING[k] + 1) * points, :
            ]
        nt = (((1,), (1,)), ((), ()))
        for k in range(count // chunk):
            here = pl.ds(k * chunk, chunk)
            pair = lax.dot_general(own_ref[...], panel_ref[here, mine], nt, preferred_element_type=F32)
            pair += lax.dot_general(proj[...], panel_ref[here, sibs], nt, preferred_element_type=F32)
            weighted = jnp.concatenate(
                [
                    (
                        (scr_refs[0][:, here] if j == 0 else scr_refs[j][0, :, here].astype(F32))
                        * pair[j * points : (j + 1) * points]
                    ).astype(BF16)
                    for j in range(4)
                ],
                0,
            )
            send = jnp.dot(weighted, panel_ref[here, sibs], preferred_element_type=F32)
            keep = jnp.dot(weighted, panel_ref[here, mine], preferred_element_type=F32)
            if k == 0:
                send_ref[...] = send
                keep_ref[...] = keep
            else:
                send_ref[...] += send
                keep_ref[...] += keep

    return pl.pallas_call(
        kernel,
        out_shape=[jax.ShapeDtypeStruct((rows, half), F32)] * 2,
        in_specs=[vmem_spec()] * 11,
        out_specs=[vmem_spec()] * 2,
        scratch_shapes=[pltpu.VMEM((rows, half), BF16), pltpu.VMEM((count, states), BF16)],
        compiler_params=params(24),
        name="direct",
    )(proj_own, proj_other, *lines, own, *boxes)


def finish(psi, keep, got):
    states, count = psi.shape
    points = count // 4
    cols = keep.shape[1]

    def kernel(psi_ref, keep_ref, got_ref, out_ref, high, low):
        for k in range(4):
            here = slice(k * points, (k + 1) * points)
            there = slice(SIBLING[k] * points, (SIBLING[k] + 1) * points)
            back = keep_ref[here, :] + got_ref[there, :]
            top = back.astype(BF16)
            high[here, :] = top
            low[here, :] = (back - top.astype(F32)).astype(BF16)
        total = jnp.dot(psi_ref[...], high[...], preferred_element_type=F32)
        total += jnp.dot(psi_ref[...], low[...], preferred_element_type=F32)
        out_ref[...] = total.astype(BF16)

    return pl.pallas_call(
        kernel,
        out_shape=jax.ShapeDtypeStruct((states, cols), BF16),
        in_specs=[vmem_spec()] * 3,
        out_specs=vmem_spec(),
        scratch_shapes=[pltpu.VMEM((count, cols), BF16)] * 2,
        compiler_params=params(16),
        name="finish",
    )(psi, keep, got)


def shards(trial, psi_v, psi_c, screened):
    rows, states = trial.shape[1:]
    half = states // 2
    devices = lax.axis_size(TILE_VEC)
    own, near, far = pack(screened, psi_v)
    block = psi_c[:, 0, :].T
    line = jnp.concatenate([block, shift(block, "x", 1), shift(block, "x", -1), shift(block, "x", 2)], 0)
    halves = trial[0].reshape(rows, 2, half).transpose(1, 0, 2)
    copies = jnp.broadcast_to(halves[None, :, None], (devices // 4, 2, 2, rows, half))
    copies, near, far, line = lax.optimization_barrier((copies, near, far, line))
    trial_half = exchange(copies.reshape(devices, rows, half), TILE_VEC).reshape(-1, half)
    near = swap(near)
    far = lax.ppermute(far, "zh", [(0, 1), (1, 0)])
    behind, ahead = shift(line, "y", 1), shift(line, "y", -1)
    far, behind, ahead = lax.optimization_barrier((far, behind, ahead))
    passed = swap(far[1:])
    middle = line.shape[0] // 2
    beyond = [shift(behind[:middle], "y", 1), shift(ahead[middle:], "y", -1)]
    passed, beyond = lax.optimization_barrier((passed, beyond))
    proj_own, psi = project(trial_half, psi_v, near, far, passed)
    proj_other = swap(proj_own)
    panel = [line, behind, ahead, *beyond]
    keep, send = direct(proj_own, proj_other, panel, own, [near, far, passed])
    got = swap(send)
    term = finish(psi, keep, got)
    parts = exchange(term.reshape(devices, rows, half), TILE_VEC)
    parts = parts.reshape(-1, 2, 2, rows, half).astype(F32)
    total = jnp.sum(parts, axis=(0, 2))
    return total.transpose(1, 0, 2).reshape(1, rows, states)


def solution(mesh):
    split = Mesh(
        mesh.devices.reshape(2, 4, 4, 2, mesh.shape["vec"]),
        TILE_VEC,
    )
    return jax.shard_map(
        shards,
        mesh=split,
        in_specs=(P(None, TILE_VEC, None), P(None, TILE), P(None, "zl", TILE), P(TILE, "zl")),
        out_specs=P(None, TILE_VEC, None),
        check_vma=False,
    )
```

```python
import jax
import jax.numpy as jnp
from jax import lax
from jax.experimental import pallas as pl
from jax.experimental.pallas import tpu as pltpu
from jax.sharding import Mesh
from jax.sharding import PartitionSpec as P

TILE_VEC = ("zh", "y", "x", "core", "zl")
TILE = ("zh", "y", "x", "core")
STEPS = (0, -1, 1, -2)
F32 = jnp.float32
BF16 = jnp.bfloat16
SIBLING = (1, 0, 3, 2)


def shift(value, axis, by):
    n = lax.axis_size(axis)
    return lax.ppermute(value, axis, [(k, (k + by) % n) for k in range(n)])


def exchange(value, axes):
    return lax.all_to_all(value, axes, split_axis=0, concat_axis=0, tiled=True)


def swap(value):
    return lax.ppermute(value, "core", [(0, 1), (1, 0)])


def vmem_spec():
    return pl.BlockSpec(memory_space=pltpu.VMEM)


def params(mebibytes):
    return pltpu.CompilerParams(vmem_limit_bytes=mebibytes * 1024 * 1024)


def pack(screened, left):
    points, count = screened.shape
    plane, steps = count // 2, 4
    width = plane // 2
    rows = points // steps

    def kernel(in_ref, left_ref, own_ref, near_ref, far_ref):
        core, zh = lax.axis_index("core"), lax.axis_index("zh")
        low = lax.broadcasted_iota(jnp.int32, (rows, 128), 1) < 64
        first = core == 0
        for far in range(2):
            base = plane * (zh if far == 0 else 1 - zh)
            for m in range(width // 128):
                a = in_ref[:, pl.ds(pl.multiple_of(base + m * 256, 256), 128)]
                b = in_ref[:, pl.ds(pl.multiple_of(base + m * 256 + 128, 128), 128)]
                zero = jnp.where(low, a, pltpu.roll(b, 64, 1))
                one = jnp.where(low, pltpu.roll(a, 64, 1), b)
                here = pl.ds(m * 128, 128)
                mine, others = jnp.where(first, zero, one), jnp.where(first, one, zero)
                if far == 0:
                    own_ref[:, here] = mine
                    near_ref[0, :, here] = others.astype(BF16)
                else:
                    far_ref[0, :, here] = mine.astype(BF16)
                    far_ref[1, :, here] = others.astype(BF16)
        for g in range(left_ref.shape[0] // points):
            start = pl.multiple_of(g * points + pl.program_id(0) * rows, rows)
            piece = left_ref[pl.ds(start, rows), :]
            near_ref[1, :, pl.ds(g * points, points)] = piece
            far_ref[2, :, pl.ds(g * points, points)] = piece

    return pl.pallas_call(
        kernel,
        grid=(steps,),
        out_shape=[
            jax.ShapeDtypeStruct((points, width), F32),
            jax.ShapeDtypeStruct((2, points, width), BF16),
            jax.ShapeDtypeStruct((3, points, width), BF16),
        ],
        in_specs=[
            pl.BlockSpec((rows, count), lambda k: (k, 0)),
            pl.BlockSpec(left.shape, lambda k: (0, 0)),
        ],
        out_specs=[
            pl.BlockSpec((rows, width), lambda k: (k, 0)),
            pl.BlockSpec((2, rows, width), lambda k: (0, k, 0)),
            pl.BlockSpec((3, rows, width), lambda k: (0, k, 0)),
        ],
        compiler_params=params(8),
        name="pack",
    )(screened, left)


def project(trial_half, left, near, far, passed):
    states, points = left.shape
    cols = trial_half.shape[1]

    def kernel(trial_ref, left_ref, *refs):
        boxes, (out_ref, psi_ref) = refs[:3], refs[3:]
        psi_ref[:, :points] = left_ref[...]
        for k in range(1, 4):
            box = boxes[k - 1]
            for g in range(states // points):
                psi_ref[g * points : (g + 1) * points, k * points : (k + 1) * points] = box[
                    box.shape[0] - 1, :, g * points : (g + 1) * points
                ]
        out_ref[...] = lax.dot_general(
            psi_ref[...], trial_ref[...], (((0,), (0,)), ((), ())), preferred_element_type=F32
        ).astype(BF16)

    return pl.pallas_call(
        kernel,
        out_shape=[
            jax.ShapeDtypeStruct((4 * points, cols), BF16),
            jax.ShapeDtypeStruct((states, 4 * points), BF16),
        ],
        in_specs=[vmem_spec()] * 5,
        out_specs=[vmem_spec()] * 2,
        compiler_params=params(12),
        name="project",
    )(trial_half, left, near, far, passed)


def direct(proj_own, proj_other, lines, own, boxes):
    rows, half = proj_own.shape
    points = rows // 4
    block = lines[0].shape[0] // 4
    count, states = 16 * block, lines[0].shape[1]
    chunk = 512

    def kernel(own_ref, other_ref, *refs):
        line_refs, scr_refs, (keep_ref, send_ref, proj, panel_ref) = refs[:5], refs[5:9], refs[9:]
        y, x = lax.axis_index("y"), lax.axis_index("x")
        for k in range(16):
            at = lax.rem(y + STEPS[k // 4] + 4, 4) * 4 + lax.rem(x + STEPS[k % 4] + 4, 4)
            ref, row = (line_refs[k // 4], k % 4) if k < 12 else (line_refs[k // 2 - 3], k % 2)
            panel_ref[pl.ds(pl.multiple_of(at * block, block), block), :] = ref[
                row * block : (row + 1) * block, :
            ]
        core = lax.axis_index("core")
        mine = pl.ds(pl.multiple_of(core * half, half), half)
        sibs = pl.ds(pl.multiple_of((1 - core) * half, half), half)
        for k in range(4):
            proj[k * points : (k + 1) * points, :] = other_ref[
                SIBLING[k] * points : (SIBLING[k] + 1) * points, :
            ]
        nt = (((1,), (1,)), ((), ()))
        for k in range(count // chunk):
            here = pl.ds(k * chunk, chunk)
            pair = lax.dot_general(own_ref[...], panel_ref[here, mine], nt, preferred_element_type=F32)
            pair += lax.dot_general(proj[...], panel_ref[here, sibs], nt, preferred_element_type=F32)
            weighted = jnp.concatenate(
                [
                    (
                        (scr_refs[0][:, here] if j == 0 else scr_refs[j][0, :, here].astype(F32))
                        * pair[j * points : (j + 1) * points]
                    ).astype(BF16)
                    for j in range(4)
                ],
                0,
            )
            send = jnp.dot(weighted, panel_ref[here, sibs], preferred_element_type=F32)
            keep = jnp.dot(weighted, panel_ref[here, mine], preferred_element_type=F32)
            if k == 0:
                send_ref[...] = send
                keep_ref[...] = keep
            else:
                send_ref[...] += send
                keep_ref[...] += keep

    return pl.pallas_call(
        kernel,
        out_shape=[jax.ShapeDtypeStruct((rows, half), F32)] * 2,
        in_specs=[vmem_spec()] * 11,
        out_specs=[vmem_spec()] * 2,
        scratch_shapes=[pltpu.VMEM((rows, half), BF16), pltpu.VMEM((count, states), BF16)],
        compiler_params=params(24),
        name="direct",
    )(proj_own, proj_other, *lines, own, *boxes)


def finish(psi, keep, got):
    states, count = psi.shape
    points = count // 4
    cols = keep.shape[1]

    def kernel(psi_ref, keep_ref, got_ref, out_ref, high, low):
        for k in range(4):
            here = slice(k * points, (k + 1) * points)
            there = slice(SIBLING[k] * points, (SIBLING[k] + 1) * points)
            back = keep_ref[here, :] + got_ref[there, :]
            top = back.astype(BF16)
            high[here, :] = top
            low[here, :] = (back - top.astype(F32)).astype(BF16)
        total = jnp.dot(psi_ref[...], high[...], preferred_element_type=F32)
        total += jnp.dot(psi_ref[...], low[...], preferred_element_type=F32)
        out_ref[...] = total.astype(BF16)

    return pl.pallas_call(
        kernel,
        out_shape=jax.ShapeDtypeStruct((states, cols), BF16),
        in_specs=[vmem_spec()] * 3,
        out_specs=vmem_spec(),
        scratch_shapes=[pltpu.VMEM((count, cols), BF16)] * 2,
        compiler_params=params(16),
        name="finish",
    )(psi, keep, got)


def shards(trial, psi_v, psi_c, screened):
    rows, states = trial.shape[1:]
    half = states // 2
    devices = lax.axis_size(TILE_VEC)
    own, near, far = pack(screened, psi_v)
    block = psi_c[:, 0, :].T
    line = jnp.concatenate([block, shift(block, "x", 1), shift(block, "x", -1), shift(block, "x", 2)], 0)
    halves = trial[0].reshape(rows, 2, half).transpose(1, 0, 2)
    copies = jnp.broadcast_to(halves[None, :, None], (devices // 4, 2, 2, rows, half))
    copies, near, far, line = lax.optimization_barrier((copies, near, far, line))
    trial_half = exchange(copies.reshape(devices, rows, half), TILE_VEC).reshape(-1, half)
    near = swap(near)
    far = lax.ppermute(far, "zh", [(0, 1), (1, 0)])
    behind, ahead = shift(line, "y", 1), shift(line, "y", -1)
    middle = line.shape[0] // 2
    beyond = [shift(behind[:middle], "y", 1), shift(ahead[middle:], "y", -1)]
    far, beyond = lax.optimization_barrier((far, beyond))
    passed = swap(far[1:])
    proj_own, psi = project(trial_half, psi_v, near, far, passed)
    proj_other = swap(proj_own)
    panel = [line, behind, ahead, *beyond]
    keep, send = direct(proj_own, proj_other, panel, own, [near, far, passed])
    got = swap(send)
    term = finish(psi, keep, got)
    parts = exchange(term.reshape(devices, rows, half), TILE_VEC)
    parts = parts.reshape(-1, 2, 2, rows, half).astype(F32)
    total = jnp.sum(parts, axis=(0, 2))
    return total.transpose(1, 0, 2).reshape(1, rows, states)


def solution(mesh):
    split = Mesh(
        mesh.devices.reshape(2, 4, 4, 2, mesh.shape["vec"]),
        TILE_VEC,
    )
    return jax.shard_map(
        shards,
        mesh=split,
        in_specs=(P(None, TILE_VEC, None), P(None, TILE), P(None, "zl", TILE), P(TILE, "zl")),
        out_specs=P(None, TILE_VEC, None),
        check_vma=False,
    )
```

```python
import jax
import jax.numpy as jnp
from jax import lax
from jax.experimental import pallas as pl
from jax.experimental.pallas import tpu as pltpu
from jax.sharding import Mesh
from jax.sharding import PartitionSpec as P

TILE_VEC = ("zh", "y", "x", "core", "zl")
TILE = ("zh", "y", "x", "core")
STEPS = (0, -1, 1, -2)
F32 = jnp.float32
BF16 = jnp.bfloat16
SIBLING = (1, 0, 3, 2)


def shift(value, axis, by):
    n = lax.axis_size(axis)
    return lax.ppermute(value, axis, [(k, (k + by) % n) for k in range(n)])


def exchange(value, axes):
    return lax.all_to_all(value, axes, split_axis=0, concat_axis=0, tiled=True)


def swap(value):
    return lax.ppermute(value, "core", [(0, 1), (1, 0)])


def vmem_spec():
    return pl.BlockSpec(memory_space=pltpu.VMEM)


def params(mebibytes):
    return pltpu.CompilerParams(vmem_limit_bytes=mebibytes * 1024 * 1024)


def pack(screened, left):
    points, count = screened.shape
    plane, steps = count // 2, 4
    width = plane // 2
    rows = points // steps

    def kernel(in_ref, left_ref, own_ref, near_ref, far_ref):
        core, zh = lax.axis_index("core"), lax.axis_index("zh")
        low = lax.broadcasted_iota(jnp.int32, (rows, 128), 1) < 64
        first = core == 0
        for far in range(2):
            base = plane * (zh if far == 0 else 1 - zh)
            for m in range(width // 128):
                a = in_ref[:, pl.ds(pl.multiple_of(base + m * 256, 256), 128)]
                b = in_ref[:, pl.ds(pl.multiple_of(base + m * 256 + 128, 128), 128)]
                zero = jnp.where(low, a, pltpu.roll(b, 64, 1))
                one = jnp.where(low, pltpu.roll(a, 64, 1), b)
                here = pl.ds(m * 128, 128)
                mine, others = jnp.where(first, zero, one), jnp.where(first, one, zero)
                if far == 0:
                    own_ref[:, here] = mine
                    near_ref[0, :, here] = others.astype(BF16)
                else:
                    far_ref[0, :, here] = mine.astype(BF16)
                    far_ref[1, :, here] = others.astype(BF16)
        for g in range(left_ref.shape[0] // points):
            start = pl.multiple_of(g * points + pl.program_id(0) * rows, rows)
            piece = left_ref[pl.ds(start, rows), :]
            near_ref[1, :, pl.ds(g * points, points)] = piece
            far_ref[2, :, pl.ds(g * points, points)] = piece

    return pl.pallas_call(
        kernel,
        grid=(steps,),
        out_shape=[
            jax.ShapeDtypeStruct((points, width), F32),
            jax.ShapeDtypeStruct((2, points, width), BF16),
            jax.ShapeDtypeStruct((3, points, width), BF16),
        ],
        in_specs=[
            pl.BlockSpec((rows, count), lambda k: (k, 0)),
            pl.BlockSpec(left.shape, lambda k: (0, 0)),
        ],
        out_specs=[
            pl.BlockSpec((rows, width), lambda k: (k, 0)),
            pl.BlockSpec((2, rows, width), lambda k: (0, k, 0)),
            pl.BlockSpec((3, rows, width), lambda k: (0, k, 0)),
        ],
        compiler_params=params(58),
        name="pack",
    )(screened, left)


def project(trial_half, left, near, far, passed):
    states, points = left.shape
    cols = trial_half.shape[1]

    def kernel(trial_ref, left_ref, *refs):
        boxes, (out_ref, psi_ref) = refs[:3], refs[3:]
        psi_ref[:, :points] = left_ref[...]
        for k in range(1, 4):
            box = boxes[k - 1]
            for g in range(states // points):
                psi_ref[g * points : (g + 1) * points, k * points : (k + 1) * points] = box[
                    box.shape[0] - 1, :, g * points : (g + 1) * points
                ]
        out_ref[...] = lax.dot_general(
            psi_ref[...], trial_ref[...], (((0,), (0,)), ((), ())), preferred_element_type=F32
        ).astype(BF16)

    return pl.pallas_call(
        kernel,
        out_shape=[
            jax.ShapeDtypeStruct((4 * points, cols), BF16),
            jax.ShapeDtypeStruct((states, 4 * points), BF16),
        ],
        in_specs=[vmem_spec()] * 5,
        out_specs=[vmem_spec()] * 2,
        compiler_params=params(12),
        name="project",
    )(trial_half, left, near, far, passed)


def direct(proj_own, proj_other, lines, own, boxes):
    rows, half = proj_own.shape
    points = rows // 4
    block = lines[0].shape[0] // 4
    count, states = 16 * block, lines[0].shape[1]
    chunk = 512

    def kernel(own_ref, other_ref, *refs):
        line_refs, scr_refs, (keep_ref, send_ref, proj, panel_ref) = refs[:5], refs[5:9], refs[9:]
        y, x = lax.axis_index("y"), lax.axis_index("x")
        for k in range(16):
            at = lax.rem(y + STEPS[k // 4] + 4, 4) * 4 + lax.rem(x + STEPS[k % 4] + 4, 4)
            ref, row = (line_refs[k // 4], k % 4) if k < 12 else (line_refs[k // 2 - 3], k % 2)
            panel_ref[pl.ds(pl.multiple_of(at * block, block), block), :] = ref[
                row * block : (row + 1) * block, :
            ]
        core = lax.axis_index("core")
        mine = pl.ds(pl.multiple_of(core * half, half), half)
        sibs = pl.ds(pl.multiple_of((1 - core) * half, half), half)
        for k in range(4):
            proj[k * points : (k + 1) * points, :] = other_ref[
                SIBLING[k] * points : (SIBLING[k] + 1) * points, :
            ]
        nt = (((1,), (1,)), ((), ()))
        for k in range(count // chunk):
            here = pl.ds(k * chunk, chunk)
            pair = lax.dot_general(own_ref[...], panel_ref[here, mine], nt, preferred_element_type=F32)
            pair += lax.dot_general(proj[...], panel_ref[here, sibs], nt, preferred_element_type=F32)
            weighted = jnp.concatenate(
                [
                    (
                        (scr_refs[0][:, here] if j == 0 else scr_refs[j][j // 3, :, here].astype(F32))
                        * pair[j * points : (j + 1) * points]
                    ).astype(BF16)
                    for j in range(4)
                ],
                0,
            )
            send = jnp.dot(weighted, panel_ref[here, sibs], preferred_element_type=F32)
            keep = jnp.dot(weighted, panel_ref[here, mine], preferred_element_type=F32)
            if k == 0:
                send_ref[...] = send
                keep_ref[...] = keep
            else:
                send_ref[...] += send
                keep_ref[...] += keep

    return pl.pallas_call(
        kernel,
        out_shape=[jax.ShapeDtypeStruct((rows, half), F32)] * 2,
        in_specs=[vmem_spec()] * 11,
        out_specs=[vmem_spec()] * 2,
        scratch_shapes=[pltpu.VMEM((rows, half), BF16), pltpu.VMEM((count, states), BF16)],
        compiler_params=params(24),
        name="direct",
    )(proj_own, proj_other, *lines, own, *boxes)


def finish(psi, keep, got):
    states, count = psi.shape
    points = count // 4
    cols = keep.shape[1]

    def kernel(psi_ref, keep_ref, got_ref, out_ref, high, low):
        for k in range(4):
            here = slice(k * points, (k + 1) * points)
            there = slice(SIBLING[k] * points, (SIBLING[k] + 1) * points)
            back = keep_ref[here, :] + got_ref[there, :]
            top = back.astype(BF16)
            high[here, :] = top
            low[here, :] = (back - top.astype(F32)).astype(BF16)
        total = jnp.dot(psi_ref[...], high[...], preferred_element_type=F32)
        total += jnp.dot(psi_ref[...], low[...], preferred_element_type=F32)
        out_ref[...] = total.astype(BF16)

    return pl.pallas_call(
        kernel,
        out_shape=jax.ShapeDtypeStruct((states, cols), BF16),
        in_specs=[vmem_spec()] * 3,
        out_specs=vmem_spec(),
        scratch_shapes=[pltpu.VMEM((count, cols), BF16)] * 2,
        compiler_params=params(16),
        name="finish",
    )(psi, keep, got)


def shards(trial, psi_v, psi_c, screened):
    rows, states = trial.shape[1:]
    half = states // 2
    devices = lax.axis_size(TILE_VEC)
    own, near, far = pack(screened, psi_v)
    block = psi_c[:, 0, :].T
    line = jnp.concatenate([block, shift(block, "x", 1), shift(block, "x", -1), shift(block, "x", 2)], 0)
    halves = trial[0].reshape(rows, 2, half).transpose(1, 0, 2)
    copies = jnp.broadcast_to(halves[None, :, None], (devices // 4, 2, 2, rows, half))
    copies, near, far, line = lax.optimization_barrier((copies, near, far, line))
    trial_half = exchange(copies.reshape(devices, rows, half), TILE_VEC).reshape(-1, half)
    near = swap(near)
    far = lax.ppermute(far, "zh", [(0, 1), (1, 0)])
    behind, ahead = shift(line, "y", 1), shift(line, "y", -1)
    middle = line.shape[0] // 2
    beyond = [shift(behind[:middle], "y", 1), shift(ahead[middle:], "y", -1)]
    far, *_ = lax.optimization_barrier((far, behind, ahead))
    passed = swap(far)
    proj_own, psi = project(trial_half, psi_v, near, far, passed)
    proj_own, beyond = lax.optimization_barrier((proj_own, beyond))
    proj_other = swap(proj_own)
    panel = [line, behind, ahead, *beyond]
    keep, send = direct(proj_own, proj_other, panel, own, [near, far, passed])
    got = swap(send)
    term = finish(psi, keep, got)
    parts = exchange(term.reshape(devices, rows, half), TILE_VEC)
    parts = parts.reshape(-1, 2, 2, rows, half).astype(F32)
    total = jnp.sum(parts, axis=(0, 2))
    return total.transpose(1, 0, 2).reshape(1, rows, states)


def solution(mesh):
    split = Mesh(
        mesh.devices.reshape(2, 4, 4, 2, mesh.shape["vec"]),
        TILE_VEC,
    )
    return jax.shard_map(
        shards,
        mesh=split,
        in_specs=(P(None, TILE_VEC, None), P(None, TILE), P(None, "zl", TILE), P(TILE, "zl")),
        out_specs=P(None, TILE_VEC, None),
        check_vma=False,
    )
```

```python
import jax
import jax.numpy as jnp
from jax import lax
from jax.experimental import pallas as pl
from jax.experimental.pallas import tpu as pltpu
from jax.sharding import Mesh
from jax.sharding import PartitionSpec as P

TILE_VEC = ("zh", "y", "x", "core", "zl")
TILE = ("zh", "y", "x", "core")
STEPS = (0, -1, 1, -2)
F32 = jnp.float32
BF16 = jnp.bfloat16
SIBLING = (1, 0, 3, 2)


def shift(value, axis, by):
    n = lax.axis_size(axis)
    return lax.ppermute(value, axis, [(k, (k + by) % n) for k in range(n)])


def exchange(value, axes):
    return lax.all_to_all(value, axes, split_axis=0, concat_axis=0, tiled=True)


def swap(value):
    return lax.ppermute(value, "core", [(0, 1), (1, 0)])


def across(value):
    return lax.ppermute(value, "zh", [(0, 1), (1, 0)])


def vmem_spec():
    return pl.BlockSpec(memory_space=pltpu.VMEM)


def params(mebibytes):
    return pltpu.CompilerParams(vmem_limit_bytes=mebibytes * 1024 * 1024)


def project(trial_half, lefts):
    states, points = lefts[0].shape
    cols = trial_half.shape[1]

    def kernel(trial_ref, *refs):
        left_refs, (out_ref, psi_ref) = refs[:4], refs[4:]
        for k in range(4):
            psi_ref[:, k * points : (k + 1) * points] = left_refs[k][...]
        out_ref[...] = lax.dot_general(
            psi_ref[...], trial_ref[...], (((0,), (0,)), ((), ())), preferred_element_type=F32
        ).astype(BF16)

    return pl.pallas_call(
        kernel,
        out_shape=[
            jax.ShapeDtypeStruct((4 * points, cols), BF16),
            jax.ShapeDtypeStruct((states, 4 * points), BF16),
        ],
        in_specs=[vmem_spec()] * 5,
        out_specs=[vmem_spec()] * 2,
        compiler_params=params(12),
        name="project",
    )(trial_half, *lefts)


def direct(proj_own, proj_other, lines, screened, raws):
    rows, half = proj_own.shape
    points = rows // 4
    block = lines[0].shape[0] // 4
    count, states = 16 * block, lines[0].shape[1]
    chunk = 512

    def kernel(own_ref, other_ref, *refs):
        line_refs, screened_ref, raw_refs, refs = refs[:5], refs[5], refs[6:9], refs[9:]
        keep_ref, send_ref, proj, panel_ref, weighted, mine_ref, sem = refs
        y, x, zh = lax.axis_index("y"), lax.axis_index("x"), lax.axis_index("zh")
        core = lax.axis_index("core")
        plane = pl.ds(pl.multiple_of(zh * 2 * count, 2 * count), 2 * count)
        load = pltpu.make_async_copy(screened_ref.at[:, plane], mine_ref, sem)
        load.start()
        for k in range(16):
            at = lax.rem(y + STEPS[k // 4] + 4, 4) * 4 + lax.rem(x + STEPS[k % 4] + 4, 4)
            ref, row = (line_refs[k // 4], k % 4) if k < 12 else (line_refs[k // 2 - 3], k % 2)
            panel_ref[pl.ds(pl.multiple_of(at * block, block), block), :] = ref[
                row * block : (row + 1) * block, :
            ]
        mine = pl.ds(pl.multiple_of(core * half, half), half)
        sibs = pl.ds(pl.multiple_of((1 - core) * half, half), half)
        for k in range(4):
            proj[k * points : (k + 1) * points, :] = other_ref[
                SIBLING[k] * points : (SIBLING[k] + 1) * points, :
            ]
        low = lax.broadcasted_iota(jnp.int32, (points, 128), 1) < 64
        first = core == 0
        nt = (((1,), (1,)), ((), ()))
        for k in range(count // chunk):
            here = pl.ds(k * chunk, chunk)
            pair = lax.dot_general(own_ref[...], panel_ref[here, mine], nt, preferred_element_type=F32)
            pair += lax.dot_general(proj[...], panel_ref[here, sibs], nt, preferred_element_type=F32)
            if k == 0:
                load.wait()
            for j, ref in enumerate((mine_ref, *raw_refs)):
                for m in range(chunk // 128):
                    start = 2 * (k * chunk + m * 128)
                    a = ref[:, start : start + 128].astype(F32)
                    b = ref[:, start + 128 : start + 256].astype(F32)
                    rolled = pltpu.roll(jnp.where(first, b, a), 64, 1)
                    weights = jnp.where(
                        low, jnp.where(first, a, rolled), jnp.where(first, rolled, b)
                    )
                    part = pair[j * points : (j + 1) * points, m * 128 : (m + 1) * 128]
                    weighted[j * points : (j + 1) * points, m * 128 : (m + 1) * 128] = (
                        weights * part
                    ).astype(BF16)
            send = jnp.dot(weighted[...], panel_ref[here, sibs], preferred_element_type=F32)
            keep = jnp.dot(weighted[...], panel_ref[here, mine], preferred_element_type=F32)
            if k == 0:
                send_ref[...] = send
                keep_ref[...] = keep
            else:
                send_ref[...] += send
                keep_ref[...] += keep

    return pl.pallas_call(
        kernel,
        out_shape=[jax.ShapeDtypeStruct((rows, half), F32)] * 2,
        in_specs=[vmem_spec()] * 7 + [pl.BlockSpec(memory_space=pl.ANY)] + [vmem_spec()] * 3,
        out_specs=[vmem_spec()] * 2,
        scratch_shapes=[
            pltpu.VMEM((rows, half), BF16),
            pltpu.VMEM((count, states), BF16),
            pltpu.VMEM((rows, chunk), BF16),
            pltpu.VMEM((points, 2 * count), F32),
            pltpu.SemaphoreType.DMA,
        ],
        compiler_params=params(24),
        name="direct",
    )(proj_own, proj_other, *lines, screened, *raws)


def finish(psi, keep, got):
    states, count = psi.shape
    points = count // 4
    cols = keep.shape[1]

    def kernel(psi_ref, keep_ref, got_ref, out_ref, high, low):
        for k in range(4):
            here = slice(k * points, (k + 1) * points)
            there = slice(SIBLING[k] * points, (SIBLING[k] + 1) * points)
            back = keep_ref[here, :] + got_ref[there, :]
            top = back.astype(BF16)
            high[here, :] = top
            low[here, :] = (back - top.astype(F32)).astype(BF16)
        total = jnp.dot(psi_ref[...], high[...], preferred_element_type=F32)
        total += jnp.dot(psi_ref[...], low[...], preferred_element_type=F32)
        out_ref[...] = total.astype(BF16)

    return pl.pallas_call(
        kernel,
        out_shape=jax.ShapeDtypeStruct((states, cols), BF16),
        in_specs=[vmem_spec()] * 3,
        out_specs=vmem_spec(),
        scratch_shapes=[pltpu.VMEM((count, cols), BF16)] * 2,
        compiler_params=params(16),
        name="finish",
    )(psi, keep, got)


def shards(trial, psi_v, psi_c, screened):
    rows, states = trial.shape[1:]
    half = states // 2
    devices = lax.axis_size(TILE_VEC)
    zh = lax.axis_index("zh")
    width = screened.shape[1] // 2
    partner = across(psi_v)
    far = across(lax.dynamic_slice_in_dim(screened, (1 - zh) * width, width, 1).astype(BF16))
    near = lax.dynamic_slice_in_dim(screened, zh * width, width, 1).astype(BF16)
    block = psi_c[:, 0, :].T
    line = jnp.concatenate([block, shift(block, "x", 1), shift(block, "x", -1), shift(block, "x", 2)], 0)
    halves = trial[0].reshape(rows, 2, half).transpose(1, 0, 2)
    copies = jnp.broadcast_to(halves[None, :, None], (devices // 4, 2, 2, rows, half))
    copies, line, near, partner = lax.optimization_barrier((copies, line, near, partner))
    trial_half = exchange(copies.reshape(devices, rows, half), TILE_VEC).reshape(-1, half)
    behind, ahead = shift(line, "y", 1), shift(line, "y", -1)
    middle = line.shape[0] // 2
    beyond = [shift(behind[:middle], "y", 1), shift(ahead[middle:], "y", -1)]
    far, *_ = lax.optimization_barrier((far, behind, ahead))
    raws = [swap(near), far, swap(far)]
    lefts = [psi_v, swap(psi_v), partner, swap(partner)]
    proj_own, psi = project(trial_half, lefts)
    proj_own, beyond = lax.optimization_barrier((proj_own, beyond))
    proj_other = swap(proj_own)
    panel = [line, behind, ahead, *beyond]
    keep, send = direct(proj_own, proj_other, panel, screened, raws)
    got = swap(send)
    term = finish(psi, keep, got)
    parts = exchange(term.reshape(devices, rows, half), TILE_VEC)
    parts = parts.reshape(-1, 2, 2, rows, half).astype(F32)
    total = jnp.sum(parts, axis=(0, 2))
    return total.transpose(1, 0, 2).reshape(1, rows, states)


def solution(mesh):
    split = Mesh(
        mesh.devices.reshape(2, 4, 4, 2, mesh.shape["vec"]),
        TILE_VEC,
    )
    return jax.shard_map(
        shards,
        mesh=split,
        in_specs=(P(None, TILE_VEC, None), P(None, TILE), P(None, "zl", TILE), P(TILE, "zl")),
        out_specs=P(None, TILE_VEC, None),
        check_vma=False,
    )
```

```python
import jax
import jax.numpy as jnp
from jax import lax
from jax.experimental import pallas as pl
from jax.experimental.pallas import tpu as pltpu
from jax.sharding import Mesh
from jax.sharding import PartitionSpec as P

TILE_VEC = ("zh", "y", "x", "core", "zl")
TILE = ("zh", "y", "x", "core")
STEPS = (0, -1, 1, -2)
F32 = jnp.float32
BF16 = jnp.bfloat16
SIBLING = (1, 0, 3, 2)


def shift(value, axis, by):
    n = lax.axis_size(axis)
    return lax.ppermute(value, axis, [(k, (k + by) % n) for k in range(n)])


def exchange(value, axes):
    return lax.all_to_all(value, axes, split_axis=0, concat_axis=0, tiled=True)


def swap(value):
    return lax.ppermute(value, "core", [(0, 1), (1, 0)])


def vmem_spec():
    return pl.BlockSpec(memory_space=pltpu.VMEM)


def params(mebibytes):
    return pltpu.CompilerParams(vmem_limit_bytes=mebibytes * 1024 * 1024)


def pack(screened, left):
    points, count = screened.shape
    plane, steps = count // 2, 4
    width = plane // 2
    rows = points // steps

    def kernel(in_ref, left_ref, own_ref, near_ref, far_ref):
        core, zh = lax.axis_index("core"), lax.axis_index("zh")
        low = lax.broadcasted_iota(jnp.int32, (rows, 128), 1) < 64
        first = core == 0
        for far in range(2):
            base = plane * (zh if far == 0 else 1 - zh)
            for m in range(width // 128):
                a = in_ref[:, pl.ds(pl.multiple_of(base + m * 256, 256), 128)]
                b = in_ref[:, pl.ds(pl.multiple_of(base + m * 256 + 128, 128), 128)]
                zero = jnp.where(low, a, pltpu.roll(b, 64, 1))
                one = jnp.where(low, pltpu.roll(a, 64, 1), b)
                here = pl.ds(m * 128, 128)
                mine, others = jnp.where(first, zero, one), jnp.where(first, one, zero)
                if far == 0:
                    own_ref[:, here] = mine
                    near_ref[0, :, here] = others.astype(BF16)
                else:
                    far_ref[0, :, here] = mine.astype(BF16)
                    far_ref[1, :, here] = others.astype(BF16)
        for g in range(left_ref.shape[0] // points):
            start = pl.multiple_of(g * points + pl.program_id(0) * rows, rows)
            piece = left_ref[pl.ds(start, rows), :]
            near_ref[1, :, pl.ds(g * points, points)] = piece
            far_ref[2, :, pl.ds(g * points, points)] = piece

    return pl.pallas_call(
        kernel,
        grid=(steps,),
        out_shape=[
            jax.ShapeDtypeStruct((points, width), F32),
            jax.ShapeDtypeStruct((2, points, width), BF16),
            jax.ShapeDtypeStruct((3, points, width), BF16),
        ],
        in_specs=[
            pl.BlockSpec((rows, count), lambda k: (k, 0)),
            pl.BlockSpec(left.shape, lambda k: (0, 0)),
        ],
        out_specs=[
            pl.BlockSpec((rows, width), lambda k: (k, 0)),
            pl.BlockSpec((2, rows, width), lambda k: (0, k, 0)),
            pl.BlockSpec((3, rows, width), lambda k: (0, k, 0)),
        ],
        compiler_params=params(8),
        name="pack",
    )(screened, left)


def project(trial_half, left, near, far, passed):
    states, points = left.shape
    cols = trial_half.shape[1]

    def kernel(trial_ref, left_ref, *refs):
        boxes, (out_ref, psi_ref) = refs[:3], refs[3:]
        psi_ref[:, :points] = left_ref[...]
        for k in range(1, 4):
            box = boxes[k - 1]
            for g in range(states // points):
                psi_ref[g * points : (g + 1) * points, k * points : (k + 1) * points] = box[
                    box.shape[0] - 1, :, g * points : (g + 1) * points
                ]
        out_ref[...] = lax.dot_general(
            psi_ref[...], trial_ref[...], (((0,), (0,)), ((), ())), preferred_element_type=F32
        ).astype(BF16)

    return pl.pallas_call(
        kernel,
        out_shape=[
            jax.ShapeDtypeStruct((4 * points, cols), BF16),
            jax.ShapeDtypeStruct((states, 4 * points), BF16),
        ],
        in_specs=[vmem_spec()] * 5,
        out_specs=[vmem_spec()] * 2,
        compiler_params=params(12),
        name="project",
    )(trial_half, left, near, far, passed)


def direct(proj_own, proj_other, lines, own, boxes):
    rows, half = proj_own.shape
    points = rows // 4
    block = lines[0].shape[0] // 4
    count, states = 16 * block, lines[0].shape[1]
    chunk = 512

    def kernel(own_ref, other_ref, *refs):
        line_refs, scr_refs, (keep_ref, send_ref, proj, panel_ref) = refs[:4], refs[4:8], refs[8:]
        y, x = lax.axis_index("y"), lax.axis_index("x")
        for k in range(16):
            at = lax.rem(y + STEPS[k // 4] + 4, 4) * 4 + lax.rem(x + STEPS[k % 4] + 4, 4)
            panel_ref[pl.ds(pl.multiple_of(at * block, block), block), :] = line_refs[k // 4][
                k % 4 * block : (k % 4 + 1) * block, :
            ]
        core = lax.axis_index("core")
        mine = pl.ds(pl.multiple_of(core * half, half), half)
        sibs = pl.ds(pl.multiple_of((1 - core) * half, half), half)
        for k in range(4):
            proj[k * points : (k + 1) * points, :] = other_ref[
                SIBLING[k] * points : (SIBLING[k] + 1) * points, :
            ]
        nt = (((1,), (1,)), ((), ()))
        for k in range(count // chunk):
            here = pl.ds(k * chunk, chunk)
            pair = lax.dot_general(own_ref[...], panel_ref[here, mine], nt, preferred_element_type=F32)
            pair += lax.dot_general(proj[...], panel_ref[here, sibs], nt, preferred_element_type=F32)
            weighted = jnp.concatenate(
                [
                    (
                        (scr_refs[0][:, here] if j == 0 else scr_refs[j][j // 3, :, here].astype(F32))
                        * pair[j * points : (j + 1) * points]
                    ).astype(BF16)
                    for j in range(4)
                ],
                0,
            )
            send = jnp.dot(weighted, panel_ref[here, sibs], preferred_element_type=F32)
            keep = jnp.dot(weighted, panel_ref[here, mine], preferred_element_type=F32)
            if k == 0:
                send_ref[...] = send
                keep_ref[...] = keep
            else:
                send_ref[...] += send
                keep_ref[...] += keep

    return pl.pallas_call(
        kernel,
        out_shape=[jax.ShapeDtypeStruct((rows, half), F32)] * 2,
        in_specs=[vmem_spec()] * 10,
        out_specs=[vmem_spec()] * 2,
        scratch_shapes=[pltpu.VMEM((rows, half), BF16), pltpu.VMEM((count, states), BF16)],
        compiler_params=params(24),
        name="direct",
    )(proj_own, proj_other, *lines, own, *boxes)


def finish(psi, keep, got):
    states, count = psi.shape
    points = count // 4
    cols = keep.shape[1]

    def kernel(psi_ref, keep_ref, got_ref, out_ref, high, low):
        for k in range(4):
            here = slice(k * points, (k + 1) * points)
            there = slice(SIBLING[k] * points, (SIBLING[k] + 1) * points)
            back = keep_ref[here, :] + got_ref[there, :]
            top = back.astype(BF16)
            high[here, :] = top
            low[here, :] = (back - top.astype(F32)).astype(BF16)
        total = jnp.dot(psi_ref[...], high[...], preferred_element_type=F32)
        total += jnp.dot(psi_ref[...], low[...], preferred_element_type=F32)
        out_ref[...] = total.astype(BF16)

    return pl.pallas_call(
        kernel,
        out_shape=jax.ShapeDtypeStruct((states, cols), BF16),
        in_specs=[vmem_spec()] * 3,
        out_specs=vmem_spec(),
        scratch_shapes=[pltpu.VMEM((count, cols), BF16)] * 2,
        compiler_params=params(16),
        name="finish",
    )(psi, keep, got)


def shards(trial, psi_v, psi_c, screened):
    rows, states = trial.shape[1:]
    half = states // 2
    devices = lax.axis_size(TILE_VEC)
    own, near, far = pack(screened, psi_v)
    block = psi_c[:, 0, :].T
    line = jnp.concatenate([block, shift(block, "x", 1), shift(block, "x", -1), shift(block, "x", 2)], 0)
    halves = trial[0].reshape(rows, 2, half).transpose(1, 0, 2)
    copies = jnp.broadcast_to(halves[None, :, None], (devices // 4, 2, 2, rows, half))
    copies, near, far, line = lax.optimization_barrier((copies, near, far, line))
    trial_half = exchange(copies.reshape(devices, rows, half), TILE_VEC).reshape(-1, half)
    near = swap(near)
    far = lax.ppermute(far, "zh", [(0, 1), (1, 0)])
    behind, ahead = shift(line, "y", 1), shift(line, "y", -1)
    opposite = shift(line, "y", 2)
    far, *_ = lax.optimization_barrier((far, behind, ahead, opposite))
    passed = swap(far)
    proj_own, psi = project(trial_half, psi_v, near, far, passed)
    proj_other = swap(proj_own)
    panel = [line, behind, ahead, opposite]
    keep, send = direct(proj_own, proj_other, panel, own, [near, far, passed])
    got = swap(send)
    term = finish(psi, keep, got)
    parts = exchange(term.reshape(devices, rows, half), TILE_VEC)
    parts = parts.reshape(-1, 2, 2, rows, half).astype(F32)
    total = jnp.sum(parts, axis=(0, 2))
    return total.transpose(1, 0, 2).reshape(1, rows, states)


def solution(mesh):
    split = Mesh(
        mesh.devices.reshape(2, 4, 4, 2, mesh.shape["vec"]),
        TILE_VEC,
    )
    return jax.shard_map(
        shards,
        mesh=split,
        in_specs=(P(None, TILE_VEC, None), P(None, TILE), P(None, "zl", TILE), P(TILE, "zl")),
        out_specs=P(None, TILE_VEC, None),
        check_vma=False,
    )
```

```python
import jax
import jax.numpy as jnp
from jax import lax
from jax.experimental import pallas as pl
from jax.experimental.pallas import tpu as pltpu
from jax.sharding import Mesh
from jax.sharding import PartitionSpec as P

TILE_VEC = ("zh", "y", "x", "core", "zl")
TILE = ("zh", "y", "x", "core")
PLANE = ("y", "x")
ORDER = ("zh", "core", "zl", "y", "x")
STEPS = (0, -1, 1, -2)
F32 = jnp.float32
BF16 = jnp.bfloat16
SIBLING = (1, 0, 3, 2)


def shift(value, axis, by):
    n = lax.axis_size(axis)
    return lax.ppermute(value, axis, [(k, (k + by) % n) for k in range(n)])


def exchange(value, axes):
    return lax.all_to_all(value, axes, split_axis=0, concat_axis=0, tiled=True)


def swap(value):
    return lax.ppermute(value, "core", [(0, 1), (1, 0)])


def vmem_spec():
    return pl.BlockSpec(memory_space=pltpu.VMEM)


def params(mebibytes):
    return pltpu.CompilerParams(vmem_limit_bytes=mebibytes * 1024 * 1024)


def pack(screened, left):
    points, count = screened.shape
    plane, steps = count // 2, 4
    width = plane // 2
    rows = points // steps

    def kernel(in_ref, left_ref, own_ref, near_ref, far_ref):
        core, zh = lax.axis_index("core"), lax.axis_index("zh")
        low = lax.broadcasted_iota(jnp.int32, (rows, 128), 1) < 64
        first = core == 0
        for far in range(2):
            base = plane * (zh if far == 0 else 1 - zh)
            for m in range(width // 128):
                a = in_ref[:, pl.ds(pl.multiple_of(base + m * 256, 256), 128)]
                b = in_ref[:, pl.ds(pl.multiple_of(base + m * 256 + 128, 128), 128)]
                zero = jnp.where(low, a, pltpu.roll(b, 64, 1))
                one = jnp.where(low, pltpu.roll(a, 64, 1), b)
                here = pl.ds(m * 128, 128)
                mine, others = jnp.where(first, zero, one), jnp.where(first, one, zero)
                if far == 0:
                    own_ref[:, here] = mine
                    near_ref[0, :, here] = others.astype(BF16)
                else:
                    far_ref[0, :, here] = mine.astype(BF16)
                    far_ref[1, :, here] = others.astype(BF16)
        for g in range(left_ref.shape[0] // points):
            start = pl.multiple_of(g * points + pl.program_id(0) * rows, rows)
            piece = left_ref[pl.ds(start, rows), :]
            near_ref[1, :, pl.ds(g * points, points)] = piece
            far_ref[2, :, pl.ds(g * points, points)] = piece

    return pl.pallas_call(
        kernel,
        grid=(steps,),
        out_shape=[
            jax.ShapeDtypeStruct((points, width), F32),
            jax.ShapeDtypeStruct((2, points, width), BF16),
            jax.ShapeDtypeStruct((3, points, width), BF16),
        ],
        in_specs=[
            pl.BlockSpec((rows, count), lambda k: (k, 0)),
            pl.BlockSpec(left.shape, lambda k: (0, 0)),
        ],
        out_specs=[
            pl.BlockSpec((rows, width), lambda k: (k, 0)),
            pl.BlockSpec((2, rows, width), lambda k: (0, k, 0)),
            pl.BlockSpec((3, rows, width), lambda k: (0, k, 0)),
        ],
        compiler_params=params(8),
        name="pack",
    )(screened, left)


def project(rounds, left, near, far, passed):
    states, points = left.shape
    block = rounds[0].shape[0] // 2
    cols = rounds[0].shape[1]

    def kernel(*refs):
        trial_refs, left_ref, boxes, (out_ref, psi_ref, trial) = refs[:4], refs[4], refs[5:8], refs[8:]
        core = lax.axis_index("core")
        place = 2 * lax.axis_index("zh") + lax.axis_index("zl")
        for k in range(4):
            source = lax.rem(place + STEPS[k] + 4, 4)
            for m in range(2):
                owner = core if m == 0 else 1 - core
                group = lax.div(source, 2) * 4 + owner * 2 + lax.rem(source, 2)
                trial[pl.ds(pl.multiple_of(group * block, block), block), :] = trial_refs[k][
                    m * block : (m + 1) * block, :
                ]
        psi_ref[:, :points] = left_ref[...]
        for k in range(1, 4):
            box = boxes[k - 1]
            for g in range(states // points):
                psi_ref[g * points : (g + 1) * points, k * points : (k + 1) * points] = box[
                    box.shape[0] - 1, :, g * points : (g + 1) * points
                ]
        out_ref[...] = lax.dot_general(
            psi_ref[...], trial[...], (((0,), (0,)), ((), ())), preferred_element_type=F32
        ).astype(BF16)

    return pl.pallas_call(
        kernel,
        out_shape=[
            jax.ShapeDtypeStruct((4 * points, cols), BF16),
            jax.ShapeDtypeStruct((states, 4 * points), BF16),
        ],
        in_specs=[vmem_spec()] * 8,
        out_specs=[vmem_spec()] * 2,
        scratch_shapes=[pltpu.VMEM((states, cols), BF16)],
        compiler_params=params(12),
        name="project",
    )(*rounds, left, near, far, passed)


def direct(proj_own, proj_other, lines, own, boxes):
    rows, half = proj_own.shape
    points = rows // 4
    block = lines[0].shape[0] // 4
    count, states = 16 * block, lines[0].shape[1]
    chunk = 512

    def kernel(own_ref, other_ref, *refs):
        line_refs, scr_refs, (keep_ref, send_ref, proj, panel_ref) = refs[:5], refs[5:9], refs[9:]
        y, x = lax.axis_index("y"), lax.axis_index("x")
        for k in range(16):
            at = lax.rem(y + STEPS[k // 4] + 4, 4) * 4 + lax.rem(x + STEPS[k % 4] + 4, 4)
            ref, row = (line_refs[k // 4], k % 4) if k < 12 else (line_refs[k // 2 - 3], k % 2)
            panel_ref[pl.ds(pl.multiple_of(at * block, block), block), :] = ref[
                row * block : (row + 1) * block, :
            ]
        core = lax.axis_index("core")
        mine = pl.ds(pl.multiple_of(core * half, half), half)
        sibs = pl.ds(pl.multiple_of((1 - core) * half, half), half)
        for k in range(4):
            proj[k * points : (k + 1) * points, :] = other_ref[
                SIBLING[k] * points : (SIBLING[k] + 1) * points, :
            ]
        nt = (((1,), (1,)), ((), ()))
        for k in range(count // chunk):
            here = pl.ds(k * chunk, chunk)
            pair = lax.dot_general(own_ref[...], panel_ref[here, mine], nt, preferred_element_type=F32)
            pair += lax.dot_general(proj[...], panel_ref[here, sibs], nt, preferred_element_type=F32)
            weighted = jnp.concatenate(
                [
                    (
                        (scr_refs[0][:, here] if j == 0 else scr_refs[j][0, :, here].astype(F32))
                        * pair[j * points : (j + 1) * points]
                    ).astype(BF16)
                    for j in range(4)
                ],
                0,
            )
            send = jnp.dot(weighted, panel_ref[here, sibs], preferred_element_type=F32)
            keep = jnp.dot(weighted, panel_ref[here, mine], preferred_element_type=F32)
            if k == 0:
                send_ref[...] = send
                keep_ref[...] = keep
            else:
                send_ref[...] += send
                keep_ref[...] += keep

    return pl.pallas_call(
        kernel,
        out_shape=[jax.ShapeDtypeStruct((rows, half), F32)] * 2,
        in_specs=[vmem_spec()] * 11,
        out_specs=[vmem_spec()] * 2,
        scratch_shapes=[pltpu.VMEM((rows, half), BF16), pltpu.VMEM((count, states), BF16)],
        compiler_params=params(24),
        name="direct",
    )(proj_own, proj_other, *lines, own, *boxes)


def finish(psi, keep, got):
    states, count = psi.shape
    points = count // 4
    cols = keep.shape[1]

    def kernel(psi_ref, keep_ref, got_ref, out_ref, high, low):
        for k in range(4):
            here = slice(k * points, (k + 1) * points)
            there = slice(SIBLING[k] * points, (SIBLING[k] + 1) * points)
            back = keep_ref[here, :] + got_ref[there, :]
            top = back.astype(BF16)
            high[here, :] = top
            low[here, :] = (back - top.astype(F32)).astype(BF16)
        total = jnp.dot(psi_ref[...], high[...], preferred_element_type=F32)
        total += jnp.dot(psi_ref[...], low[...], preferred_element_type=F32)
        out_ref[...] = total.astype(BF16)

    return pl.pallas_call(
        kernel,
        out_shape=jax.ShapeDtypeStruct((states, cols), BF16),
        in_specs=[vmem_spec()] * 3,
        out_specs=vmem_spec(),
        scratch_shapes=[pltpu.VMEM((count, cols), BF16)] * 2,
        compiler_params=params(16),
        name="finish",
    )(psi, keep, got)


def ring(value, by):
    return lax.ppermute(value, ("zh", "zl"), [(k, (k + by) % 4) for k in range(4)])


def to_all(value):
    copies = jnp.broadcast_to(value[None], (lax.axis_size(PLANE), *value.shape))
    return copies


def shards(trial, psi_v, psi_c, screened):
    rows, states = trial.shape[1:]
    half = states // 2
    devices = lax.axis_size(ORDER)
    core = lax.axis_index("core")
    left = psi_v.reshape(2, 4, 4, 2, 2, rows, -1).transpose(0, 3, 4, 1, 2, 5, 6).reshape(psi_v.shape)
    own, near, far = pack(screened, left)
    block = psi_c[:, 0, :].T
    line = jnp.concatenate([block, shift(block, "x", 1), shift(block, "x", -1), shift(block, "x", 2)], 0)
    copies, near, far, line = lax.optimization_barrier((to_all(trial[0]), near, far, line))
    level = exchange(copies, PLANE).reshape(-1, states)
    near = swap(near)
    far = lax.ppermute(far, "zh", [(0, 1), (1, 0)])
    behind, ahead = shift(line, "y", 1), shift(line, "y", -1)
    mine = lax.dynamic_slice_in_dim(level, core * half, half, 1)
    sent = lax.dynamic_slice_in_dim(level, (1 - core) * half, half, 1)
    pieces = jnp.concatenate([mine, swap(sent)], 0)
    pieces, near, behind, ahead = lax.optimization_barrier((pieces, near, behind, ahead))
    rounds = [pieces, ring(pieces, 1), ring(pieces, -1), ring(pieces, 2)]
    far, _ = lax.optimization_barrier((far, pieces))
    passed = swap(far[1:])
    middle = line.shape[0] // 2
    beyond = [shift(behind[:middle], "y", 1), shift(ahead[middle:], "y", -1)]
    rounds, beyond = lax.optimization_barrier((rounds, beyond))
    proj_own, psi = project(rounds, left, near, far, passed)
    proj_other = swap(proj_own)
    panel = [line, behind, ahead, *beyond]
    keep, send = direct(proj_own, proj_other, panel, own, [near, far, passed])
    got = swap(send)
    term = finish(psi, keep, got)
    parts = exchange(term.reshape(devices, rows, half), ORDER)
    parts = parts.reshape(2, 2, 2, -1, rows, half).astype(F32)
    total = jnp.sum(parts, axis=(0, 2, 3))
    return total.transpose(1, 0, 2).reshape(1, rows, states)


def solution(mesh):
    split = Mesh(
        mesh.devices.reshape(2, 4, 4, 2, mesh.shape["vec"]),
        TILE_VEC,
    )
    return jax.shard_map(
        shards,
        mesh=split,
        in_specs=(P(None, TILE_VEC, None), P(None, TILE), P(None, "zl", TILE), P(TILE, "zl")),
        out_specs=P(None, TILE_VEC, None),
        check_vma=False,
    )
```

```python
import jax
import jax.numpy as jnp
from jax import lax
from jax.experimental import pallas as pl
from jax.experimental.pallas import tpu as pltpu
from jax.sharding import Mesh
from jax.sharding import PartitionSpec as P

TILE_VEC = ("zh", "y", "x", "core", "zl")
TILE = ("zh", "y", "x", "core")
STEPS = (0, -1, 1, -2)
F32 = jnp.float32
BF16 = jnp.bfloat16
SIBLING = (1, 0, 3, 2)


def shift(value, axis, by):
    n = lax.axis_size(axis)
    return lax.ppermute(value, axis, [(k, (k + by) % n) for k in range(n)])


def exchange(value, axes):
    return lax.all_to_all(value, axes, split_axis=0, concat_axis=0, tiled=True)


def swap(value):
    return lax.ppermute(value, "core", [(0, 1), (1, 0)])


def vmem_spec():
    return pl.BlockSpec(memory_space=pltpu.VMEM)


def params(mebibytes):
    return pltpu.CompilerParams(vmem_limit_bytes=mebibytes * 1024 * 1024)


def pack(screened, left):
    points, count = screened.shape
    plane, steps = count // 2, 4
    width = plane // 2
    rows = points // steps

    def kernel(in_ref, left_ref, own_ref, near_ref, far_ref):
        core, zh = lax.axis_index("core"), lax.axis_index("zh")
        low = lax.broadcasted_iota(jnp.int32, (rows, 128), 1) < 64
        first = core == 0
        for far in range(2):
            base = plane * (zh if far == 0 else 1 - zh)
            for m in range(width // 128):
                a = in_ref[:, pl.ds(pl.multiple_of(base + m * 256, 256), 128)]
                b = in_ref[:, pl.ds(pl.multiple_of(base + m * 256 + 128, 128), 128)]
                zero = jnp.where(low, a, pltpu.roll(b, 64, 1))
                one = jnp.where(low, pltpu.roll(a, 64, 1), b)
                here = pl.ds(m * 128, 128)
                mine, others = jnp.where(first, zero, one), jnp.where(first, one, zero)
                if far == 0:
                    own_ref[:, here] = mine
                    near_ref[0, :, here] = others.astype(BF16)
                else:
                    far_ref[0, :, here] = mine.astype(BF16)
                    far_ref[1, :, here] = others.astype(BF16)
        for g in range(left_ref.shape[0] // points):
            start = pl.multiple_of(g * points + pl.program_id(0) * rows, rows)
            piece = left_ref[pl.ds(start, rows), :]
            near_ref[1, :, pl.ds(g * points, points)] = piece
            far_ref[2, :, pl.ds(g * points, points)] = piece

    return pl.pallas_call(
        kernel,
        grid=(steps,),
        out_shape=[
            jax.ShapeDtypeStruct((points, width), F32),
            jax.ShapeDtypeStruct((2, points, width), BF16),
            jax.ShapeDtypeStruct((3, points, width), BF16),
        ],
        in_specs=[
            pl.BlockSpec((rows, count), lambda k: (k, 0)),
            pl.BlockSpec(left.shape, lambda k: (0, 0)),
        ],
        out_specs=[
            pl.BlockSpec((rows, width), lambda k: (k, 0)),
            pl.BlockSpec((2, rows, width), lambda k: (0, k, 0)),
            pl.BlockSpec((3, rows, width), lambda k: (0, k, 0)),
        ],
        compiler_params=params(8),
        name="pack",
    )(screened, left)


def project(trial_half, left, near, far, passed):
    states, points = left.shape
    cols = trial_half.shape[1]

    def kernel(trial_ref, left_ref, *refs):
        boxes, (out_ref, psi_ref, sem) = refs[:3], refs[3:]
        load = pltpu.make_async_copy(left_ref, psi_ref.at[:, :points], sem)
        load.start()
        for k in range(1, 4):
            box = boxes[k - 1]
            for g in range(states // points):
                psi_ref[g * points : (g + 1) * points, k * points : (k + 1) * points] = box[
                    box.shape[0] - 1, :, g * points : (g + 1) * points
                ]
        load.wait()
        out_ref[...] = lax.dot_general(
            psi_ref[...], trial_ref[...], (((0,), (0,)), ((), ())), preferred_element_type=F32
        ).astype(BF16)

    return pl.pallas_call(
        kernel,
        out_shape=[
            jax.ShapeDtypeStruct((4 * points, cols), BF16),
            jax.ShapeDtypeStruct((states, 4 * points), BF16),
        ],
        in_specs=[vmem_spec(), pl.BlockSpec(memory_space=pl.ANY)] + [vmem_spec()] * 3,
        out_specs=[vmem_spec()] * 2,
        scratch_shapes=[pltpu.SemaphoreType.DMA],
        compiler_params=params(12),
        name="project",
    )(trial_half, left, near, far, passed)


def direct(proj_own, proj_other, lines, own, boxes):
    rows, half = proj_own.shape
    points = rows // 4
    block = lines[0].shape[0] // 4
    count, states = 16 * block, lines[0].shape[1]
    chunk = 512

    def kernel(own_ref, other_ref, *refs):
        line_refs, scr_refs, (weighted_ref, panel_ref, send_ref, proj) = refs[:5], refs[5:9], refs[9:]
        y, x = lax.axis_index("y"), lax.axis_index("x")
        for k in range(16):
            at = lax.rem(y + STEPS[k // 4] + 4, 4) * 4 + lax.rem(x + STEPS[k % 4] + 4, 4)
            ref, row = (line_refs[k // 4], k % 4) if k < 12 else (line_refs[k // 2 - 3], k % 2)
            panel_ref[pl.ds(pl.multiple_of(at * block, block), block), :] = ref[
                row * block : (row + 1) * block, :
            ]
        core = lax.axis_index("core")
        mine = pl.ds(pl.multiple_of(core * half, half), half)
        sibs = pl.ds(pl.multiple_of((1 - core) * half, half), half)
        for k in range(4):
            proj[k * points : (k + 1) * points, :] = other_ref[
                SIBLING[k] * points : (SIBLING[k] + 1) * points, :
            ]
        nt = (((1,), (1,)), ((), ()))
        for k in range(count // chunk):
            here = pl.ds(k * chunk, chunk)
            pair = lax.dot_general(own_ref[...], panel_ref[here, mine], nt, preferred_element_type=F32)
            pair += lax.dot_general(proj[...], panel_ref[here, sibs], nt, preferred_element_type=F32)
            weighted = jnp.concatenate(
                [
                    (
                        (scr_refs[0][:, here] if j == 0 else scr_refs[j][0, :, here].astype(F32))
                        * pair[j * points : (j + 1) * points]
                    ).astype(BF16)
                    for j in range(4)
                ],
                0,
            )
            weighted_ref[:, here] = weighted
        send_ref[...] = jnp.dot(weighted_ref[...], panel_ref[:, sibs], preferred_element_type=F32)

    return pl.pallas_call(
        kernel,
        out_shape=[
            jax.ShapeDtypeStruct((rows, count), BF16),
            jax.ShapeDtypeStruct((count, states), BF16),
            jax.ShapeDtypeStruct((rows, half), F32),
        ],
        in_specs=[vmem_spec()] * 11,
        out_specs=[vmem_spec()] * 3,
        scratch_shapes=[pltpu.VMEM((rows, half), BF16)],
        compiler_params=params(24),
        name="direct",
    )(proj_own, proj_other, *lines, own, *boxes)


def own_half(weighted, panel):
    rows, count = weighted.shape
    half = panel.shape[1] // 2

    def kernel(weighted_ref, panel_ref, keep_ref):
        mine = pl.ds(pl.multiple_of(lax.axis_index("core") * half, half), half)
        keep_ref[...] = jnp.dot(weighted_ref[...], panel_ref[:, mine], preferred_element_type=F32)

    return pl.pallas_call(
        kernel,
        out_shape=jax.ShapeDtypeStruct((rows, half), F32),
        in_specs=[vmem_spec()] * 2,
        out_specs=vmem_spec(),
        compiler_params=params(16),
        name="own_half",
    )(weighted, panel)


def finish(psi, keep, got):
    states, count = psi.shape
    points = count // 4
    cols = keep.shape[1]

    def kernel(psi_ref, keep_ref, got_ref, out_ref, high, low):
        for k in range(4):
            here = slice(k * points, (k + 1) * points)
            there = slice(SIBLING[k] * points, (SIBLING[k] + 1) * points)
            back = keep_ref[here, :] + got_ref[there, :]
            top = back.astype(BF16)
            high[here, :] = top
            low[here, :] = (back - top.astype(F32)).astype(BF16)
        total = jnp.dot(psi_ref[...], high[...], preferred_element_type=F32)
        total += jnp.dot(psi_ref[...], low[...], preferred_element_type=F32)
        out_ref[...] = total.astype(BF16)

    return pl.pallas_call(
        kernel,
        out_shape=jax.ShapeDtypeStruct((states, cols), BF16),
        in_specs=[vmem_spec()] * 3,
        out_specs=vmem_spec(),
        scratch_shapes=[pltpu.VMEM((count, cols), BF16)] * 2,
        compiler_params=params(16),
        name="finish",
    )(psi, keep, got)


def shards(trial, psi_v, psi_c, screened):
    rows, states = trial.shape[1:]
    half = states // 2
    devices = lax.axis_size(TILE_VEC)
    own, near, far = pack(screened, psi_v)
    block = psi_c[:, 0, :].T
    line = jnp.concatenate([block, shift(block, "x", 1), shift(block, "x", -1), shift(block, "x", 2)], 0)
    halves = trial[0].reshape(rows, 2, half).transpose(1, 0, 2)
    copies = jnp.broadcast_to(halves[None, :, None], (devices // 4, 2, 2, rows, half))
    copies, near, far, line = lax.optimization_barrier((copies, near, far, line))
    trial_half = exchange(copies.reshape(devices, rows, half), TILE_VEC).reshape(-1, half)
    near = swap(near)
    far = lax.ppermute(far, "zh", [(0, 1), (1, 0)])
    behind, ahead = shift(line, "y", 1), shift(line, "y", -1)
    middle = line.shape[0] // 2
    beyond = [shift(behind[:middle], "y", 1), shift(ahead[middle:], "y", -1)]
    far, beyond = lax.optimization_barrier((far, beyond))
    passed = swap(far[1:])
    proj_own, psi = project(trial_half, psi_v, near, far, passed)
    proj_other = swap(proj_own)
    panel = [line, behind, ahead, *beyond]
    weighted, ordered, send = direct(proj_own, proj_other, panel, own, [near, far, passed])
    got = swap(send)
    keep = own_half(weighted, ordered)
    term = finish(psi, keep, got)
    parts = exchange(term.reshape(devices, rows, half), TILE_VEC)
    parts = parts.reshape(-1, 2, 2, rows, half).astype(F32)
    total = jnp.sum(parts, axis=(0, 2))
    return total.transpose(1, 0, 2).reshape(1, rows, states)


def solution(mesh):
    split = Mesh(
        mesh.devices.reshape(2, 4, 4, 2, mesh.shape["vec"]),
        TILE_VEC,
    )
    return jax.shard_map(
        shards,
        mesh=split,
        in_specs=(P(None, TILE_VEC, None), P(None, TILE), P(None, "zl", TILE), P(TILE, "zl")),
        out_specs=P(None, TILE_VEC, None),
        check_vma=False,
    )
```

```python
import jax
import jax.numpy as jnp
from jax import lax
from jax.experimental import pallas as pl
from jax.experimental.pallas import tpu as pltpu
from jax.sharding import Mesh
from jax.sharding import PartitionSpec as P

TILE_VEC = ("zh", "y", "x", "core", "zl")
TILE = ("zh", "y", "x", "core")
STEPS = (0, -1, 1, -2)
F32 = jnp.float32
BF16 = jnp.bfloat16
SIBLING = (1, 0, 3, 2)


def shift(value, axis, by):
    n = lax.axis_size(axis)
    return lax.ppermute(value, axis, [(k, (k + by) % n) for k in range(n)])


def exchange(value, axes):
    return lax.all_to_all(value, axes, split_axis=0, concat_axis=0, tiled=True)


def swap(value):
    return lax.ppermute(value, "core", [(0, 1), (1, 0)])


def vmem_spec():
    return pl.BlockSpec(memory_space=pltpu.VMEM)


def params(mebibytes):
    return pltpu.CompilerParams(vmem_limit_bytes=mebibytes * 1024 * 1024)


def pack(screened, left):
    points, count = screened.shape
    plane, steps = count // 2, 4
    width = plane // 2
    rows = points // steps

    def kernel(in_ref, left_ref, own_ref, near_ref, far_ref):
        core, zh = lax.axis_index("core"), lax.axis_index("zh")
        low = lax.broadcasted_iota(jnp.int32, (rows, 128), 1) < 64
        first = core == 0
        for far in range(2):
            base = plane * (zh if far == 0 else 1 - zh)
            for m in range(width // 128):
                a = in_ref[:, pl.ds(pl.multiple_of(base + m * 256, 256), 128)]
                b = in_ref[:, pl.ds(pl.multiple_of(base + m * 256 + 128, 128), 128)]
                zero = jnp.where(low, a, pltpu.roll(b, 64, 1))
                one = jnp.where(low, pltpu.roll(a, 64, 1), b)
                here = pl.ds(m * 128, 128)
                mine, others = jnp.where(first, zero, one), jnp.where(first, one, zero)
                if far == 0:
                    own_ref[:, here] = mine
                    near_ref[0, :, here] = others.astype(BF16)
                else:
                    far_ref[0, :, here] = mine.astype(BF16)
                    far_ref[1, :, here] = others.astype(BF16)
        for g in range(left_ref.shape[0] // points):
            start = pl.multiple_of(g * points + pl.program_id(0) * rows, rows)
            piece = left_ref[pl.ds(start, rows), :]
            near_ref[1, :, pl.ds(g * points, points)] = piece
            far_ref[2, :, pl.ds(g * points, points)] = piece

    return pl.pallas_call(
        kernel,
        grid=(steps,),
        out_shape=[
            jax.ShapeDtypeStruct((points, width), F32),
            jax.ShapeDtypeStruct((2, points, width), BF16),
            jax.ShapeDtypeStruct((3, points, width), BF16),
        ],
        in_specs=[
            pl.BlockSpec((rows, count), lambda k: (k, 0)),
            pl.BlockSpec(left.shape, lambda k: (0, 0)),
        ],
        out_specs=[
            pl.BlockSpec((rows, width), lambda k: (k, 0)),
            pl.BlockSpec((2, rows, width), lambda k: (0, k, 0)),
            pl.BlockSpec((3, rows, width), lambda k: (0, k, 0)),
        ],
        compiler_params=params(8),
        name="pack",
    )(screened, left)


def project(trial_half, left, near, far, passed):
    states, points = left.shape
    cols = trial_half.shape[1]

    def kernel(trial_ref, left_ref, *refs):
        boxes, (out_ref, psi_ref, sem) = refs[:3], refs[3:]
        load = pltpu.make_async_copy(left_ref, psi_ref.at[:, :points], sem)
        load.start()
        for k in range(1, 4):
            box = boxes[k - 1]
            for g in range(states // points):
                psi_ref[g * points : (g + 1) * points, k * points : (k + 1) * points] = box[
                    box.shape[0] - 1, :, g * points : (g + 1) * points
                ]
        load.wait()
        out_ref[...] = lax.dot_general(
            psi_ref[...], trial_ref[...], (((0,), (0,)), ((), ())), preferred_element_type=F32
        ).astype(BF16)

    return pl.pallas_call(
        kernel,
        out_shape=[
            jax.ShapeDtypeStruct((4 * points, cols), BF16),
            jax.ShapeDtypeStruct((states, 4 * points), BF16),
        ],
        in_specs=[vmem_spec(), pl.BlockSpec(memory_space=pl.ANY)] + [vmem_spec()] * 3,
        out_specs=[vmem_spec()] * 2,
        scratch_shapes=[pltpu.SemaphoreType.DMA],
        compiler_params=params(12),
        name="project",
    )(trial_half, left, near, far, passed)


def direct(proj_own, proj_other, lines, own, boxes):
    rows, half = proj_own.shape
    points = rows // 4
    block = lines[0].shape[0] // 4
    count, states = 16 * block, lines[0].shape[1]
    chunk = 512

    def kernel(own_ref, other_ref, *refs):
        line_refs, scr_refs, (weighted_ref, panel_ref, send_ref, proj) = refs[:5], refs[5:9], refs[9:]
        y, x = lax.axis_index("y"), lax.axis_index("x")
        for k in range(16):
            at = lax.rem(y + STEPS[k // 4] + 4, 4) * 4 + lax.rem(x + STEPS[k % 4] + 4, 4)
            ref, row = (line_refs[k // 4], k % 4) if k < 12 else (line_refs[k // 2 - 3], k % 2)
            panel_ref[pl.ds(pl.multiple_of(at * block, block), block), :] = ref[
                row * block : (row + 1) * block, :
            ]
        core = lax.axis_index("core")
        mine = pl.ds(pl.multiple_of(core * half, half), half)
        sibs = pl.ds(pl.multiple_of((1 - core) * half, half), half)
        for k in range(4):
            proj[k * points : (k + 1) * points, :] = other_ref[
                SIBLING[k] * points : (SIBLING[k] + 1) * points, :
            ]
        nt = (((1,), (1,)), ((), ()))
        for k in range(count // chunk):
            here = pl.ds(k * chunk, chunk)
            pair = lax.dot_general(own_ref[...], panel_ref[here, mine], nt, preferred_element_type=F32)
            pair += lax.dot_general(proj[...], panel_ref[here, sibs], nt, preferred_element_type=F32)
            weighted = jnp.concatenate(
                [
                    (
                        (scr_refs[0][:, here] if j == 0 else scr_refs[j][0, :, here].astype(F32))
                        * pair[j * points : (j + 1) * points]
                    ).astype(BF16)
                    for j in range(4)
                ],
                0,
            )
            weighted_ref[:, here] = weighted
        send_ref[...] = jnp.dot(weighted_ref[...], panel_ref[:, sibs], preferred_element_type=F32)

    return pl.pallas_call(
        kernel,
        out_shape=[
            jax.ShapeDtypeStruct((rows, count), BF16),
            jax.ShapeDtypeStruct((count, states), BF16),
            jax.ShapeDtypeStruct((rows, half), F32),
        ],
        in_specs=[vmem_spec()] * 11,
        out_specs=[vmem_spec()] * 3,
        scratch_shapes=[pltpu.VMEM((rows, half), BF16)],
        compiler_params=params(24),
        name="direct",
    )(proj_own, proj_other, *lines, own, *boxes)


def own_half(weighted, panel):
    rows, count = weighted.shape
    half = panel.shape[1] // 2

    def kernel(weighted_ref, panel_ref, keep_ref):
        mine = pl.ds(pl.multiple_of(lax.axis_index("core") * half, half), half)
        keep_ref[...] = jnp.dot(weighted_ref[...], panel_ref[:, mine], preferred_element_type=F32)

    return pl.pallas_call(
        kernel,
        out_shape=jax.ShapeDtypeStruct((rows, half), F32),
        in_specs=[vmem_spec()] * 2,
        out_specs=vmem_spec(),
        compiler_params=params(16),
        name="own_half",
    )(weighted, panel)


def finish(psi, keep, got):
    states, count = psi.shape
    points = count // 4
    cols = keep.shape[1]

    def kernel(psi_ref, keep_ref, got_ref, out_ref, high, low):
        for k in range(4):
            here = slice(k * points, (k + 1) * points)
            there = slice(SIBLING[k] * points, (SIBLING[k] + 1) * points)
            back = keep_ref[here, :] + got_ref[there, :]
            top = back.astype(BF16)
            high[here, :] = top
            low[here, :] = (back - top.astype(F32)).astype(BF16)
        total = jnp.dot(psi_ref[...], high[...], preferred_element_type=F32)
        total += jnp.dot(psi_ref[...], low[...], preferred_element_type=F32)
        out_ref[...] = total.astype(BF16)

    return pl.pallas_call(
        kernel,
        out_shape=jax.ShapeDtypeStruct((states, cols), BF16),
        in_specs=[vmem_spec()] * 3,
        out_specs=vmem_spec(),
        scratch_shapes=[pltpu.VMEM((count, cols), BF16)] * 2,
        compiler_params=params(16),
        name="finish",
    )(psi, keep, got)


def shards(trial, psi_v, psi_c, screened):
    rows, states = trial.shape[1:]
    half = states // 2
    devices = lax.axis_size(TILE_VEC)
    own, near, far = pack(screened, psi_v)
    block, near, far = lax.optimization_barrier((psi_c[:, 0, :].T, near, far))
    line = jnp.concatenate([block, shift(block, "x", 1), shift(block, "x", -1), shift(block, "x", 2)], 0)
    halves = trial[0].reshape(rows, 2, half).transpose(1, 0, 2)
    copies = jnp.broadcast_to(halves[None, :, None], (devices // 4, 2, 2, rows, half))
    copies, line = lax.optimization_barrier((copies, line))
    trial_half = exchange(copies.reshape(devices, rows, half), TILE_VEC).reshape(-1, half)
    near = swap(near)
    far = lax.ppermute(far, "zh", [(0, 1), (1, 0)])
    behind, ahead = shift(line, "y", 1), shift(line, "y", -1)
    middle = line.shape[0] // 2
    beyond = [shift(behind[:middle], "y", 1), shift(ahead[middle:], "y", -1)]
    far, *_ = lax.optimization_barrier((far, behind, ahead))
    passed = swap(far[1:])
    proj_own, psi = project(trial_half, psi_v, near, far, passed)
    proj_own, beyond = lax.optimization_barrier((proj_own, beyond))
    proj_other = swap(proj_own)
    panel = [line, behind, ahead, *beyond]
    weighted, ordered, send = direct(proj_own, proj_other, panel, own, [near, far, passed])
    got = swap(send)
    keep = own_half(weighted, ordered)
    term = finish(psi, keep, got)
    parts = exchange(term.reshape(devices, rows, half), TILE_VEC)
    parts = parts.reshape(-1, 2, 2, rows, half).astype(F32)
    total = jnp.sum(parts, axis=(0, 2))
    return total.transpose(1, 0, 2).reshape(1, rows, states)


def solution(mesh):
    split = Mesh(
        mesh.devices.reshape(2, 4, 4, 2, mesh.shape["vec"]),
        TILE_VEC,
    )
    return jax.shard_map(
        shards,
        mesh=split,
        in_specs=(P(None, TILE_VEC, None), P(None, TILE), P(None, "zl", TILE), P(TILE, "zl")),
        out_specs=P(None, TILE_VEC, None),
        check_vma=False,
    )
```

```python
import jax
import jax.numpy as jnp
from jax import lax
from jax.experimental import pallas as pl
from jax.experimental.pallas import tpu as pltpu
from jax.sharding import Mesh
from jax.sharding import PartitionSpec as P

TILE_VEC = ("zh", "y", "x", "core", "zl")
TILE = ("zh", "y", "x", "core")
STEPS = (0, -1, 1, -2)
F32 = jnp.float32
BF16 = jnp.bfloat16
SIBLING = (1, 0, 3, 2)


def shift(value, axis, by):
    n = lax.axis_size(axis)
    return lax.ppermute(value, axis, [(k, (k + by) % n) for k in range(n)])


def exchange(value, axes):
    return lax.all_to_all(value, axes, split_axis=0, concat_axis=0, tiled=True)


def swap(value):
    return lax.ppermute(value, "core", [(0, 1), (1, 0)])


def vmem_spec():
    return pl.BlockSpec(memory_space=pltpu.VMEM)


def params(mebibytes):
    return pltpu.CompilerParams(vmem_limit_bytes=mebibytes * 1024 * 1024)


def pack(screened):
    points, count = screened.shape
    plane, steps = count // 2, 4
    width = plane // 2
    rows = points // steps

    def kernel(in_ref, own_ref, near_ref, far_ref):
        core, zh = lax.axis_index("core"), lax.axis_index("zh")
        low = lax.broadcasted_iota(jnp.int32, (rows, 128), 1) < 64
        first = core == 0
        for far in range(2):
            base = plane * (zh if far == 0 else 1 - zh)
            for m in range(width // 128):
                a = in_ref[:, pl.ds(pl.multiple_of(base + m * 256, 256), 128)]
                b = in_ref[:, pl.ds(pl.multiple_of(base + m * 256 + 128, 128), 128)]
                zero = jnp.where(low, a, pltpu.roll(b, 64, 1))
                one = jnp.where(low, pltpu.roll(a, 64, 1), b)
                here = pl.ds(m * 128, 128)
                mine, others = jnp.where(first, zero, one), jnp.where(first, one, zero)
                if far == 0:
                    own_ref[:, here] = mine
                    near_ref[:, here] = others.astype(BF16)
                else:
                    far_ref[0, :, here] = mine.astype(BF16)
                    far_ref[1, :, here] = others.astype(BF16)

    return pl.pallas_call(
        kernel,
        grid=(steps,),
        out_shape=[
            jax.ShapeDtypeStruct((points, width), F32),
            jax.ShapeDtypeStruct((points, width), BF16),
            jax.ShapeDtypeStruct((2, points, width), BF16),
        ],
        in_specs=[pl.BlockSpec((rows, count), lambda k: (k, 0))],
        out_specs=[
            pl.BlockSpec((rows, width), lambda k: (k, 0)),
            pl.BlockSpec((rows, width), lambda k: (k, 0)),
            pl.BlockSpec((2, rows, width), lambda k: (0, k, 0)),
        ],
        compiler_params=params(8),
        name="pack",
    )(screened)


def project(trial_half, psi):
    count, cols = psi.shape[1], trial_half.shape[1]

    def kernel(trial_ref, psi_ref, out_ref):
        out_ref[...] = lax.dot_general(
            psi_ref[...], trial_ref[...], (((0,), (0,)), ((), ())), preferred_element_type=F32
        ).astype(BF16)

    return pl.pallas_call(
        kernel,
        out_shape=jax.ShapeDtypeStruct((count, cols), BF16),
        in_specs=[vmem_spec()] * 2,
        out_specs=vmem_spec(),
        compiler_params=params(12),
        name="project",
    )(trial_half, psi)


def direct(proj_own, proj_other, lines, own, boxes):
    rows, half = proj_own.shape
    points = rows // 4
    block = lines[0].shape[0] // 4
    count, states = 16 * block, lines[0].shape[1]
    chunk = 512

    def kernel(own_ref, other_ref, *refs):
        line_refs, scr_refs, (weighted_ref, panel_ref, send_ref, proj) = refs[:5], refs[5:9], refs[9:]
        y, x = lax.axis_index("y"), lax.axis_index("x")
        for k in range(16):
            at = lax.rem(y + STEPS[k // 4] + 4, 4) * 4 + lax.rem(x + STEPS[k % 4] + 4, 4)
            ref, row = (line_refs[k // 4], k % 4) if k < 12 else (line_refs[k // 2 - 3], k % 2)
            panel_ref[pl.ds(pl.multiple_of(at * block, block), block), :] = ref[
                row * block : (row + 1) * block, :
            ]
        core = lax.axis_index("core")
        mine = pl.ds(pl.multiple_of(core * half, half), half)
        sibs = pl.ds(pl.multiple_of((1 - core) * half, half), half)
        for k in range(4):
            proj[k * points : (k + 1) * points, :] = other_ref[
                SIBLING[k] * points : (SIBLING[k] + 1) * points, :
            ]
        nt = (((1,), (1,)), ((), ()))
        for k in range(count // chunk):
            here = pl.ds(k * chunk, chunk)
            pair = lax.dot_general(own_ref[...], panel_ref[here, mine], nt, preferred_element_type=F32)
            pair += lax.dot_general(proj[...], panel_ref[here, sibs], nt, preferred_element_type=F32)
            weighted = jnp.concatenate(
                [
                    (
                        (scr_refs[j][0, :, here] if j == 2 else scr_refs[j][:, here]).astype(F32)
                        * pair[j * points : (j + 1) * points]
                    ).astype(BF16)
                    for j in range(4)
                ],
                0,
            )
            weighted_ref[:, here] = weighted
        send_ref[...] = jnp.dot(weighted_ref[...], panel_ref[:, sibs], preferred_element_type=F32)

    return pl.pallas_call(
        kernel,
        out_shape=[
            jax.ShapeDtypeStruct((rows, count), BF16),
            jax.ShapeDtypeStruct((count, states), BF16),
            jax.ShapeDtypeStruct((rows, half), F32),
        ],
        in_specs=[vmem_spec()] * 11,
        out_specs=[vmem_spec()] * 3,
        scratch_shapes=[pltpu.VMEM((rows, half), BF16)],
        compiler_params=params(24),
        name="direct",
    )(proj_own, proj_other, *lines, own, *boxes)


def own_half(weighted, panel):
    rows, count = weighted.shape
    half = panel.shape[1] // 2

    def kernel(weighted_ref, panel_ref, keep_ref):
        mine = pl.ds(pl.multiple_of(lax.axis_index("core") * half, half), half)
        keep_ref[...] = jnp.dot(weighted_ref[...], panel_ref[:, mine], preferred_element_type=F32)

    return pl.pallas_call(
        kernel,
        out_shape=jax.ShapeDtypeStruct((rows, half), F32),
        in_specs=[vmem_spec()] * 2,
        out_specs=vmem_spec(),
        compiler_params=params(16),
        name="own_half",
    )(weighted, panel)


def finish(psi, keep, got):
    states, count = psi.shape
    points = count // 4
    cols = keep.shape[1]

    def kernel(psi_ref, keep_ref, got_ref, out_ref, high, low):
        for k in range(4):
            here = slice(k * points, (k + 1) * points)
            there = slice(SIBLING[k] * points, (SIBLING[k] + 1) * points)
            back = keep_ref[here, :] + got_ref[there, :]
            top = back.astype(BF16)
            high[here, :] = top
            low[here, :] = (back - top.astype(F32)).astype(BF16)
        total = jnp.dot(psi_ref[...], high[...], preferred_element_type=F32)
        total += jnp.dot(psi_ref[...], low[...], preferred_element_type=F32)
        out_ref[...] = total.astype(BF16)

    return pl.pallas_call(
        kernel,
        out_shape=jax.ShapeDtypeStruct((states, cols), BF16),
        in_specs=[vmem_spec()] * 3,
        out_specs=vmem_spec(),
        scratch_shapes=[pltpu.VMEM((count, cols), BF16)] * 2,
        compiler_params=params(16),
        name="finish",
    )(psi, keep, got)


def shards(trial, psi_v, psi_c, screened):
    rows, states = trial.shape[1:]
    half = states // 2
    devices = lax.axis_size(TILE_VEC)
    partner = lax.ppermute(psi_v, "zh", [(0, 1), (1, 0)])
    own, near, far = pack(screened)
    block = psi_c[:, 0, :].T
    line = jnp.concatenate([block, shift(block, "x", 1), shift(block, "x", -1), shift(block, "x", 2)], 0)
    halves = trial[0].reshape(rows, 2, half).transpose(1, 0, 2)
    copies = jnp.broadcast_to(halves[None, :, None], (devices // 4, 2, 2, rows, half))
    copies, near, far, line, partner = lax.optimization_barrier((copies, near, far, line, partner))
    trial_half = exchange(copies.reshape(devices, rows, half), TILE_VEC).reshape(-1, half)
    far = lax.ppermute(far, "zh", [(0, 1), (1, 0)])
    behind, ahead = shift(line, "y", 1), shift(line, "y", -1)
    middle = line.shape[0] // 2
    beyond = [shift(behind[:middle], "y", 1), shift(ahead[middle:], "y", -1)]
    far, partner = lax.optimization_barrier((far, partner))
    psi = jnp.concatenate([psi_v, swap(psi_v), partner, swap(partner)], 1)
    near, psi, beyond = lax.optimization_barrier((near, psi, beyond))
    near = swap(near)
    trial_half, near = lax.optimization_barrier((trial_half, near))
    passed = swap(far[1])
    proj_own = project(trial_half, psi)
    proj_other = swap(proj_own)
    panel = [line, behind, ahead, *beyond]
    weighted, ordered, send = direct(proj_own, proj_other, panel, own, [near, far, passed])
    got = swap(send)
    keep = own_half(weighted, ordered)
    term = finish(psi, keep, got)
    parts = exchange(term.reshape(devices, rows, half), TILE_VEC)
    parts = parts.reshape(-1, 2, 2, rows, half).astype(F32)
    total = jnp.sum(parts, axis=(0, 2))
    return total.transpose(1, 0, 2).reshape(1, rows, states)


def solution(mesh):
    split = Mesh(
        mesh.devices.reshape(2, 4, 4, 2, mesh.shape["vec"]),
        TILE_VEC,
    )
    return jax.shard_map(
        shards,
        mesh=split,
        in_specs=(P(None, TILE_VEC, None), P(None, TILE), P(None, "zl", TILE), P(TILE, "zl")),
        out_specs=P(None, TILE_VEC, None),
        check_vma=False,
    )
```

```python
import jax
import jax.numpy as jnp
from jax import lax
from jax.experimental import pallas as pl
from jax.experimental.pallas import tpu as pltpu
from jax.sharding import Mesh
from jax.sharding import PartitionSpec as P

TILE_VEC = ("zh", "y", "x", "core", "zl")
TILE = ("zh", "y", "x", "core")
STEPS = (0, -1, 1, -2)
F32 = jnp.float32
BF16 = jnp.bfloat16
SIBLING = (1, 0, 3, 2)


def shift(value, axis, by):
    n = lax.axis_size(axis)
    return lax.ppermute(value, axis, [(k, (k + by) % n) for k in range(n)])


def exchange(value, axes):
    return lax.all_to_all(value, axes, split_axis=0, concat_axis=0, tiled=True)


def swap(value):
    return lax.ppermute(value, "core", [(0, 1), (1, 0)])


def vmem_spec():
    return pl.BlockSpec(memory_space=pltpu.VMEM)


def params(mebibytes):
    return pltpu.CompilerParams(vmem_limit_bytes=mebibytes * 1024 * 1024)


def pack(screened):
    points, count = screened.shape
    plane, steps = count // 2, 4
    width = plane // 2
    rows = points // steps

    def kernel(in_ref, own_ref, near_ref, far_ref):
        core, zh = lax.axis_index("core"), lax.axis_index("zh")
        low = lax.broadcasted_iota(jnp.int32, (rows, 128), 1) < 64
        first = core == 0
        for far in range(2):
            base = plane * (zh if far == 0 else 1 - zh)
            for m in range(width // 128):
                a = in_ref[:, pl.ds(pl.multiple_of(base + m * 256, 256), 128)]
                b = in_ref[:, pl.ds(pl.multiple_of(base + m * 256 + 128, 128), 128)]
                zero = jnp.where(low, a, pltpu.roll(b, 64, 1))
                one = jnp.where(low, pltpu.roll(a, 64, 1), b)
                here = pl.ds(m * 128, 128)
                mine, others = jnp.where(first, zero, one), jnp.where(first, one, zero)
                if far == 0:
                    own_ref[:, here] = mine
                    near_ref[:, here] = others.astype(BF16)
                else:
                    far_ref[0, :, here] = mine.astype(BF16)
                    far_ref[1, :, here] = others.astype(BF16)

    return pl.pallas_call(
        kernel,
        grid=(steps,),
        out_shape=[
            jax.ShapeDtypeStruct((points, width), F32),
            jax.ShapeDtypeStruct((points, width), BF16),
            jax.ShapeDtypeStruct((2, points, width), BF16),
        ],
        in_specs=[pl.BlockSpec((rows, count), lambda k: (k, 0))],
        out_specs=[
            pl.BlockSpec((rows, width), lambda k: (k, 0)),
            pl.BlockSpec((rows, width), lambda k: (k, 0)),
            pl.BlockSpec((2, rows, width), lambda k: (0, k, 0)),
        ],
        compiler_params=params(8),
        name="pack",
    )(screened)


def project(trial_half, psi):
    count, cols = psi.shape[1], trial_half.shape[1]

    def kernel(trial_ref, psi_ref, out_ref):
        out_ref[...] = lax.dot_general(
            psi_ref[...], trial_ref[...], (((0,), (0,)), ((), ())), preferred_element_type=F32
        ).astype(BF16)

    return pl.pallas_call(
        kernel,
        out_shape=jax.ShapeDtypeStruct((count, cols), BF16),
        in_specs=[vmem_spec()] * 2,
        out_specs=vmem_spec(),
        compiler_params=params(12),
        name="project",
    )(trial_half, psi)


def direct(proj_own, proj_other, lines, own, boxes):
    rows, half = proj_own.shape
    points = rows // 4
    block = lines[0].shape[0] // 4
    count, states = 16 * block, lines[0].shape[1]
    chunk = 512

    def kernel(own_ref, other_ref, *refs):
        line_refs, scr_refs, (weighted_ref, panel_ref, send_ref, proj) = refs[:5], refs[5:9], refs[9:]
        y, x = lax.axis_index("y"), lax.axis_index("x")
        for k in range(16):
            at = lax.rem(y + STEPS[k // 4] + 4, 4) * 4 + lax.rem(x + STEPS[k % 4] + 4, 4)
            ref, row = (line_refs[k // 4], k % 4) if k < 12 else (line_refs[k // 2 - 3], k % 2)
            panel_ref[pl.ds(pl.multiple_of(at * block, block), block), :] = ref[
                row * block : (row + 1) * block, :
            ]
        core = lax.axis_index("core")
        mine = pl.ds(pl.multiple_of(core * half, half), half)
        sibs = pl.ds(pl.multiple_of((1 - core) * half, half), half)
        for k in range(4):
            proj[k * points : (k + 1) * points, :] = other_ref[
                SIBLING[k] * points : (SIBLING[k] + 1) * points, :
            ]
        nt = (((1,), (1,)), ((), ()))
        for k in range(count // chunk):
            here = pl.ds(k * chunk, chunk)
            pair = lax.dot_general(own_ref[...], panel_ref[here, mine], nt, preferred_element_type=F32)
            pair += lax.dot_general(proj[...], panel_ref[here, sibs], nt, preferred_element_type=F32)
            weighted = jnp.concatenate(
                [
                    (
                        (scr_refs[j][0, :, here] if j == 2 else scr_refs[j][:, here]).astype(F32)
                        * pair[j * points : (j + 1) * points]
                    ).astype(BF16)
                    for j in range(4)
                ],
                0,
            )
            weighted_ref[:, here] = weighted
        send_ref[...] = jnp.dot(weighted_ref[...], panel_ref[:, sibs], preferred_element_type=F32)

    return pl.pallas_call(
        kernel,
        out_shape=[
            jax.ShapeDtypeStruct((rows, count), BF16),
            jax.ShapeDtypeStruct((count, states), BF16),
            jax.ShapeDtypeStruct((rows, half), F32),
        ],
        in_specs=[vmem_spec()] * 11,
        out_specs=[vmem_spec()] * 3,
        scratch_shapes=[pltpu.VMEM((rows, half), BF16)],
        compiler_params=params(24),
        name="direct",
    )(proj_own, proj_other, *lines, own, *boxes)


def own_half(weighted, panel):
    rows, count = weighted.shape
    half = panel.shape[1] // 2

    def kernel(weighted_ref, panel_ref, keep_ref):
        mine = pl.ds(pl.multiple_of(lax.axis_index("core") * half, half), half)
        keep_ref[...] = jnp.dot(weighted_ref[...], panel_ref[:, mine], preferred_element_type=F32)

    return pl.pallas_call(
        kernel,
        out_shape=jax.ShapeDtypeStruct((rows, half), F32),
        in_specs=[vmem_spec()] * 2,
        out_specs=vmem_spec(),
        compiler_params=params(16),
        name="own_half",
    )(weighted, panel)


def finish(psi, keep, got):
    states, count = psi.shape
    points = count // 4
    cols = keep.shape[1]

    def kernel(psi_ref, keep_ref, got_ref, out_ref, high, low):
        for k in range(4):
            here = slice(k * points, (k + 1) * points)
            there = slice(SIBLING[k] * points, (SIBLING[k] + 1) * points)
            back = keep_ref[here, :] + got_ref[there, :]
            top = back.astype(BF16)
            high[here, :] = top
            low[here, :] = (back - top.astype(F32)).astype(BF16)
        total = jnp.dot(psi_ref[...], high[...], preferred_element_type=F32)
        total += jnp.dot(psi_ref[...], low[...], preferred_element_type=F32)
        out_ref[...] = total.astype(BF16)

    return pl.pallas_call(
        kernel,
        out_shape=jax.ShapeDtypeStruct((states, cols), BF16),
        in_specs=[vmem_spec()] * 3,
        out_specs=vmem_spec(),
        scratch_shapes=[pltpu.VMEM((count, cols), BF16)] * 2,
        compiler_params=params(16),
        name="finish",
    )(psi, keep, got)


def shards(trial, psi_v, psi_c, screened):
    rows, states = trial.shape[1:]
    half = states // 2
    devices = lax.axis_size(TILE_VEC)
    partner = lax.ppermute(psi_v, "zh", [(0, 1), (1, 0)])
    own, near, far = pack(screened)
    block = psi_c[:, 0, :].T
    line = jnp.concatenate([block, shift(block, "x", 1), shift(block, "x", -1), shift(block, "x", 2)], 0)
    halves = trial[0].reshape(rows, 2, half).transpose(1, 0, 2)
    copies = jnp.broadcast_to(halves[None, :, None], (devices // 4, 2, 2, rows, half))
    copies, near, far, line, partner = lax.optimization_barrier((copies, near, far, line, partner))
    trial_half = exchange(copies.reshape(devices, rows, half), TILE_VEC).reshape(-1, half)
    far = lax.ppermute(far, "zh", [(0, 1), (1, 0)])
    behind, ahead = shift(line, "y", 1), shift(line, "y", -1)
    middle = line.shape[0] // 2
    beyond = [shift(behind[:middle], "y", 1), shift(ahead[middle:], "y", -1)]
    far, partner, *_ = lax.optimization_barrier((far, partner, behind, ahead))
    psi = jnp.concatenate([psi_v, swap(psi_v), partner, swap(partner)], 1)
    near, psi = lax.optimization_barrier((near, psi))
    near = swap(near)
    trial_half, near, beyond = lax.optimization_barrier((trial_half, near, beyond))
    passed = swap(far[1])
    proj_own = project(trial_half, psi)
    proj_other = swap(proj_own)
    panel = [line, behind, ahead, *beyond]
    weighted, ordered, send = direct(proj_own, proj_other, panel, own, [near, far, passed])
    got = swap(send)
    keep = own_half(weighted, ordered)
    term = finish(psi, keep, got)
    parts = exchange(term.reshape(devices, rows, half), TILE_VEC)
    parts = parts.reshape(-1, 2, 2, rows, half).astype(F32)
    total = jnp.sum(parts, axis=(0, 2))
    return total.transpose(1, 0, 2).reshape(1, rows, states)


def solution(mesh):
    split = Mesh(
        mesh.devices.reshape(2, 4, 4, 2, mesh.shape["vec"]),
        TILE_VEC,
    )
    return jax.shard_map(
        shards,
        mesh=split,
        in_specs=(P(None, TILE_VEC, None), P(None, TILE), P(None, "zl", TILE), P(TILE, "zl")),
        out_specs=P(None, TILE_VEC, None),
        check_vma=False,
    )
```

```python
import jax
import jax.numpy as jnp
from jax import lax
from jax.experimental import pallas as pl
from jax.experimental.pallas import tpu as pltpu
from jax.sharding import Mesh
from jax.sharding import PartitionSpec as P

TILE_VEC = ("zh", "y", "x", "core", "zl")
TILE = ("zh", "y", "x", "core")
STEPS = (0, -1, 1, -2)
F32 = jnp.float32
BF16 = jnp.bfloat16
SIBLING = (1, 0, 3, 2)


def shift(value, axis, by):
    n = lax.axis_size(axis)
    return lax.ppermute(value, axis, [(k, (k + by) % n) for k in range(n)])


def exchange(value, axes):
    return lax.all_to_all(value, axes, split_axis=0, concat_axis=0, tiled=True)


def swap(value):
    return lax.ppermute(value, "core", [(0, 1), (1, 0)])


def vmem_spec():
    return pl.BlockSpec(memory_space=pltpu.VMEM)


def params(mebibytes):
    return pltpu.CompilerParams(vmem_limit_bytes=mebibytes * 1024 * 1024)


def pack(screened):
    points, count = screened.shape
    plane, steps = count // 2, 4
    width = plane // 2
    rows = points // steps

    def kernel(in_ref, own_ref, near_ref, far_ref):
        core, zh = lax.axis_index("core"), lax.axis_index("zh")
        low = lax.broadcasted_iota(jnp.int32, (rows, 128), 1) < 64
        first = core == 0
        for far in range(2):
            base = plane * (zh if far == 0 else 1 - zh)
            for m in range(width // 128):
                a = in_ref[:, pl.ds(pl.multiple_of(base + m * 256, 256), 128)]
                b = in_ref[:, pl.ds(pl.multiple_of(base + m * 256 + 128, 128), 128)]
                zero = jnp.where(low, a, pltpu.roll(b, 64, 1))
                one = jnp.where(low, pltpu.roll(a, 64, 1), b)
                here = pl.ds(m * 128, 128)
                mine, others = jnp.where(first, zero, one), jnp.where(first, one, zero)
                if far == 0:
                    own_ref[:, here] = mine
                    near_ref[:, here] = others.astype(BF16)
                else:
                    far_ref[0, :, here] = mine.astype(BF16)
                    far_ref[1, :, here] = others.astype(BF16)

    return pl.pallas_call(
        kernel,
        grid=(steps,),
        out_shape=[
            jax.ShapeDtypeStruct((points, width), F32),
            jax.ShapeDtypeStruct((points, width), BF16),
            jax.ShapeDtypeStruct((2, points, width), BF16),
        ],
        in_specs=[pl.BlockSpec((rows, count), lambda k: (k, 0))],
        out_specs=[
            pl.BlockSpec((rows, width), lambda k: (k, 0)),
            pl.BlockSpec((rows, width), lambda k: (k, 0)),
            pl.BlockSpec((2, rows, width), lambda k: (0, k, 0)),
        ],
        compiler_params=params(8),
        name="pack",
    )(screened)


def project(trial_half, psi):
    count, cols = psi.shape[1], trial_half.shape[1]

    def kernel(trial_ref, psi_ref, out_ref):
        out_ref[...] = lax.dot_general(
            psi_ref[...], trial_ref[...], (((0,), (0,)), ((), ())), preferred_element_type=F32
        ).astype(BF16)

    return pl.pallas_call(
        kernel,
        out_shape=jax.ShapeDtypeStruct((count, cols), BF16),
        in_specs=[vmem_spec()] * 2,
        out_specs=vmem_spec(),
        compiler_params=params(12),
        name="project",
    )(trial_half, psi)


def direct(proj_own, proj_other, lines, own, boxes):
    rows, half = proj_own.shape
    points = rows // 4
    block = lines[0].shape[0] // 4
    count, states = 16 * block, lines[0].shape[1]
    chunk = 512

    def kernel(own_ref, other_ref, *refs):
        line_refs, scr_refs, (weighted_ref, panel_ref, send_ref, proj) = refs[:5], refs[5:9], refs[9:]
        y, x = lax.axis_index("y"), lax.axis_index("x")
        for k in range(16):
            at = lax.rem(y + STEPS[k // 4] + 4, 4) * 4 + lax.rem(x + STEPS[k % 4] + 4, 4)
            ref, row = (line_refs[k // 4], k % 4) if k < 12 else (line_refs[k // 2 - 3], k % 2)
            panel_ref[pl.ds(pl.multiple_of(at * block, block), block), :] = ref[
                row * block : (row + 1) * block, :
            ]
        core = lax.axis_index("core")
        mine = pl.ds(pl.multiple_of(core * half, half), half)
        sibs = pl.ds(pl.multiple_of((1 - core) * half, half), half)
        for k in range(4):
            proj[k * points : (k + 1) * points, :] = other_ref[
                SIBLING[k] * points : (SIBLING[k] + 1) * points, :
            ]
        nt = (((1,), (1,)), ((), ()))
        for k in range(count // chunk):
            here = pl.ds(k * chunk, chunk)
            pair = lax.dot_general(own_ref[...], panel_ref[here, mine], nt, preferred_element_type=F32)
            pair += lax.dot_general(proj[...], panel_ref[here, sibs], nt, preferred_element_type=F32)
            weighted = jnp.concatenate(
                [
                    (
                        (scr_refs[j][0, :, here] if j == 2 else scr_refs[j][:, here]).astype(F32)
                        * pair[j * points : (j + 1) * points]
                    ).astype(BF16)
                    for j in range(4)
                ],
                0,
            )
            weighted_ref[:, here] = weighted
        send_ref[...] = jnp.dot(weighted_ref[...], panel_ref[:, sibs], preferred_element_type=F32)

    return pl.pallas_call(
        kernel,
        out_shape=[
            jax.ShapeDtypeStruct((rows, count), BF16),
            jax.ShapeDtypeStruct((count, states), BF16),
            jax.ShapeDtypeStruct((rows, half), F32),
        ],
        in_specs=[vmem_spec()] * 11,
        out_specs=[vmem_spec()] * 3,
        scratch_shapes=[pltpu.VMEM((rows, half), BF16)],
        compiler_params=params(24),
        name="direct",
    )(proj_own, proj_other, *lines, own, *boxes)


def own_half(weighted, panel):
    rows, count = weighted.shape
    half = panel.shape[1] // 2

    def kernel(weighted_ref, panel_ref, keep_ref):
        mine = pl.ds(pl.multiple_of(lax.axis_index("core") * half, half), half)
        keep_ref[...] = jnp.dot(weighted_ref[...], panel_ref[:, mine], preferred_element_type=F32)

    return pl.pallas_call(
        kernel,
        out_shape=jax.ShapeDtypeStruct((rows, half), F32),
        in_specs=[vmem_spec()] * 2,
        out_specs=vmem_spec(),
        compiler_params=params(16),
        name="own_half",
    )(weighted, panel)


def finish(psi, keep, got):
    states, count = psi.shape
    points = count // 4
    cols = keep.shape[1]

    def kernel(psi_ref, keep_ref, got_ref, out_ref, high, low):
        for k in range(4):
            here = slice(k * points, (k + 1) * points)
            there = slice(SIBLING[k] * points, (SIBLING[k] + 1) * points)
            back = keep_ref[here, :] + got_ref[there, :]
            top = back.astype(BF16)
            high[here, :] = top
            low[here, :] = (back - top.astype(F32)).astype(BF16)
        total = jnp.dot(psi_ref[...], high[...], preferred_element_type=F32)
        total += jnp.dot(psi_ref[...], low[...], preferred_element_type=F32)
        out_ref[...] = total.astype(BF16)

    return pl.pallas_call(
        kernel,
        out_shape=jax.ShapeDtypeStruct((states, cols), BF16),
        in_specs=[vmem_spec()] * 3,
        out_specs=vmem_spec(),
        scratch_shapes=[pltpu.VMEM((count, cols), BF16)] * 2,
        compiler_params=params(16),
        name="finish",
    )(psi, keep, got)


def shards(trial, psi_v, psi_c, screened):
    rows, states = trial.shape[1:]
    half = states // 2
    devices = lax.axis_size(TILE_VEC)
    partner = lax.ppermute(psi_v, "zh", [(0, 1), (1, 0)])
    own, near, far = pack(screened)
    block = psi_c[:, 0, :].T
    line = jnp.concatenate([block, shift(block, "x", 1), shift(block, "x", -1), shift(block, "x", 2)], 0)
    halves = trial[0].reshape(rows, 2, half).transpose(1, 0, 2)
    copies = jnp.broadcast_to(halves[None, :, None], (devices // 4, 2, 2, rows, half))
    copies, near, far, line, partner = lax.optimization_barrier((copies, near, far, line, partner))
    trial_half = exchange(copies.reshape(devices, rows, half), TILE_VEC).reshape(-1, half)
    far = lax.ppermute(far, "zh", [(0, 1), (1, 0)])
    behind, ahead = shift(line, "y", 1), shift(line, "y", -1)
    middle = line.shape[0] // 2
    beyond = [shift(behind[:middle], "y", 1), shift(ahead[middle:], "y", -1)]
    far, partner, *_ = lax.optimization_barrier((far, partner, behind, ahead))
    psi = jnp.concatenate([psi_v, swap(psi_v), partner, swap(partner)], 1)
    near, psi = lax.optimization_barrier((near, psi))
    near = swap(near)
    trial_half, near = lax.optimization_barrier((trial_half, near))
    passed = swap(far[1])
    proj_own = project(trial_half, psi)
    proj_own, beyond = lax.optimization_barrier((proj_own, beyond))
    proj_other = swap(proj_own)
    panel = [line, behind, ahead, *beyond]
    weighted, ordered, send = direct(proj_own, proj_other, panel, own, [near, far, passed])
    got = swap(send)
    keep = own_half(weighted, ordered)
    term = finish(psi, keep, got)
    parts = exchange(term.reshape(devices, rows, half), TILE_VEC)
    parts = parts.reshape(-1, 2, 2, rows, half).astype(F32)
    total = jnp.sum(parts, axis=(0, 2))
    return total.transpose(1, 0, 2).reshape(1, rows, states)


def solution(mesh):
    split = Mesh(
        mesh.devices.reshape(2, 4, 4, 2, mesh.shape["vec"]),
        TILE_VEC,
    )
    return jax.shard_map(
        shards,
        mesh=split,
        in_specs=(P(None, TILE_VEC, None), P(None, TILE), P(None, "zl", TILE), P(TILE, "zl")),
        out_specs=P(None, TILE_VEC, None),
        check_vma=False,
    )
```

```python
import jax
import jax.numpy as jnp
from jax import lax
from jax.experimental import pallas as pl
from jax.experimental.pallas import tpu as pltpu
from jax.sharding import Mesh
from jax.sharding import PartitionSpec as P

TILE_VEC = ("zh", "y", "x", "core", "zl")
TILE = ("zh", "y", "x", "core")
ORDER = ("y", "x", "zh", "zl", "core")
STEPS = (0, -1, 1, -2)
F32 = jnp.float32
BF16 = jnp.bfloat16
SIBLING = (1, 0, 3, 2)


def shift(value, axis, by):
    n = lax.axis_size(axis)
    return lax.ppermute(value, axis, [(k, (k + by) % n) for k in range(n)])


def exchange(value, axes):
    return lax.all_to_all(value, axes, split_axis=0, concat_axis=0, tiled=True)


def swap(value):
    return lax.ppermute(value, "core", [(0, 1), (1, 0)])


def vmem_spec():
    return pl.BlockSpec(memory_space=pltpu.VMEM)


def params(mebibytes):
    return pltpu.CompilerParams(vmem_limit_bytes=mebibytes * 1024 * 1024)


def pack(screened, left):
    points, count = screened.shape
    plane, steps = count // 2, 4
    width = plane // 2
    rows = points // steps

    def kernel(in_ref, left_ref, own_ref, near_ref, far_ref):
        core, zh = lax.axis_index("core"), lax.axis_index("zh")
        low = lax.broadcasted_iota(jnp.int32, (rows, 128), 1) < 64
        first = core == 0
        for far in range(2):
            base = plane * (zh if far == 0 else 1 - zh)
            for m in range(width // 128):
                a = in_ref[:, pl.ds(pl.multiple_of(base + m * 256, 256), 128)]
                b = in_ref[:, pl.ds(pl.multiple_of(base + m * 256 + 128, 128), 128)]
                zero = jnp.where(low, a, pltpu.roll(b, 64, 1))
                one = jnp.where(low, pltpu.roll(a, 64, 1), b)
                here = pl.ds(m * 128, 128)
                mine, others = jnp.where(first, zero, one), jnp.where(first, one, zero)
                if far == 0:
                    own_ref[:, here] = mine
                    near_ref[0, :, here] = others.astype(BF16)
                else:
                    far_ref[0, :, here] = mine.astype(BF16)
                    far_ref[1, :, here] = others.astype(BF16)
        for g in range(left_ref.shape[0] // points):
            start = pl.multiple_of(g * points + pl.program_id(0) * rows, rows)
            piece = left_ref[pl.ds(start, rows), :]
            near_ref[1, :, pl.ds(g * points, points)] = piece
            far_ref[2, :, pl.ds(g * points, points)] = piece

    return pl.pallas_call(
        kernel,
        grid=(steps,),
        out_shape=[
            jax.ShapeDtypeStruct((points, width), F32),
            jax.ShapeDtypeStruct((2, points, width), BF16),
            jax.ShapeDtypeStruct((3, points, width), BF16),
        ],
        in_specs=[
            pl.BlockSpec((rows, count), lambda k: (k, 0)),
            pl.BlockSpec(left.shape, lambda k: (0, 0)),
        ],
        out_specs=[
            pl.BlockSpec((rows, width), lambda k: (k, 0)),
            pl.BlockSpec((2, rows, width), lambda k: (0, k, 0)),
            pl.BlockSpec((3, rows, width), lambda k: (0, k, 0)),
        ],
        compiler_params=params(8),
        name="pack",
    )(screened, left)


def project(trial_half, left, near, far, passed):
    states, points = left.shape
    cols = trial_half.shape[1]

    def kernel(trial_ref, left_ref, *refs):
        boxes, (out_ref, psi_ref, sem) = refs[:3], refs[3:]
        load = pltpu.make_async_copy(left_ref, psi_ref.at[:, :points], sem)
        load.start()
        for k in range(1, 4):
            box = boxes[k - 1]
            for g in range(states // points):
                psi_ref[g * points : (g + 1) * points, k * points : (k + 1) * points] = box[
                    box.shape[0] - 1, :, g * points : (g + 1) * points
                ]
        load.wait()
        out_ref[...] = lax.dot_general(
            psi_ref[...], trial_ref[...], (((0,), (0,)), ((), ())), preferred_element_type=F32
        ).astype(BF16)

    return pl.pallas_call(
        kernel,
        out_shape=[
            jax.ShapeDtypeStruct((4 * points, cols), BF16),
            jax.ShapeDtypeStruct((states, 4 * points), BF16),
        ],
        in_specs=[vmem_spec(), pl.BlockSpec(memory_space=pl.ANY)] + [vmem_spec()] * 3,
        out_specs=[vmem_spec()] * 2,
        scratch_shapes=[pltpu.SemaphoreType.DMA],
        compiler_params=params(12),
        name="project",
    )(trial_half, left, near, far, passed)


def direct(proj_own, proj_other, lines, own, boxes):
    rows, half = proj_own.shape
    points = rows // 4
    block = lines[0].shape[0] // 4
    count, states = 16 * block, lines[0].shape[1]
    chunk = 512

    def kernel(own_ref, other_ref, *refs):
        line_refs, scr_refs, (weighted_ref, panel_ref, send_ref, proj) = refs[:5], refs[5:9], refs[9:]
        y, x = lax.axis_index("y"), lax.axis_index("x")
        for k in range(16):
            at = lax.rem(y + STEPS[k // 4] + 4, 4) * 4 + lax.rem(x + STEPS[k % 4] + 4, 4)
            ref, row = (line_refs[k // 4], k % 4) if k < 12 else (line_refs[k // 2 - 3], k % 2)
            panel_ref[pl.ds(pl.multiple_of(at * block, block), block), :] = ref[
                row * block : (row + 1) * block, :
            ]
        core = lax.axis_index("core")
        mine = pl.ds(pl.multiple_of(core * half, half), half)
        sibs = pl.ds(pl.multiple_of((1 - core) * half, half), half)
        for k in range(4):
            proj[k * points : (k + 1) * points, :] = other_ref[
                SIBLING[k] * points : (SIBLING[k] + 1) * points, :
            ]
        nt = (((1,), (1,)), ((), ()))
        for k in range(count // chunk):
            here = pl.ds(k * chunk, chunk)
            pair = lax.dot_general(own_ref[...], panel_ref[here, mine], nt, preferred_element_type=F32)
            pair += lax.dot_general(proj[...], panel_ref[here, sibs], nt, preferred_element_type=F32)
            weighted = jnp.concatenate(
                [
                    (
                        (scr_refs[0][:, here] if j == 0 else scr_refs[j][0, :, here].astype(F32))
                        * pair[j * points : (j + 1) * points]
                    ).astype(BF16)
                    for j in range(4)
                ],
                0,
            )
            weighted_ref[:, here] = weighted
        send_ref[...] = jnp.dot(weighted_ref[...], panel_ref[:, sibs], preferred_element_type=F32)

    return pl.pallas_call(
        kernel,
        out_shape=[
            jax.ShapeDtypeStruct((rows, count), BF16),
            jax.ShapeDtypeStruct((count, states), BF16),
            jax.ShapeDtypeStruct((rows, half), F32),
        ],
        in_specs=[vmem_spec()] * 11,
        out_specs=[vmem_spec()] * 3,
        scratch_shapes=[pltpu.VMEM((rows, half), BF16)],
        compiler_params=params(24),
        name="direct",
    )(proj_own, proj_other, *lines, own, *boxes)


def own_half(weighted, panel):
    rows, count = weighted.shape
    half = panel.shape[1] // 2

    def kernel(weighted_ref, panel_ref, keep_ref):
        mine = pl.ds(pl.multiple_of(lax.axis_index("core") * half, half), half)
        keep_ref[...] = jnp.dot(weighted_ref[...], panel_ref[:, mine], preferred_element_type=F32)

    return pl.pallas_call(
        kernel,
        out_shape=jax.ShapeDtypeStruct((rows, half), F32),
        in_specs=[vmem_spec()] * 2,
        out_specs=vmem_spec(),
        compiler_params=params(16),
        name="own_half",
    )(weighted, panel)


def finish(psi, keep, got):
    states, count = psi.shape
    points = count // 4
    cols = keep.shape[1]

    def kernel(psi_ref, keep_ref, got_ref, out_ref, high, low):
        for k in range(4):
            here = slice(k * points, (k + 1) * points)
            there = slice(SIBLING[k] * points, (SIBLING[k] + 1) * points)
            back = keep_ref[here, :] + got_ref[there, :]
            top = back.astype(BF16)
            high[here, :] = top
            low[here, :] = (back - top.astype(F32)).astype(BF16)
        total = jnp.dot(psi_ref[...], high[...], preferred_element_type=F32)
        total += jnp.dot(psi_ref[...], low[...], preferred_element_type=F32)
        out_ref[...] = total.astype(BF16)

    return pl.pallas_call(
        kernel,
        out_shape=jax.ShapeDtypeStruct((states, cols), BF16),
        in_specs=[vmem_spec()] * 3,
        out_specs=vmem_spec(),
        scratch_shapes=[pltpu.VMEM((count, cols), BF16)] * 2,
        compiler_params=params(16),
        name="finish",
    )(psi, keep, got)


def shards(trial, psi_v, psi_c, screened):
    rows, states = trial.shape[1:]
    half = states // 2
    devices = lax.axis_size(TILE_VEC)
    left = psi_v.reshape(2, 4, 4, 2, 2, rows, -1).transpose(1, 2, 0, 4, 3, 5, 6).reshape(psi_v.shape)
    own, near, far = pack(screened, left)
    block = psi_c[:, 0, :].T
    line = jnp.concatenate([block, shift(block, "x", 1), shift(block, "x", -1), shift(block, "x", 2)], 0)
    halves = trial[0].reshape(rows, 2, half).transpose(1, 0, 2)
    copies = jnp.broadcast_to(halves[None], (devices // 2, 2, rows, half))
    copies, near, far, line = lax.optimization_barrier((copies, near, far, line))
    trial_half = exchange(copies.reshape(devices, rows, half), ORDER).reshape(-1, half)
    near = swap(near)
    far = lax.ppermute(far, "zh", [(0, 1), (1, 0)])
    behind, ahead = shift(line, "y", 1), shift(line, "y", -1)
    middle = line.shape[0] // 2
    beyond = [shift(behind[:middle], "y", 1), shift(ahead[middle:], "y", -1)]
    far, beyond = lax.optimization_barrier((far, beyond))
    passed = swap(far[1:])
    proj_own, psi = project(trial_half, left, near, far, passed)
    proj_other = swap(proj_own)
    panel = [line, behind, ahead, *beyond]
    weighted, ordered, send = direct(proj_own, proj_other, panel, own, [near, far, passed])
    got = swap(send)
    keep = own_half(weighted, ordered)
    term = finish(psi, keep, got)
    parts = exchange(term.reshape(devices, rows, half), ORDER)
    parts = parts.reshape(-1, 2, rows, half).astype(F32)
    total = jnp.sum(parts, axis=0)
    return total.transpose(1, 0, 2).reshape(1, rows, states)


def solution(mesh):
    split = Mesh(
        mesh.devices.reshape(2, 4, 4, 2, mesh.shape["vec"]),
        TILE_VEC,
    )
    return jax.shard_map(
        shards,
        mesh=split,
        in_specs=(P(None, TILE_VEC, None), P(None, TILE), P(None, "zl", TILE), P(TILE, "zl")),
        out_specs=P(None, TILE_VEC, None),
        check_vma=False,
    )
```

```python
import jax
import jax.numpy as jnp
from jax import lax
from jax.experimental import pallas as pl
from jax.experimental.pallas import tpu as pltpu
from jax.sharding import Mesh
from jax.sharding import PartitionSpec as P

TILE_VEC = ("zh", "y", "x", "core", "zl")
TILE = ("zh", "y", "x", "core")
STEPS = (0, -1, 1, -2)
F32 = jnp.float32
BF16 = jnp.bfloat16
SIBLING = (1, 0, 3, 2)


def shift(value, axis, by):
    n = lax.axis_size(axis)
    return lax.ppermute(value, axis, [(k, (k + by) % n) for k in range(n)])


def exchange(value, axes):
    return lax.all_to_all(value, axes, split_axis=0, concat_axis=0, tiled=True)


def swap(value):
    return lax.ppermute(value, "core", [(0, 1), (1, 0)])


def vmem_spec():
    return pl.BlockSpec(memory_space=pltpu.VMEM)


def params(mebibytes):
    return pltpu.CompilerParams(vmem_limit_bytes=mebibytes * 1024 * 1024)


def pack(screened, left):
    points, count = screened.shape
    plane, steps = count // 2, 4
    width = plane // 2
    rows = points // steps

    def kernel(in_ref, left_ref, own_ref, near_ref, far_ref):
        core, zh = lax.axis_index("core"), lax.axis_index("zh")
        low = lax.broadcasted_iota(jnp.int32, (rows, 128), 1) < 64
        first = core == 0
        for far in range(2):
            base = plane * (zh if far == 0 else 1 - zh)
            for m in range(width // 128):
                a = in_ref[:, pl.ds(pl.multiple_of(base + m * 256, 256), 128)]
                b = in_ref[:, pl.ds(pl.multiple_of(base + m * 256 + 128, 128), 128)]
                zero = jnp.where(low, a, pltpu.roll(b, 64, 1))
                one = jnp.where(low, pltpu.roll(a, 64, 1), b)
                here = pl.ds(m * 128, 128)
                mine, others = jnp.where(first, zero, one), jnp.where(first, one, zero)
                if far == 0:
                    own_ref[:, here] = mine
                    near_ref[0, :, here] = others.astype(BF16)
                else:
                    far_ref[0, :, here] = mine.astype(BF16)
                    far_ref[1, :, here] = others.astype(BF16)
        for g in range(left_ref.shape[0] // points):
            start = pl.multiple_of(g * points + pl.program_id(0) * rows, rows)
            piece = left_ref[pl.ds(start, rows), :]
            near_ref[1, :, pl.ds(g * points, points)] = piece
            far_ref[2, :, pl.ds(g * points, points)] = piece

    return pl.pallas_call(
        kernel,
        grid=(steps,),
        out_shape=[
            jax.ShapeDtypeStruct((points, width), F32),
            jax.ShapeDtypeStruct((2, points, width), BF16),
            jax.ShapeDtypeStruct((3, points, width), BF16),
        ],
        in_specs=[
            pl.BlockSpec((rows, count), lambda k: (k, 0)),
            pl.BlockSpec(left.shape, lambda k: (0, 0)),
        ],
        out_specs=[
            pl.BlockSpec((rows, width), lambda k: (k, 0)),
            pl.BlockSpec((2, rows, width), lambda k: (0, k, 0)),
            pl.BlockSpec((3, rows, width), lambda k: (0, k, 0)),
        ],
        compiler_params=params(8),
        name="pack",
    )(screened, left)


def project(trial_half, left, near, far, passed):
    states, points = left.shape
    cols = trial_half.shape[1]

    def kernel(trial_ref, left_ref, *refs):
        boxes, (out_ref, psi_ref, sem) = refs[:3], refs[3:]
        load = pltpu.make_async_copy(left_ref, psi_ref.at[:, :points], sem)
        load.start()
        for k in range(1, 4):
            box = boxes[k - 1]
            for g in range(states // points):
                psi_ref[g * points : (g + 1) * points, k * points : (k + 1) * points] = box[
                    box.shape[0] - 1, :, g * points : (g + 1) * points
                ]
        load.wait()
        out_ref[...] = lax.dot_general(
            psi_ref[...], trial_ref[...], (((0,), (0,)), ((), ())), preferred_element_type=F32
        ).astype(BF16)

    return pl.pallas_call(
        kernel,
        out_shape=[
            jax.ShapeDtypeStruct((4 * points, cols), BF16),
            jax.ShapeDtypeStruct((states, 4 * points), BF16),
        ],
        in_specs=[vmem_spec(), pl.BlockSpec(memory_space=pl.ANY)] + [vmem_spec()] * 3,
        out_specs=[vmem_spec()] * 2,
        scratch_shapes=[pltpu.SemaphoreType.DMA],
        compiler_params=params(12),
        name="project",
    )(trial_half, left, near, far, passed)


def direct(proj_own, proj_other, lines, own, boxes):
    rows, half = proj_own.shape
    points = rows // 4
    block = lines[0].shape[0] // 4
    count, states = 16 * block, lines[0].shape[1]
    chunk = 512

    def kernel(own_ref, other_ref, *refs):
        line_refs, scr_refs, (weighted_ref, panel_ref, send_ref, proj) = refs[:5], refs[5:9], refs[9:]
        y, x = lax.axis_index("y"), lax.axis_index("x")
        for k in range(16):
            at = lax.rem(y + STEPS[k // 4] + 4, 4) * 4 + lax.rem(x + STEPS[k % 4] + 4, 4)
            ref, row = (line_refs[k // 4], k % 4) if k < 12 else (line_refs[k // 2 - 3], k % 2)
            panel_ref[pl.ds(pl.multiple_of(at * block, block), block), :] = ref[
                row * block : (row + 1) * block, :
            ]
        core = lax.axis_index("core")
        mine = pl.ds(pl.multiple_of(core * half, half), half)
        sibs = pl.ds(pl.multiple_of((1 - core) * half, half), half)
        for k in range(4):
            proj[k * points : (k + 1) * points, :] = other_ref[
                SIBLING[k] * points : (SIBLING[k] + 1) * points, :
            ]
        nt = (((1,), (1,)), ((), ()))
        for k in range(count // chunk):
            here = pl.ds(k * chunk, chunk)
            pair = lax.dot_general(own_ref[...], panel_ref[here, mine], nt, preferred_element_type=F32)
            pair += lax.dot_general(proj[...], panel_ref[here, sibs], nt, preferred_element_type=F32)
            weighted = jnp.concatenate(
                [
                    (
                        (scr_refs[0][:, here] if j == 0 else scr_refs[j][0, :, here].astype(F32))
                        * pair[j * points : (j + 1) * points]
                    ).astype(BF16)
                    for j in range(4)
                ],
                0,
            )
            weighted_ref[:, here] = weighted
        send = jnp.dot(weighted_ref[...], panel_ref[:, sibs], preferred_element_type=F32)
        send_ref[...] = send.astype(BF16)

    return pl.pallas_call(
        kernel,
        out_shape=[
            jax.ShapeDtypeStruct((rows, count), BF16),
            jax.ShapeDtypeStruct((count, states), BF16),
            jax.ShapeDtypeStruct((rows, half), BF16),
        ],
        in_specs=[vmem_spec()] * 11,
        out_specs=[vmem_spec()] * 3,
        scratch_shapes=[pltpu.VMEM((rows, half), BF16)],
        compiler_params=params(24),
        name="direct",
    )(proj_own, proj_other, *lines, own, *boxes)


def own_half(weighted, panel):
    rows, count = weighted.shape
    half = panel.shape[1] // 2

    def kernel(weighted_ref, panel_ref, keep_ref):
        mine = pl.ds(pl.multiple_of(lax.axis_index("core") * half, half), half)
        keep_ref[...] = jnp.dot(weighted_ref[...], panel_ref[:, mine], preferred_element_type=F32)

    return pl.pallas_call(
        kernel,
        out_shape=jax.ShapeDtypeStruct((rows, half), F32),
        in_specs=[vmem_spec()] * 2,
        out_specs=vmem_spec(),
        compiler_params=params(16),
        name="own_half",
    )(weighted, panel)


def finish(psi, keep, got):
    states, count = psi.shape
    points = count // 4
    cols = keep.shape[1]

    def kernel(psi_ref, keep_ref, got_ref, out_ref, high, low):
        for k in range(4):
            here = slice(k * points, (k + 1) * points)
            there = slice(SIBLING[k] * points, (SIBLING[k] + 1) * points)
            back = keep_ref[here, :] + got_ref[there, :].astype(F32)
            top = back.astype(BF16)
            high[here, :] = top
            low[here, :] = (back - top.astype(F32)).astype(BF16)
        total = jnp.dot(psi_ref[...], high[...], preferred_element_type=F32)
        total += jnp.dot(psi_ref[...], low[...], preferred_element_type=F32)
        out_ref[...] = total.astype(BF16)

    return pl.pallas_call(
        kernel,
        out_shape=jax.ShapeDtypeStruct((states, cols), BF16),
        in_specs=[vmem_spec()] * 3,
        out_specs=vmem_spec(),
        scratch_shapes=[pltpu.VMEM((count, cols), BF16)] * 2,
        compiler_params=params(16),
        name="finish",
    )(psi, keep, got)


def shards(trial, psi_v, psi_c, screened):
    rows, states = trial.shape[1:]
    half = states // 2
    devices = lax.axis_size(TILE_VEC)
    own, near, far = pack(screened, psi_v)
    block = psi_c[:, 0, :].T
    line = jnp.concatenate([block, shift(block, "x", 1), shift(block, "x", -1), shift(block, "x", 2)], 0)
    halves = trial[0].reshape(rows, 2, half).transpose(1, 0, 2)
    copies = jnp.broadcast_to(halves[None, :, None], (devices // 4, 2, 2, rows, half))
    copies, near, far, line = lax.optimization_barrier((copies, near, far, line))
    trial_half = exchange(copies.reshape(devices, rows, half), TILE_VEC).reshape(-1, half)
    near = swap(near)
    far = lax.ppermute(far, "zh", [(0, 1), (1, 0)])
    behind, ahead = shift(line, "y", 1), shift(line, "y", -1)
    middle = line.shape[0] // 2
    beyond = [shift(behind[:middle], "y", 1), shift(ahead[middle:], "y", -1)]
    far, beyond = lax.optimization_barrier((far, beyond))
    passed = swap(far[1:])
    proj_own, psi = project(trial_half, psi_v, near, far, passed)
    proj_other = swap(proj_own)
    panel = [line, behind, ahead, *beyond]
    weighted, ordered, send = direct(proj_own, proj_other, panel, own, [near, far, passed])
    got = swap(send)
    keep = own_half(weighted, ordered)
    term = finish(psi, keep, got)
    parts = exchange(term.reshape(devices, rows, half), TILE_VEC)
    parts = parts.reshape(-1, 2, 2, rows, half).astype(F32)
    total = jnp.sum(parts, axis=(0, 2))
    return total.transpose(1, 0, 2).reshape(1, rows, states)


def solution(mesh):
    split = Mesh(
        mesh.devices.reshape(2, 4, 4, 2, mesh.shape["vec"]),
        TILE_VEC,
    )
    return jax.shard_map(
        shards,
        mesh=split,
        in_specs=(P(None, TILE_VEC, None), P(None, TILE), P(None, "zl", TILE), P(TILE, "zl")),
        out_specs=P(None, TILE_VEC, None),
        check_vma=False,
    )
```

```python
import jax
import jax.numpy as jnp
from jax import lax
from jax.experimental import pallas as pl
from jax.experimental.pallas import tpu as pltpu
from jax.sharding import Mesh
from jax.sharding import PartitionSpec as P

TILE_VEC = ("zh", "y", "x", "core", "zl")
TILE = ("zh", "y", "x", "core")
STEPS = (0, -1, 1, -2)
F32 = jnp.float32
BF16 = jnp.bfloat16
SIBLING = (1, 0, 3, 2)


def shift(value, axis, by):
    n = lax.axis_size(axis)
    return lax.ppermute(value, axis, [(k, (k + by) % n) for k in range(n)])


def exchange(value, axes):
    return lax.all_to_all(value, axes, split_axis=0, concat_axis=0, tiled=True)


def swap(value):
    return lax.ppermute(value, "core", [(0, 1), (1, 0)])


def vmem_spec():
    return pl.BlockSpec(memory_space=pltpu.VMEM)


def params(mebibytes):
    return pltpu.CompilerParams(vmem_limit_bytes=mebibytes * 1024 * 1024)


def pack(screened, left):
    points, count = screened.shape
    plane, steps = count // 2, 4
    width = plane // 2
    rows = points // steps

    def kernel(in_ref, left_ref, own_ref, near_ref, far_ref):
        core, zh = lax.axis_index("core"), lax.axis_index("zh")
        low = lax.broadcasted_iota(jnp.int32, (rows, 128), 1) < 64
        first = core == 0
        for far in range(2):
            base = plane * (zh if far == 0 else 1 - zh)
            for m in range(width // 128):
                a = in_ref[:, pl.ds(pl.multiple_of(base + m * 256, 256), 128)]
                b = in_ref[:, pl.ds(pl.multiple_of(base + m * 256 + 128, 128), 128)]
                zero = jnp.where(low, a, pltpu.roll(b, 64, 1))
                one = jnp.where(low, pltpu.roll(a, 64, 1), b)
                here = pl.ds(m * 128, 128)
                mine, others = jnp.where(first, zero, one), jnp.where(first, one, zero)
                if far == 0:
                    own_ref[:, here] = mine
                    near_ref[0, :, here] = others.astype(BF16)
                else:
                    far_ref[0, :, here] = mine.astype(BF16)
                    far_ref[1, :, here] = others.astype(BF16)
        for g in range(left_ref.shape[0] // points):
            start = pl.multiple_of(g * points + pl.program_id(0) * rows, rows)
            piece = left_ref[pl.ds(start, rows), :]
            near_ref[1, :, pl.ds(g * points, points)] = piece
            far_ref[2, :, pl.ds(g * points, points)] = piece

    return pl.pallas_call(
        kernel,
        grid=(steps,),
        out_shape=[
            jax.ShapeDtypeStruct((points, width), F32),
            jax.ShapeDtypeStruct((2, points, width), BF16),
            jax.ShapeDtypeStruct((3, points, width), BF16),
        ],
        in_specs=[
            pl.BlockSpec((rows, count), lambda k: (k, 0)),
            pl.BlockSpec(left.shape, lambda k: (0, 0)),
        ],
        out_specs=[
            pl.BlockSpec((rows, width), lambda k: (k, 0)),
            pl.BlockSpec((2, rows, width), lambda k: (0, k, 0)),
            pl.BlockSpec((3, rows, width), lambda k: (0, k, 0)),
        ],
        compiler_params=params(8),
        name="pack",
    )(screened, left)


def project(trial_half, left, near, far, passed):
    states, points = left.shape
    cols = trial_half.shape[1]

    def kernel(trial_ref, left_ref, *refs):
        boxes, (out_ref, psi_ref, sem) = refs[:3], refs[3:]
        load = pltpu.make_async_copy(left_ref, psi_ref.at[:, :points], sem)
        load.start()
        for k in range(1, 4):
            box = boxes[k - 1]
            for g in range(states // points):
                psi_ref[g * points : (g + 1) * points, k * points : (k + 1) * points] = box[
                    box.shape[0] - 1, :, g * points : (g + 1) * points
                ]
        load.wait()
        out_ref[...] = lax.dot_general(
            psi_ref[...], trial_ref[...], (((0,), (0,)), ((), ())), preferred_element_type=F32
        ).astype(BF16)

    return pl.pallas_call(
        kernel,
        out_shape=[
            jax.ShapeDtypeStruct((4 * points, cols), BF16),
            jax.ShapeDtypeStruct((states, 4 * points), BF16),
        ],
        in_specs=[vmem_spec(), pl.BlockSpec(memory_space=pl.ANY)] + [vmem_spec()] * 3,
        out_specs=[vmem_spec()] * 2,
        scratch_shapes=[pltpu.SemaphoreType.DMA],
        compiler_params=params(12),
        name="project",
    )(trial_half, left, near, far, passed)


NT = (((1,), (1,)), ((), ()))


def own_pairs(proj_own, lines):
    rows, half = proj_own.shape
    block = lines[0].shape[0] // 4
    count, states = 16 * block, lines[0].shape[1]

    def kernel(own_ref, *refs):
        line_refs, (panel_ref, pair_ref) = refs[:5], refs[5:]
        y, x = lax.axis_index("y"), lax.axis_index("x")
        for k in range(16):
            at = lax.rem(y + STEPS[k // 4] + 4, 4) * 4 + lax.rem(x + STEPS[k % 4] + 4, 4)
            ref, row = (line_refs[k // 4], k % 4) if k < 12 else (line_refs[k // 2 - 3], k % 2)
            panel_ref[pl.ds(pl.multiple_of(at * block, block), block), :] = ref[
                row * block : (row + 1) * block, :
            ]
        mine = pl.ds(pl.multiple_of(lax.axis_index("core") * half, half), half)
        pair_ref[...] = lax.dot_general(own_ref[...], panel_ref[:, mine], NT, preferred_element_type=F32)

    return pl.pallas_call(
        kernel,
        out_shape=[
            jax.ShapeDtypeStruct((count, states), BF16),
            jax.ShapeDtypeStruct((rows, count), F32),
        ],
        in_specs=[vmem_spec()] * 6,
        out_specs=[vmem_spec()] * 2,
        compiler_params=params(16),
        name="own_pairs",
    )(proj_own, *lines)


def direct(proj_other, panel, pairs, own, boxes):
    rows, half = proj_other.shape
    points = rows // 4
    count = panel.shape[0]
    chunk = 512

    def kernel(other_ref, panel_ref, pair_ref, *refs):
        scr_refs, (weighted_ref, send_ref, proj) = refs[:4], refs[4:]
        core = lax.axis_index("core")
        sibs = pl.ds(pl.multiple_of((1 - core) * half, half), half)
        for k in range(4):
            proj[k * points : (k + 1) * points, :] = other_ref[
                SIBLING[k] * points : (SIBLING[k] + 1) * points, :
            ]
        for k in range(count // chunk):
            here = pl.ds(k * chunk, chunk)
            pair = pair_ref[:, here] + lax.dot_general(
                proj[...], panel_ref[here, sibs], NT, preferred_element_type=F32
            )
            for j in range(4):
                mine = slice(j * points, (j + 1) * points)
                weights = scr_refs[j][:, here] if j == 0 else scr_refs[j][0, :, here].astype(F32)
                weighted_ref[mine, here] = (weights * pair[mine]).astype(BF16)
        send = jnp.dot(weighted_ref[...], panel_ref[:, sibs], preferred_element_type=F32)
        send_ref[...] = send.astype(BF16)

    return pl.pallas_call(
        kernel,
        out_shape=[
            jax.ShapeDtypeStruct((rows, count), BF16),
            jax.ShapeDtypeStruct((rows, half), BF16),
        ],
        in_specs=[vmem_spec()] * 7,
        out_specs=[vmem_spec()] * 2,
        scratch_shapes=[pltpu.VMEM((rows, half), BF16)],
        compiler_params=params(24),
        name="direct",
    )(proj_other, panel, pairs, own, *boxes)


def own_half(weighted, panel):
    rows, count = weighted.shape
    half = panel.shape[1] // 2

    def kernel(weighted_ref, panel_ref, keep_ref):
        mine = pl.ds(pl.multiple_of(lax.axis_index("core") * half, half), half)
        keep_ref[...] = jnp.dot(weighted_ref[...], panel_ref[:, mine], preferred_element_type=F32)

    return pl.pallas_call(
        kernel,
        out_shape=jax.ShapeDtypeStruct((rows, half), F32),
        in_specs=[vmem_spec()] * 2,
        out_specs=vmem_spec(),
        compiler_params=params(16),
        name="own_half",
    )(weighted, panel)


def finish(psi, keep, got):
    states, count = psi.shape
    points = count // 4
    cols = keep.shape[1]

    def kernel(psi_ref, keep_ref, got_ref, out_ref, high, low):
        for k in range(4):
            here = slice(k * points, (k + 1) * points)
            there = slice(SIBLING[k] * points, (SIBLING[k] + 1) * points)
            back = keep_ref[here, :] + got_ref[there, :].astype(F32)
            top = back.astype(BF16)
            high[here, :] = top
            low[here, :] = (back - top.astype(F32)).astype(BF16)
        total = jnp.dot(psi_ref[...], high[...], preferred_element_type=F32)
        total += jnp.dot(psi_ref[...], low[...], preferred_element_type=F32)
        out_ref[...] = total.astype(BF16)

    return pl.pallas_call(
        kernel,
        out_shape=jax.ShapeDtypeStruct((states, cols), BF16),
        in_specs=[vmem_spec()] * 3,
        out_specs=vmem_spec(),
        scratch_shapes=[pltpu.VMEM((count, cols), BF16)] * 2,
        compiler_params=params(16),
        name="finish",
    )(psi, keep, got)


def shards(trial, psi_v, psi_c, screened):
    rows, states = trial.shape[1:]
    half = states // 2
    devices = lax.axis_size(TILE_VEC)
    own, near, far = pack(screened, psi_v)
    block = psi_c[:, 0, :].T
    line = jnp.concatenate([block, shift(block, "x", 1), shift(block, "x", -1), shift(block, "x", 2)], 0)
    halves = trial[0].reshape(rows, 2, half).transpose(1, 0, 2)
    copies = jnp.broadcast_to(halves[None, :, None], (devices // 4, 2, 2, rows, half))
    copies, near, far, line = lax.optimization_barrier((copies, near, far, line))
    trial_half = exchange(copies.reshape(devices, rows, half), TILE_VEC).reshape(-1, half)
    near = swap(near)
    far = lax.ppermute(far, "zh", [(0, 1), (1, 0)])
    behind, ahead = shift(line, "y", 1), shift(line, "y", -1)
    middle = line.shape[0] // 2
    beyond = [shift(behind[:middle], "y", 1), shift(ahead[middle:], "y", -1)]
    far, beyond = lax.optimization_barrier((far, beyond))
    passed = swap(far[1:])
    proj_own, psi = project(trial_half, psi_v, near, far, passed)
    proj_other = swap(proj_own)
    panel = [line, behind, ahead, *beyond]
    ordered, pairs = own_pairs(proj_own, panel)
    weighted, send = direct(proj_other, ordered, pairs, own, [near, far, passed])
    got = swap(send)
    keep = own_half(weighted, ordered)
    term = finish(psi, keep, got)
    parts = exchange(term.reshape(devices, rows, half), TILE_VEC)
    parts = parts.reshape(-1, 2, 2, rows, half).astype(F32)
    total = jnp.sum(parts, axis=(0, 2))
    return total.transpose(1, 0, 2).reshape(1, rows, states)


def solution(mesh):
    split = Mesh(
        mesh.devices.reshape(2, 4, 4, 2, mesh.shape["vec"]),
        TILE_VEC,
    )
    return jax.shard_map(
        shards,
        mesh=split,
        in_specs=(P(None, TILE_VEC, None), P(None, TILE), P(None, "zl", TILE), P(TILE, "zl")),
        out_specs=P(None, TILE_VEC, None),
        check_vma=False,
    )
```

```python
import jax
import jax.numpy as jnp
from jax import lax
from jax.experimental import pallas as pl
from jax.experimental.pallas import tpu as pltpu
from jax.sharding import Mesh
from jax.sharding import PartitionSpec as P

TILE_VEC = ("zh", "y", "x", "core", "zl")
TILE = ("zh", "y", "x", "core")
STEPS = (0, -1, 1, -2)
F32 = jnp.float32
BF16 = jnp.bfloat16
SIBLING = (1, 0, 3, 2)


def shift(value, axis, by):
    n = lax.axis_size(axis)
    return lax.ppermute(value, axis, [(k, (k + by) % n) for k in range(n)])


def exchange(value, axes):
    return lax.all_to_all(value, axes, split_axis=0, concat_axis=0, tiled=True)


def swap(value):
    return lax.ppermute(value, "core", [(0, 1), (1, 0)])


def vmem_spec():
    return pl.BlockSpec(memory_space=pltpu.VMEM)


def params(mebibytes):
    return pltpu.CompilerParams(vmem_limit_bytes=mebibytes * 1024 * 1024)


def pack(screened, left):
    points, count = screened.shape
    plane, steps = count // 2, 4
    width = plane // 2
    rows = points // steps

    def kernel(in_ref, left_ref, own_ref, near_ref, far_ref):
        core, zh = lax.axis_index("core"), lax.axis_index("zh")
        low = lax.broadcasted_iota(jnp.int32, (rows, 128), 1) < 64
        first = core == 0
        for far in range(2):
            base = plane * (zh if far == 0 else 1 - zh)
            for m in range(width // 128):
                a = in_ref[:, pl.ds(pl.multiple_of(base + m * 256, 256), 128)]
                b = in_ref[:, pl.ds(pl.multiple_of(base + m * 256 + 128, 128), 128)]
                zero = jnp.where(low, a, pltpu.roll(b, 64, 1))
                one = jnp.where(low, pltpu.roll(a, 64, 1), b)
                here = pl.ds(m * 128, 128)
                mine, others = jnp.where(first, zero, one), jnp.where(first, one, zero)
                if far == 0:
                    own_ref[:, here] = mine
                    near_ref[0, :, here] = others.astype(BF16)
                else:
                    far_ref[0, :, here] = mine.astype(BF16)
                    far_ref[1, :, here] = others.astype(BF16)
        for g in range(left_ref.shape[0] // points):
            start = pl.multiple_of(g * points + pl.program_id(0) * rows, rows)
            piece = left_ref[pl.ds(start, rows), :]
            near_ref[1, :, pl.ds(g * points, points)] = piece
            far_ref[2, :, pl.ds(g * points, points)] = piece

    return pl.pallas_call(
        kernel,
        grid=(steps,),
        out_shape=[
            jax.ShapeDtypeStruct((points, width), F32),
            jax.ShapeDtypeStruct((2, points, width), BF16),
            jax.ShapeDtypeStruct((3, points, width), BF16),
        ],
        in_specs=[
            pl.BlockSpec((rows, count), lambda k: (k, 0)),
            pl.BlockSpec(left.shape, lambda k: (0, 0)),
        ],
        out_specs=[
            pl.BlockSpec((rows, width), lambda k: (k, 0)),
            pl.BlockSpec((2, rows, width), lambda k: (0, k, 0)),
            pl.BlockSpec((3, rows, width), lambda k: (0, k, 0)),
        ],
        compiler_params=params(8),
        name="pack",
    )(screened, left)


def joined(box, slot, psi_ref, column, points):
    for g in range(psi_ref.shape[0] // points):
        psi_ref[g * points : (g + 1) * points, column * points : (column + 1) * points] = box[
            slot, :, g * points : (g + 1) * points
        ]


def project(trial_half, left, near, far):
    states, points = left.shape
    cols = trial_half.shape[1]

    def kernel(trial_ref, left_ref, near_ref, far_ref, out_ref, psi_ref, sem):
        load = pltpu.make_async_copy(left_ref, psi_ref.at[:, :points], sem)
        load.start()
        joined(near_ref, 1, psi_ref, 1, points)
        joined(far_ref, 2, psi_ref, 2, points)
        load.wait()
        out_ref[...] = lax.dot_general(
            psi_ref[...], trial_ref[...], (((0,), (0,)), ((), ())), preferred_element_type=F32
        ).astype(BF16)

    return pl.pallas_call(
        kernel,
        out_shape=[
            jax.ShapeDtypeStruct((3 * points, cols), BF16),
            jax.ShapeDtypeStruct((states, 3 * points), BF16),
        ],
        in_specs=[vmem_spec(), pl.BlockSpec(memory_space=pl.ANY)] + [vmem_spec()] * 2,
        out_specs=[vmem_spec()] * 2,
        scratch_shapes=[pltpu.SemaphoreType.DMA],
        compiler_params=params(12),
        name="project",
    )(trial_half, left, near, far)


def project_last(trial_half, passed, three):
    states = trial_half.shape[0]
    cols = trial_half.shape[1]
    points = three.shape[0] // 3

    def kernel(trial_ref, passed_ref, three_ref, out_ref, psi_ref):
        joined(passed_ref, 1, psi_ref, 0, points)
        out_ref[: 3 * points, :] = three_ref[...]
        out_ref[3 * points :, :] = lax.dot_general(
            psi_ref[...], trial_ref[...], (((0,), (0,)), ((), ())), preferred_element_type=F32
        ).astype(BF16)

    return pl.pallas_call(
        kernel,
        out_shape=[
            jax.ShapeDtypeStruct((4 * points, cols), BF16),
            jax.ShapeDtypeStruct((states, points), BF16),
        ],
        in_specs=[vmem_spec()] * 3,
        out_specs=[vmem_spec()] * 2,
        compiler_params=params(12),
        name="project_last",
    )(trial_half, passed, three)


NT = (((1,), (1,)), ((), ()))


def own_pairs(proj_own, lines):
    rows, half = proj_own.shape
    block = lines[0].shape[0] // 4
    count, states = 16 * block, lines[0].shape[1]

    def kernel(own_ref, *refs):
        line_refs, (panel_ref, pair_ref) = refs[:5], refs[5:]
        y, x = lax.axis_index("y"), lax.axis_index("x")
        for k in range(16):
            at = lax.rem(y + STEPS[k // 4] + 4, 4) * 4 + lax.rem(x + STEPS[k % 4] + 4, 4)
            ref, row = (line_refs[k // 4], k % 4) if k < 12 else (line_refs[k // 2 - 3], k % 2)
            panel_ref[pl.ds(pl.multiple_of(at * block, block), block), :] = ref[
                row * block : (row + 1) * block, :
            ]
        mine = pl.ds(pl.multiple_of(lax.axis_index("core") * half, half), half)
        pair_ref[...] = lax.dot_general(own_ref[...], panel_ref[:, mine], NT, preferred_element_type=F32)

    return pl.pallas_call(
        kernel,
        out_shape=[
            jax.ShapeDtypeStruct((count, states), BF16),
            jax.ShapeDtypeStruct((rows, count), F32),
        ],
        in_specs=[vmem_spec()] * 6,
        out_specs=[vmem_spec()] * 2,
        compiler_params=params(16),
        name="own_pairs",
    )(proj_own, *lines)


def direct(proj_other, panel, pairs, own, boxes):
    rows, half = proj_other.shape
    points = rows // 4
    count = panel.shape[0]
    chunk = 512

    def kernel(other_ref, panel_ref, pair_ref, *refs):
        scr_refs, (weighted_ref, send_ref, proj) = refs[:4], refs[4:]
        core = lax.axis_index("core")
        sibs = pl.ds(pl.multiple_of((1 - core) * half, half), half)
        for k in range(4):
            proj[k * points : (k + 1) * points, :] = other_ref[
                SIBLING[k] * points : (SIBLING[k] + 1) * points, :
            ]
        for k in range(count // chunk):
            here = pl.ds(k * chunk, chunk)
            pair = pair_ref[:, here] + lax.dot_general(
                proj[...], panel_ref[here, sibs], NT, preferred_element_type=F32
            )
            for j in range(4):
                mine = slice(j * points, (j + 1) * points)
                weights = scr_refs[j][:, here] if j == 0 else scr_refs[j][0, :, here].astype(F32)
                weighted_ref[mine, here] = (weights * pair[mine]).astype(BF16)
        send = jnp.dot(weighted_ref[...], panel_ref[:, sibs], preferred_element_type=F32)
        send_ref[...] = send.astype(BF16)

    return pl.pallas_call(
        kernel,
        out_shape=[
            jax.ShapeDtypeStruct((rows, count), BF16),
            jax.ShapeDtypeStruct((rows, half), BF16),
        ],
        in_specs=[vmem_spec()] * 7,
        out_specs=[vmem_spec()] * 2,
        scratch_shapes=[pltpu.VMEM((rows, half), BF16)],
        compiler_params=params(24),
        name="direct",
    )(proj_other, panel, pairs, own, *boxes)


def own_half(weighted, panel):
    rows, count = weighted.shape
    half = panel.shape[1] // 2

    def kernel(weighted_ref, panel_ref, keep_ref):
        mine = pl.ds(pl.multiple_of(lax.axis_index("core") * half, half), half)
        keep_ref[...] = jnp.dot(weighted_ref[...], panel_ref[:, mine], preferred_element_type=F32)

    return pl.pallas_call(
        kernel,
        out_shape=jax.ShapeDtypeStruct((rows, half), F32),
        in_specs=[vmem_spec()] * 2,
        out_specs=vmem_spec(),
        compiler_params=params(16),
        name="own_half",
    )(weighted, panel)


def finish(psi, psi_last, keep, got):
    states, points = psi_last.shape
    count = 4 * points
    cols = keep.shape[1]

    def kernel(psi_ref, last_ref, keep_ref, got_ref, out_ref, high, low):
        for k in range(4):
            here = slice(k * points, (k + 1) * points)
            there = slice(SIBLING[k] * points, (SIBLING[k] + 1) * points)
            back = keep_ref[here, :] + got_ref[there, :].astype(F32)
            top = back.astype(BF16)
            high[here, :] = top
            low[here, :] = (back - top.astype(F32)).astype(BF16)
        total = None
        for piece in (high, low):
            for ref, here in ((psi_ref, slice(0, 3 * points)), (last_ref, slice(3 * points, count))):
                part = jnp.dot(ref[...], piece[here, :], preferred_element_type=F32)
                total = part if total is None else total + part
        out_ref[...] = total.astype(BF16)

    return pl.pallas_call(
        kernel,
        out_shape=jax.ShapeDtypeStruct((states, cols), BF16),
        in_specs=[vmem_spec()] * 4,
        out_specs=vmem_spec(),
        scratch_shapes=[pltpu.VMEM((count, cols), BF16)] * 2,
        compiler_params=params(16),
        name="finish",
    )(psi, psi_last, keep, got)


def shards(trial, psi_v, psi_c, screened):
    rows, states = trial.shape[1:]
    half = states // 2
    devices = lax.axis_size(TILE_VEC)
    own, near, far = pack(screened, psi_v)
    block = psi_c[:, 0, :].T
    line = jnp.concatenate([block, shift(block, "x", 1), shift(block, "x", -1), shift(block, "x", 2)], 0)
    halves = trial[0].reshape(rows, 2, half).transpose(1, 0, 2)
    copies = jnp.broadcast_to(halves[None, :, None], (devices // 4, 2, 2, rows, half))
    copies, near, far, line = lax.optimization_barrier((copies, near, far, line))
    trial_half = exchange(copies.reshape(devices, rows, half), TILE_VEC).reshape(-1, half)
    near = swap(near)
    far = lax.ppermute(far, "zh", [(0, 1), (1, 0)])
    behind, ahead = shift(line, "y", 1), shift(line, "y", -1)
    middle = line.shape[0] // 2
    beyond = [shift(behind[:middle], "y", 1), shift(ahead[middle:], "y", -1)]
    far, beyond = lax.optimization_barrier((far, beyond))
    passed = swap(far[1:])
    three, psi = project(trial_half, psi_v, near, far)
    proj_own, psi_last = project_last(trial_half, passed, three)
    proj_other = swap(proj_own)
    panel = [line, behind, ahead, *beyond]
    ordered, pairs = own_pairs(proj_own, panel)
    weighted, send = direct(proj_other, ordered, pairs, own, [near, far, passed])
    got = swap(send)
    keep = own_half(weighted, ordered)
    term = finish(psi, psi_last, keep, got)
    parts = exchange(term.reshape(devices, rows, half), TILE_VEC)
    parts = parts.reshape(-1, 2, 2, rows, half).astype(F32)
    total = jnp.sum(parts, axis=(0, 2))
    return total.transpose(1, 0, 2).reshape(1, rows, states)


def solution(mesh):
    split = Mesh(
        mesh.devices.reshape(2, 4, 4, 2, mesh.shape["vec"]),
        TILE_VEC,
    )
    return jax.shard_map(
        shards,
        mesh=split,
        in_specs=(P(None, TILE_VEC, None), P(None, TILE), P(None, "zl", TILE), P(TILE, "zl")),
        out_specs=P(None, TILE_VEC, None),
        check_vma=False,
    )
```

```python
import jax
import jax.numpy as jnp
from jax import lax
from jax.experimental import pallas as pl
from jax.experimental.pallas import tpu as pltpu
from jax.sharding import Mesh
from jax.sharding import PartitionSpec as P

TILE_VEC = ("zh", "y", "x", "core", "zl")
TILE = ("zh", "y", "x", "core")
STEPS = (0, -1, 1, -2)
F32 = jnp.float32
BF16 = jnp.bfloat16
SIBLING = (1, 0, 3, 2)


def shift(value, axis, by):
    n = lax.axis_size(axis)
    return lax.ppermute(value, axis, [(k, (k + by) % n) for k in range(n)])


def exchange(value, axes):
    return lax.all_to_all(value, axes, split_axis=0, concat_axis=0, tiled=True)


def swap(value):
    return lax.ppermute(value, "core", [(0, 1), (1, 0)])


def vmem_spec():
    return pl.BlockSpec(memory_space=pltpu.VMEM)


def params(mebibytes):
    return pltpu.CompilerParams(vmem_limit_bytes=mebibytes * 1024 * 1024)


def pack(screened, left):
    points, count = screened.shape
    plane, steps = count // 2, 4
    width = plane // 2
    rows = points // steps

    def kernel(in_ref, left_ref, own_ref, near_ref, far_ref):
        core, zh = lax.axis_index("core"), lax.axis_index("zh")
        low = lax.broadcasted_iota(jnp.int32, (rows, 128), 1) < 64
        first = core == 0
        for far in range(2):
            base = plane * (zh if far == 0 else 1 - zh)
            for m in range(width // 128):
                a = in_ref[:, pl.ds(pl.multiple_of(base + m * 256, 256), 128)]
                b = in_ref[:, pl.ds(pl.multiple_of(base + m * 256 + 128, 128), 128)]
                zero = jnp.where(low, a, pltpu.roll(b, 64, 1))
                one = jnp.where(low, pltpu.roll(a, 64, 1), b)
                here = pl.ds(m * 128, 128)
                mine, others = jnp.where(first, zero, one), jnp.where(first, one, zero)
                if far == 0:
                    own_ref[:, here] = mine
                    near_ref[0, :, here] = others.astype(BF16)
                else:
                    far_ref[0, :, here] = mine.astype(BF16)
                    far_ref[1, :, here] = others.astype(BF16)
        for g in range(left_ref.shape[0] // points):
            start = pl.multiple_of(g * points + pl.program_id(0) * rows, rows)
            piece = left_ref[pl.ds(start, rows), :]
            near_ref[1, :, pl.ds(g * points, points)] = piece
            far_ref[2, :, pl.ds(g * points, points)] = piece

    return pl.pallas_call(
        kernel,
        grid=(steps,),
        out_shape=[
            jax.ShapeDtypeStruct((points, width), F32),
            jax.ShapeDtypeStruct((2, points, width), BF16),
            jax.ShapeDtypeStruct((3, points, width), BF16),
        ],
        in_specs=[
            pl.BlockSpec((rows, count), lambda k: (k, 0)),
            pl.BlockSpec(left.shape, lambda k: (0, 0)),
        ],
        out_specs=[
            pl.BlockSpec((rows, width), lambda k: (k, 0)),
            pl.BlockSpec((2, rows, width), lambda k: (0, k, 0)),
            pl.BlockSpec((3, rows, width), lambda k: (0, k, 0)),
        ],
        compiler_params=params(8),
        name="pack",
    )(screened, left)


def joined(box, slot, psi_ref, column, points):
    for g in range(psi_ref.shape[0] // points):
        psi_ref[g * points : (g + 1) * points, column * points : (column + 1) * points] = box[
            slot, :, g * points : (g + 1) * points
        ]


def project(trial_half, left, near, far):
    states, points = left.shape
    cols = trial_half.shape[1]

    def kernel(trial_ref, left_ref, near_ref, far_ref, out_ref, psi_ref, sem):
        load = pltpu.make_async_copy(left_ref, psi_ref.at[:, :points], sem)
        load.start()
        joined(near_ref, 1, psi_ref, 1, points)
        joined(far_ref, 2, psi_ref, 2, points)
        load.wait()
        out_ref[...] = lax.dot_general(
            psi_ref[...], trial_ref[...], (((0,), (0,)), ((), ())), preferred_element_type=F32
        ).astype(BF16)

    return pl.pallas_call(
        kernel,
        out_shape=[
            jax.ShapeDtypeStruct((3 * points, cols), BF16),
            jax.ShapeDtypeStruct((states, 3 * points), BF16),
        ],
        in_specs=[vmem_spec(), pl.BlockSpec(memory_space=pl.ANY)] + [vmem_spec()] * 2,
        out_specs=[vmem_spec()] * 2,
        scratch_shapes=[pltpu.SemaphoreType.DMA],
        compiler_params=params(12),
        name="project",
    )(trial_half, left, near, far)


def project_last(trial_half, passed, three):
    states = trial_half.shape[0]
    cols = trial_half.shape[1]
    points = three.shape[0] // 3

    def kernel(trial_ref, passed_ref, three_ref, out_ref, psi_ref):
        joined(passed_ref, 1, psi_ref, 0, points)
        out_ref[: 3 * points, :] = three_ref[...]
        out_ref[3 * points :, :] = lax.dot_general(
            psi_ref[...], trial_ref[...], (((0,), (0,)), ((), ())), preferred_element_type=F32
        ).astype(BF16)

    return pl.pallas_call(
        kernel,
        out_shape=[
            jax.ShapeDtypeStruct((4 * points, cols), BF16),
            jax.ShapeDtypeStruct((states, points), BF16),
        ],
        in_specs=[vmem_spec()] * 3,
        out_specs=[vmem_spec()] * 2,
        compiler_params=params(12),
        name="project_last",
    )(trial_half, passed, three)


NT = (((1,), (1,)), ((), ()))


def own_pairs(proj_own, lines):
    rows, half = proj_own.shape
    block = lines[0].shape[0] // 4
    count, states = 16 * block, lines[0].shape[1]

    def kernel(own_ref, *refs):
        line_refs, (panel_ref, pair_ref) = refs[:5], refs[5:]
        y, x = lax.axis_index("y"), lax.axis_index("x")
        for k in range(16):
            at = lax.rem(y + STEPS[k // 4] + 4, 4) * 4 + lax.rem(x + STEPS[k % 4] + 4, 4)
            ref, row = (line_refs[k // 4], k % 4) if k < 12 else (line_refs[k // 2 - 3], k % 2)
            panel_ref[pl.ds(pl.multiple_of(at * block, block), block), :] = ref[
                row * block : (row + 1) * block, :
            ]
        mine = pl.ds(pl.multiple_of(lax.axis_index("core") * half, half), half)
        pair_ref[...] = lax.dot_general(own_ref[...], panel_ref[:, mine], NT, preferred_element_type=F32)

    return pl.pallas_call(
        kernel,
        out_shape=[
            jax.ShapeDtypeStruct((count, states), BF16),
            jax.ShapeDtypeStruct((rows, count), F32),
        ],
        in_specs=[vmem_spec()] * 6,
        out_specs=[vmem_spec()] * 2,
        compiler_params=params(16),
        name="own_pairs",
    )(proj_own, *lines)


def direct(proj_other, panel, pairs, own, boxes):
    rows, half = proj_other.shape
    points = rows // 4
    count = panel.shape[0]
    chunk = 512

    def kernel(other_ref, panel_ref, pair_ref, *refs):
        scr_refs, (weighted_ref, send_ref, proj) = refs[:4], refs[4:]
        core = lax.axis_index("core")
        sibs = pl.ds(pl.multiple_of((1 - core) * half, half), half)
        for k in range(4):
            proj[k * points : (k + 1) * points, :] = other_ref[
                SIBLING[k] * points : (SIBLING[k] + 1) * points, :
            ]
        for k in range(count // chunk):
            here = pl.ds(k * chunk, chunk)
            pair = pair_ref[:, here] + lax.dot_general(
                proj[...], panel_ref[here, sibs], NT, preferred_element_type=F32
            )
            for j in range(4):
                mine = slice(j * points, (j + 1) * points)
                weights = scr_refs[j][:, here] if j == 0 else scr_refs[j][0, :, here].astype(F32)
                weighted_ref[mine, here] = (weights * pair[mine]).astype(BF16)
        send = jnp.dot(weighted_ref[...], panel_ref[:, sibs], preferred_element_type=F32)
        send_ref[...] = send.astype(BF16)

    return pl.pallas_call(
        kernel,
        out_shape=[
            jax.ShapeDtypeStruct((rows, count), BF16),
            jax.ShapeDtypeStruct((rows, half), BF16),
        ],
        in_specs=[vmem_spec()] * 7,
        out_specs=[vmem_spec()] * 2,
        scratch_shapes=[pltpu.VMEM((rows, half), BF16)],
        compiler_params=params(24),
        name="direct",
    )(proj_other, panel, pairs, own, *boxes)


def own_half(weighted, panel, psi, psi_last):
    rows, count = weighted.shape
    half = panel.shape[1] // 2
    states, three = psi.shape

    def kernel(weighted_ref, panel_ref, psi_ref, last_ref, keep_ref, all_ref):
        mine = pl.ds(pl.multiple_of(lax.axis_index("core") * half, half), half)
        keep_ref[...] = jnp.dot(weighted_ref[...], panel_ref[:, mine], preferred_element_type=F32)
        all_ref[:, :three] = psi_ref[...]
        all_ref[:, three:] = last_ref[...]

    return pl.pallas_call(
        kernel,
        out_shape=[
            jax.ShapeDtypeStruct((rows, half), F32),
            jax.ShapeDtypeStruct((states, three + psi_last.shape[1]), BF16),
        ],
        in_specs=[vmem_spec()] * 4,
        out_specs=[vmem_spec()] * 2,
        compiler_params=params(16),
        name="own_half",
    )(weighted, panel, psi, psi_last)


def finish(psi, keep, got):
    states, count = psi.shape
    points = count // 4
    cols = keep.shape[1]

    def kernel(psi_ref, keep_ref, got_ref, out_ref, high, low):
        for k in range(4):
            here = slice(k * points, (k + 1) * points)
            there = slice(SIBLING[k] * points, (SIBLING[k] + 1) * points)
            back = keep_ref[here, :] + got_ref[there, :].astype(F32)
            top = back.astype(BF16)
            high[here, :] = top
            low[here, :] = (back - top.astype(F32)).astype(BF16)
        total = jnp.dot(psi_ref[...], high[...], preferred_element_type=F32)
        total += jnp.dot(psi_ref[...], low[...], preferred_element_type=F32)
        out_ref[...] = total.astype(BF16)

    return pl.pallas_call(
        kernel,
        out_shape=jax.ShapeDtypeStruct((states, cols), BF16),
        in_specs=[vmem_spec()] * 3,
        out_specs=vmem_spec(),
        scratch_shapes=[pltpu.VMEM((count, cols), BF16)] * 2,
        compiler_params=params(16),
        name="finish",
    )(psi, keep, got)


def shards(trial, psi_v, psi_c, screened):
    rows, states = trial.shape[1:]
    half = states // 2
    devices = lax.axis_size(TILE_VEC)
    own, near, far = pack(screened, psi_v)
    block = psi_c[:, 0, :].T
    line = jnp.concatenate([block, shift(block, "x", 1), shift(block, "x", -1), shift(block, "x", 2)], 0)
    halves = trial[0].reshape(rows, 2, half).transpose(1, 0, 2)
    copies = jnp.broadcast_to(halves[None, :, None], (devices // 4, 2, 2, rows, half))
    copies, near, far, line = lax.optimization_barrier((copies, near, far, line))
    trial_half = exchange(copies.reshape(devices, rows, half), TILE_VEC).reshape(-1, half)
    near = swap(near)
    far = lax.ppermute(far, "zh", [(0, 1), (1, 0)])
    behind, ahead = shift(line, "y", 1), shift(line, "y", -1)
    middle = line.shape[0] // 2
    beyond = [shift(behind[:middle], "y", 1), shift(ahead[middle:], "y", -1)]
    far, beyond = lax.optimization_barrier((far, beyond))
    passed = swap(far[1:])
    three, psi = project(trial_half, psi_v, near, far)
    proj_own, psi_last = project_last(trial_half, passed, three)
    proj_other = swap(proj_own)
    panel = [line, behind, ahead, *beyond]
    ordered, pairs = own_pairs(proj_own, panel)
    weighted, send = direct(proj_other, ordered, pairs, own, [near, far, passed])
    got = swap(send)
    keep, psi = own_half(weighted, ordered, psi, psi_last)
    term = finish(psi, keep, got)
    parts = exchange(term.reshape(devices, rows, half), TILE_VEC)
    parts = parts.reshape(-1, 2, 2, rows, half).astype(F32)
    total = jnp.sum(parts, axis=(0, 2))
    return total.transpose(1, 0, 2).reshape(1, rows, states)


def solution(mesh):
    split = Mesh(
        mesh.devices.reshape(2, 4, 4, 2, mesh.shape["vec"]),
        TILE_VEC,
    )
    return jax.shard_map(
        shards,
        mesh=split,
        in_specs=(P(None, TILE_VEC, None), P(None, TILE), P(None, "zl", TILE), P(TILE, "zl")),
        out_specs=P(None, TILE_VEC, None),
        check_vma=False,
    )
```

```python
import jax
import jax.numpy as jnp
from jax import lax
from jax.experimental import pallas as pl
from jax.experimental.pallas import tpu as pltpu
from jax.sharding import Mesh
from jax.sharding import PartitionSpec as P

TILE_VEC = ("zh", "y", "x", "core", "zl")
TILE = ("zh", "y", "x", "core")
STEPS = (0, -1, 1, -2)
F32 = jnp.float32
BF16 = jnp.bfloat16
SIBLING = (1, 0, 3, 2)


def shift(value, axis, by):
    n = lax.axis_size(axis)
    return lax.ppermute(value, axis, [(k, (k + by) % n) for k in range(n)])


def exchange(value, axes):
    return lax.all_to_all(value, axes, split_axis=0, concat_axis=0, tiled=True)


def swap(value):
    return lax.ppermute(value, "core", [(0, 1), (1, 0)])


def vmem_spec():
    return pl.BlockSpec(memory_space=pltpu.VMEM)


def params(mebibytes):
    return pltpu.CompilerParams(vmem_limit_bytes=mebibytes * 1024 * 1024)


def pack(screened, left):
    points, count = screened.shape
    plane, steps = count // 2, 4
    width = plane // 2
    rows = points // steps

    def kernel(in_ref, left_ref, own_ref, near_ref, far_ref):
        core, zh = lax.axis_index("core"), lax.axis_index("zh")
        low = lax.broadcasted_iota(jnp.int32, (rows, 128), 1) < 64
        first = core == 0
        for far in range(2):
            base = plane * (zh if far == 0 else 1 - zh)
            for m in range(width // 128):
                a = in_ref[:, pl.ds(pl.multiple_of(base + m * 256, 256), 128)]
                b = in_ref[:, pl.ds(pl.multiple_of(base + m * 256 + 128, 128), 128)]
                zero = jnp.where(low, a, pltpu.roll(b, 64, 1))
                one = jnp.where(low, pltpu.roll(a, 64, 1), b)
                here = pl.ds(m * 128, 128)
                mine, others = jnp.where(first, zero, one), jnp.where(first, one, zero)
                if far == 0:
                    own_ref[:, here] = mine
                    near_ref[0, :, here] = others.astype(BF16)
                else:
                    far_ref[0, :, here] = mine.astype(BF16)
                    far_ref[1, :, here] = others.astype(BF16)
        for g in range(left_ref.shape[0] // points):
            start = pl.multiple_of(g * points + pl.program_id(0) * rows, rows)
            piece = left_ref[pl.ds(start, rows), :]
            near_ref[1, :, pl.ds(g * points, points)] = piece
            far_ref[2, :, pl.ds(g * points, points)] = piece

    return pl.pallas_call(
        kernel,
        grid=(steps,),
        out_shape=[
            jax.ShapeDtypeStruct((points, width), F32),
            jax.ShapeDtypeStruct((2, points, width), BF16),
            jax.ShapeDtypeStruct((3, points, width), BF16),
        ],
        in_specs=[
            pl.BlockSpec((rows, count), lambda k: (k, 0)),
            pl.BlockSpec(left.shape, lambda k: (0, 0)),
        ],
        out_specs=[
            pl.BlockSpec((rows, width), lambda k: (k, 0)),
            pl.BlockSpec((2, rows, width), lambda k: (0, k, 0)),
            pl.BlockSpec((3, rows, width), lambda k: (0, k, 0)),
        ],
        compiler_params=params(8),
        name="pack",
    )(screened, left)


def joined(box, slot, psi_ref, column, points):
    for g in range(psi_ref.shape[0] // points):
        psi_ref[g * points : (g + 1) * points, column * points : (column + 1) * points] = box[
            slot, :, g * points : (g + 1) * points
        ]


def project(trial_half, left, near, far):
    states, points = left.shape
    cols = trial_half.shape[1]

    def kernel(trial_ref, left_ref, near_ref, far_ref, out_ref, psi_ref, sem):
        load = pltpu.make_async_copy(left_ref, psi_ref.at[:, :points], sem)
        load.start()
        joined(near_ref, 1, psi_ref, 1, points)
        joined(far_ref, 2, psi_ref, 2, points)
        load.wait()
        out_ref[...] = lax.dot_general(
            psi_ref[...], trial_ref[...], (((0,), (0,)), ((), ())), preferred_element_type=F32
        ).astype(BF16)

    return pl.pallas_call(
        kernel,
        out_shape=[
            jax.ShapeDtypeStruct((3 * points, cols), BF16),
            jax.ShapeDtypeStruct((states, 3 * points), BF16),
        ],
        in_specs=[vmem_spec(), pl.BlockSpec(memory_space=pl.ANY)] + [vmem_spec()] * 2,
        out_specs=[vmem_spec()] * 2,
        scratch_shapes=[pltpu.SemaphoreType.DMA],
        compiler_params=params(12),
        name="project",
    )(trial_half, left, near, far)


def project_last(trial_half, passed, three):
    states = trial_half.shape[0]
    cols = trial_half.shape[1]
    points = three.shape[0] // 3

    def kernel(trial_ref, passed_ref, three_ref, out_ref, psi_ref):
        joined(passed_ref, 1, psi_ref, 0, points)
        out_ref[: 3 * points, :] = three_ref[...]
        out_ref[3 * points :, :] = lax.dot_general(
            psi_ref[...], trial_ref[...], (((0,), (0,)), ((), ())), preferred_element_type=F32
        ).astype(BF16)

    return pl.pallas_call(
        kernel,
        out_shape=[
            jax.ShapeDtypeStruct((4 * points, cols), BF16),
            jax.ShapeDtypeStruct((states, points), BF16),
        ],
        in_specs=[vmem_spec()] * 3,
        out_specs=[vmem_spec()] * 2,
        compiler_params=params(12),
        name="project_last",
    )(trial_half, passed, three)


NT = (((1,), (1,)), ((), ()))


def own_pairs(proj_own, lines):
    rows, half = proj_own.shape
    block = lines[0].shape[0] // 4
    count, states = 16 * block, lines[0].shape[1]

    def kernel(own_ref, *refs):
        line_refs, (panel_ref, pair_ref) = refs[:5], refs[5:]
        y, x = lax.axis_index("y"), lax.axis_index("x")
        for k in range(16):
            at = lax.rem(y + STEPS[k // 4] + 4, 4) * 4 + lax.rem(x + STEPS[k % 4] + 4, 4)
            ref, row = (line_refs[k // 4], k % 4) if k < 12 else (line_refs[k // 2 - 3], k % 2)
            panel_ref[pl.ds(pl.multiple_of(at * block, block), block), :] = ref[
                row * block : (row + 1) * block, :
            ]
        mine = pl.ds(pl.multiple_of(lax.axis_index("core") * half, half), half)
        pair_ref[...] = lax.dot_general(own_ref[...], panel_ref[:, mine], NT, preferred_element_type=F32)

    return pl.pallas_call(
        kernel,
        out_shape=[
            jax.ShapeDtypeStruct((count, states), BF16),
            jax.ShapeDtypeStruct((rows, count), F32),
        ],
        in_specs=[vmem_spec()] * 6,
        out_specs=[vmem_spec()] * 2,
        compiler_params=params(16),
        name="own_pairs",
    )(proj_own, *lines)


def direct(proj_other, panel, pairs, own, boxes):
    rows, half = proj_other.shape
    points = rows // 4
    count = panel.shape[0]
    chunk = 512

    def kernel(other_ref, panel_ref, pair_ref, *refs):
        scr_refs, (weighted_ref, send_ref, proj) = refs[:4], refs[4:]
        core = lax.axis_index("core")
        sibs = pl.ds(pl.multiple_of((1 - core) * half, half), half)
        for k in range(4):
            proj[k * points : (k + 1) * points, :] = other_ref[
                SIBLING[k] * points : (SIBLING[k] + 1) * points, :
            ]
        for k in range(count // chunk):
            here = pl.ds(k * chunk, chunk)
            pair = pair_ref[:, here] + lax.dot_general(
                proj[...], panel_ref[here, sibs], NT, preferred_element_type=F32
            )
            for j in range(4):
                mine = slice(j * points, (j + 1) * points)
                weights = scr_refs[j][:, here] if j == 0 else scr_refs[j][0, :, here].astype(F32)
                weighted_ref[mine, here] = (weights * pair[mine]).astype(BF16)
        send = jnp.dot(weighted_ref[...], panel_ref[:, sibs], preferred_element_type=F32)
        send_ref[...] = send.astype(BF16)

    return pl.pallas_call(
        kernel,
        out_shape=[
            jax.ShapeDtypeStruct((rows, count), BF16),
            jax.ShapeDtypeStruct((rows, half), BF16),
        ],
        in_specs=[vmem_spec()] * 7,
        out_specs=[vmem_spec()] * 2,
        scratch_shapes=[pltpu.VMEM((rows, half), BF16)],
        compiler_params=params(24),
        name="direct",
    )(proj_other, panel, pairs, own, *boxes)


def own_half(weighted, panel, psi, psi_last):
    rows, count = weighted.shape
    half = panel.shape[1] // 2
    states, three = psi.shape

    def kernel(weighted_ref, panel_ref, psi_ref, last_ref, keep_ref, all_ref):
        mine = pl.ds(pl.multiple_of(lax.axis_index("core") * half, half), half)
        keep_ref[...] = jnp.dot(weighted_ref[...], panel_ref[:, mine], preferred_element_type=F32)
        all_ref[:, :three] = psi_ref[...]
        all_ref[:, three:] = last_ref[...]

    return pl.pallas_call(
        kernel,
        out_shape=[
            jax.ShapeDtypeStruct((rows, half), F32),
            jax.ShapeDtypeStruct((states, three + psi_last.shape[1]), BF16),
        ],
        in_specs=[vmem_spec()] * 4,
        out_specs=[vmem_spec()] * 2,
        compiler_params=params(16),
        name="own_half",
    )(weighted, panel, psi, psi_last)


def finish(psi, keep, got):
    states, count = psi.shape
    points = count // 4
    cols = keep.shape[1]

    def kernel(psi_ref, keep_ref, got_ref, out_ref, high, low):
        for k in range(4):
            here = slice(k * points, (k + 1) * points)
            there = slice(SIBLING[k] * points, (SIBLING[k] + 1) * points)
            back = keep_ref[here, :] + got_ref[there, :].astype(F32)
            top = back.astype(BF16)
            high[here, :] = top
            low[here, :] = (back - top.astype(F32)).astype(BF16)
        total = jnp.dot(psi_ref[...], high[...], preferred_element_type=F32)
        total += jnp.dot(psi_ref[...], low[...], preferred_element_type=F32)
        out_ref[...] = total.astype(BF16)

    return pl.pallas_call(
        kernel,
        out_shape=jax.ShapeDtypeStruct((states, cols), BF16),
        in_specs=[vmem_spec()] * 3,
        out_specs=vmem_spec(),
        scratch_shapes=[pltpu.VMEM((count, cols), BF16)] * 2,
        compiler_params=params(16),
        name="finish",
    )(psi, keep, got)


def shards(trial, psi_v, psi_c, screened):
    rows, states = trial.shape[1:]
    half = states // 2
    devices = lax.axis_size(TILE_VEC)
    own, near, far = pack(screened, psi_v)
    block = psi_c[:, 0, :].T
    line = jnp.concatenate([block, shift(block, "x", 1), shift(block, "x", -1), shift(block, "x", 2)], 0)
    halves = trial[0].reshape(rows, 2, half).transpose(1, 0, 2)
    copies = jnp.broadcast_to(halves[None, :, None], (devices // 4, 2, 2, rows, half))
    copies, near, far, line = lax.optimization_barrier((copies, near, far, line))
    trial_half = exchange(copies.reshape(devices, rows, half), TILE_VEC).reshape(-1, half)
    near = swap(near)
    far = lax.ppermute(far, "zh", [(0, 1), (1, 0)])
    behind, ahead = shift(line, "y", 1), shift(line, "y", -1)
    middle = line.shape[0] // 2
    beyond = [shift(behind[:middle], "y", 1), shift(ahead[middle:], "y", -1)]
    tail, far, beyond = lax.optimization_barrier((far[1:], far, beyond))
    passed = swap(tail)
    three, psi = project(trial_half, psi_v, near, far)
    proj_own, psi_last = project_last(trial_half, passed, three)
    proj_other = swap(proj_own)
    panel = [line, behind, ahead, *beyond]
    ordered, pairs = own_pairs(proj_own, panel)
    weighted, send = direct(proj_other, ordered, pairs, own, [near, far, passed])
    got = swap(send)
    keep, psi = own_half(weighted, ordered, psi, psi_last)
    term = finish(psi, keep, got)
    parts = exchange(term.reshape(devices, rows, half), TILE_VEC)
    parts = parts.reshape(-1, 2, 2, rows, half).astype(F32)
    total = jnp.sum(parts, axis=(0, 2))
    return total.transpose(1, 0, 2).reshape(1, rows, states)


def solution(mesh):
    split = Mesh(
        mesh.devices.reshape(2, 4, 4, 2, mesh.shape["vec"]),
        TILE_VEC,
    )
    return jax.shard_map(
        shards,
        mesh=split,
        in_specs=(P(None, TILE_VEC, None), P(None, TILE), P(None, "zl", TILE), P(TILE, "zl")),
        out_specs=P(None, TILE_VEC, None),
        check_vma=False,
    )
```

```python
import jax
import jax.numpy as jnp
from jax import lax
from jax.experimental import pallas as pl
from jax.experimental.pallas import tpu as pltpu
from jax.sharding import Mesh
from jax.sharding import PartitionSpec as P

TILE_VEC = ("zh", "y", "x", "core", "zl")
TILE = ("zh", "y", "x", "core")
STEPS = (0, -1, 1, -2)
F32 = jnp.float32
BF16 = jnp.bfloat16
SIBLING = (1, 0, 3, 2)


def shift(value, axis, by):
    n = lax.axis_size(axis)
    return lax.ppermute(value, axis, [(k, (k + by) % n) for k in range(n)])


def exchange(value, axes):
    return lax.all_to_all(value, axes, split_axis=0, concat_axis=0, tiled=True)


def swap(value):
    return lax.ppermute(value, "core", [(0, 1), (1, 0)])


def vmem_spec():
    return pl.BlockSpec(memory_space=pltpu.VMEM)


def params(mebibytes):
    return pltpu.CompilerParams(vmem_limit_bytes=mebibytes * 1024 * 1024)


def pack(screened, left):
    points, count = screened.shape
    plane, steps = count // 2, 4
    width = plane // 2
    rows = points // steps

    def kernel(in_ref, left_ref, own_ref, near_ref, far_ref):
        core, zh = lax.axis_index("core"), lax.axis_index("zh")
        low = lax.broadcasted_iota(jnp.int32, (rows, 128), 1) < 64
        first = core == 0
        for far in range(2):
            base = plane * (zh if far == 0 else 1 - zh)
            for m in range(width // 128):
                a = in_ref[:, pl.ds(pl.multiple_of(base + m * 256, 256), 128)]
                b = in_ref[:, pl.ds(pl.multiple_of(base + m * 256 + 128, 128), 128)]
                zero = jnp.where(low, a, pltpu.roll(b, 64, 1))
                one = jnp.where(low, pltpu.roll(a, 64, 1), b)
                here = pl.ds(m * 128, 128)
                mine, others = jnp.where(first, zero, one), jnp.where(first, one, zero)
                if far == 0:
                    own_ref[:, here] = mine
                    near_ref[0, :, here] = others.astype(BF16)
                else:
                    far_ref[0, :, here] = mine.astype(BF16)
                    far_ref[1, :, here] = others.astype(BF16)
        for g in range(left_ref.shape[0] // points):
            start = pl.multiple_of(g * points + pl.program_id(0) * rows, rows)
            piece = left_ref[pl.ds(start, rows), :]
            near_ref[1, :, pl.ds(g * points, points)] = piece
            far_ref[2, :, pl.ds(g * points, points)] = piece

    return pl.pallas_call(
        kernel,
        grid=(steps,),
        out_shape=[
            jax.ShapeDtypeStruct((points, width), F32),
            jax.ShapeDtypeStruct((2, points, width), BF16),
            jax.ShapeDtypeStruct((3, points, width), BF16),
        ],
        in_specs=[
            pl.BlockSpec((rows, count), lambda k: (k, 0)),
            pl.BlockSpec(left.shape, lambda k: (0, 0)),
        ],
        out_specs=[
            pl.BlockSpec((rows, width), lambda k: (k, 0)),
            pl.BlockSpec((2, rows, width), lambda k: (0, k, 0)),
            pl.BlockSpec((3, rows, width), lambda k: (0, k, 0)),
        ],
        compiler_params=params(8),
        name="pack",
    )(screened, left)


def joined(box, slot, psi_ref, column, points):
    for g in range(psi_ref.shape[0] // points):
        psi_ref[g * points : (g + 1) * points, column * points : (column + 1) * points] = box[
            slot, :, g * points : (g + 1) * points
        ]


def project(trial_half, left, near, far):
    states, points = left.shape
    cols = trial_half.shape[1]

    def kernel(trial_ref, left_ref, near_ref, far_ref, out_ref, psi_ref, sem):
        load = pltpu.make_async_copy(left_ref, psi_ref.at[:, :points], sem)
        load.start()
        joined(near_ref, 1, psi_ref, 1, points)
        joined(far_ref, 2, psi_ref, 2, points)
        load.wait()
        out_ref[...] = lax.dot_general(
            psi_ref[...], trial_ref[...], (((0,), (0,)), ((), ())), preferred_element_type=F32
        ).astype(BF16)

    return pl.pallas_call(
        kernel,
        out_shape=[
            jax.ShapeDtypeStruct((3 * points, cols), BF16),
            jax.ShapeDtypeStruct((states, 3 * points), BF16),
        ],
        in_specs=[vmem_spec(), pl.BlockSpec(memory_space=pl.ANY)] + [vmem_spec()] * 2,
        out_specs=[vmem_spec()] * 2,
        scratch_shapes=[pltpu.SemaphoreType.DMA],
        compiler_params=params(12),
        name="project",
    )(trial_half, left, near, far)


def project_last(trial_half, passed, three):
    states = trial_half.shape[0]
    cols = trial_half.shape[1]
    points = three.shape[0] // 3

    def kernel(trial_ref, passed_ref, three_ref, out_ref, psi_ref):
        joined(passed_ref, 2, psi_ref, 0, points)
        out_ref[: 3 * points, :] = three_ref[...]
        out_ref[3 * points :, :] = lax.dot_general(
            psi_ref[...], trial_ref[...], (((0,), (0,)), ((), ())), preferred_element_type=F32
        ).astype(BF16)

    return pl.pallas_call(
        kernel,
        out_shape=[
            jax.ShapeDtypeStruct((4 * points, cols), BF16),
            jax.ShapeDtypeStruct((states, points), BF16),
        ],
        in_specs=[vmem_spec()] * 3,
        out_specs=[vmem_spec()] * 2,
        compiler_params=params(12),
        name="project_last",
    )(trial_half, passed, three)


NT = (((1,), (1,)), ((), ()))


def own_pairs(proj_own, lines):
    rows, half = proj_own.shape
    block = lines[0].shape[0] // 4
    count, states = 16 * block, lines[0].shape[1]

    def kernel(own_ref, *refs):
        line_refs, (panel_ref, pair_ref) = refs[:5], refs[5:]
        y, x = lax.axis_index("y"), lax.axis_index("x")
        for k in range(16):
            at = lax.rem(y + STEPS[k // 4] + 4, 4) * 4 + lax.rem(x + STEPS[k % 4] + 4, 4)
            ref, row = (line_refs[k // 4], k % 4) if k < 12 else (line_refs[k // 2 - 3], k % 2)
            panel_ref[pl.ds(pl.multiple_of(at * block, block), block), :] = ref[
                row * block : (row + 1) * block, :
            ]
        mine = pl.ds(pl.multiple_of(lax.axis_index("core") * half, half), half)
        pair_ref[...] = lax.dot_general(own_ref[...], panel_ref[:, mine], NT, preferred_element_type=F32)

    return pl.pallas_call(
        kernel,
        out_shape=[
            jax.ShapeDtypeStruct((count, states), BF16),
            jax.ShapeDtypeStruct((rows, count), F32),
        ],
        in_specs=[vmem_spec()] * 6,
        out_specs=[vmem_spec()] * 2,
        compiler_params=params(16),
        name="own_pairs",
    )(proj_own, *lines)


def direct(proj_other, panel, pairs, own, boxes):
    rows, half = proj_other.shape
    points = rows // 4
    count = panel.shape[0]
    chunk = 512

    def kernel(other_ref, panel_ref, pair_ref, *refs):
        scr_refs, (weighted_ref, send_ref, proj) = refs[:4], refs[4:]
        core = lax.axis_index("core")
        sibs = pl.ds(pl.multiple_of((1 - core) * half, half), half)
        for k in range(4):
            proj[k * points : (k + 1) * points, :] = other_ref[
                SIBLING[k] * points : (SIBLING[k] + 1) * points, :
            ]
        for k in range(count // chunk):
            here = pl.ds(k * chunk, chunk)
            pair = pair_ref[:, here] + lax.dot_general(
                proj[...], panel_ref[here, sibs], NT, preferred_element_type=F32
            )
            for j in range(4):
                mine = slice(j * points, (j + 1) * points)
                weights = scr_refs[j][:, here] if j == 0 else scr_refs[j][j // 3, :, here].astype(F32)
                weighted_ref[mine, here] = (weights * pair[mine]).astype(BF16)
        send = jnp.dot(weighted_ref[...], panel_ref[:, sibs], preferred_element_type=F32)
        send_ref[...] = send.astype(BF16)

    return pl.pallas_call(
        kernel,
        out_shape=[
            jax.ShapeDtypeStruct((rows, count), BF16),
            jax.ShapeDtypeStruct((rows, half), BF16),
        ],
        in_specs=[vmem_spec()] * 7,
        out_specs=[vmem_spec()] * 2,
        scratch_shapes=[pltpu.VMEM((rows, half), BF16)],
        compiler_params=params(24),
        name="direct",
    )(proj_other, panel, pairs, own, *boxes)


def own_half(weighted, panel, psi, psi_last):
    rows, count = weighted.shape
    half = panel.shape[1] // 2
    states, three = psi.shape

    def kernel(weighted_ref, panel_ref, psi_ref, last_ref, keep_ref, all_ref):
        mine = pl.ds(pl.multiple_of(lax.axis_index("core") * half, half), half)
        keep_ref[...] = jnp.dot(weighted_ref[...], panel_ref[:, mine], preferred_element_type=F32)
        all_ref[:, :three] = psi_ref[...]
        all_ref[:, three:] = last_ref[...]

    return pl.pallas_call(
        kernel,
        out_shape=[
            jax.ShapeDtypeStruct((rows, half), F32),
            jax.ShapeDtypeStruct((states, three + psi_last.shape[1]), BF16),
        ],
        in_specs=[vmem_spec()] * 4,
        out_specs=[vmem_spec()] * 2,
        compiler_params=params(16),
        name="own_half",
    )(weighted, panel, psi, psi_last)


def finish(psi, keep, got):
    states, count = psi.shape
    points = count // 4
    cols = keep.shape[1]

    def kernel(psi_ref, keep_ref, got_ref, out_ref, high, low):
        for k in range(4):
            here = slice(k * points, (k + 1) * points)
            there = slice(SIBLING[k] * points, (SIBLING[k] + 1) * points)
            back = keep_ref[here, :] + got_ref[there, :].astype(F32)
            top = back.astype(BF16)
            high[here, :] = top
            low[here, :] = (back - top.astype(F32)).astype(BF16)
        total = jnp.dot(psi_ref[...], high[...], preferred_element_type=F32)
        total += jnp.dot(psi_ref[...], low[...], preferred_element_type=F32)
        out_ref[...] = total.astype(BF16)

    return pl.pallas_call(
        kernel,
        out_shape=jax.ShapeDtypeStruct((states, cols), BF16),
        in_specs=[vmem_spec()] * 3,
        out_specs=vmem_spec(),
        scratch_shapes=[pltpu.VMEM((count, cols), BF16)] * 2,
        compiler_params=params(16),
        name="finish",
    )(psi, keep, got)


def shards(trial, psi_v, psi_c, screened):
    rows, states = trial.shape[1:]
    half = states // 2
    devices = lax.axis_size(TILE_VEC)
    own, near, far = pack(screened, psi_v)
    block = psi_c[:, 0, :].T
    line = jnp.concatenate([block, shift(block, "x", 1), shift(block, "x", -1), shift(block, "x", 2)], 0)
    halves = trial[0].reshape(rows, 2, half).transpose(1, 0, 2)
    copies = jnp.broadcast_to(halves[None, :, None], (devices // 4, 2, 2, rows, half))
    copies, near, far, line = lax.optimization_barrier((copies, near, far, line))
    trial_half = exchange(copies.reshape(devices, rows, half), TILE_VEC).reshape(-1, half)
    near = swap(near)
    far = lax.ppermute(far, "zh", [(0, 1), (1, 0)])
    behind, ahead = shift(line, "y", 1), shift(line, "y", -1)
    middle = line.shape[0] // 2
    beyond = [shift(behind[:middle], "y", 1), shift(ahead[middle:], "y", -1)]
    far, beyond = lax.optimization_barrier((far, beyond))
    passed = swap(far)
    three, psi = project(trial_half, psi_v, near, far)
    proj_own, psi_last = project_last(trial_half, passed, three)
    proj_other = swap(proj_own)
    panel = [line, behind, ahead, *beyond]
    ordered, pairs = own_pairs(proj_own, panel)
    weighted, send = direct(proj_other, ordered, pairs, own, [near, far, passed])
    got = swap(send)
    keep, psi = own_half(weighted, ordered, psi, psi_last)
    term = finish(psi, keep, got)
    parts = exchange(term.reshape(devices, rows, half), TILE_VEC)
    parts = parts.reshape(-1, 2, 2, rows, half).astype(F32)
    total = jnp.sum(parts, axis=(0, 2))
    return total.transpose(1, 0, 2).reshape(1, rows, states)


def solution(mesh):
    split = Mesh(
        mesh.devices.reshape(2, 4, 4, 2, mesh.shape["vec"]),
        TILE_VEC,
    )
    return jax.shard_map(
        shards,
        mesh=split,
        in_specs=(P(None, TILE_VEC, None), P(None, TILE), P(None, "zl", TILE), P(TILE, "zl")),
        out_specs=P(None, TILE_VEC, None),
        check_vma=False,
    )
```
